32 devices in a mesh: ctx: 16 (over z, y, x), ch: 2 (over core).
Axes of the slice: x: 2, y: 2, z: 4, core: 2. Of those that a mesh axis runs over, the one named last changes fastest.
Arguments:
- tokens: bfloat16 [16384, 8192], P('ctx', 'ch'), may hold values from -6 to 6
- in_weight: bfloat16 [128, 3, 8192], P('ctx', None, 'ch'), may hold values from -0.09375 to 0.09375
- conv_filter: float32 [128, 16384], P('ch', 'ctx'), as said below
- skip_gain: float32 [128], P('ch'), may hold values from -4 to 4
- group_order: int32 [32], replicated, may hold values from 0 to 31, each once
- out_weight: bfloat16 [128, 8192], P('ctx', 'ch'), may hold values from -0.5 to 0.5
Outputs:
- mixed: bfloat16 [16384, 8192], P('ctx', 'ch')
The draws below stay inside these ranges and needn't reach their ends.
Inputs may be any that keep to these rules, and one draw needn't show every extreme that they name: `conv_filter`: each channel's filter has a sum of squares of one over all 16384 lags. `group_order`: a permutation of the storage blocks' group numbers.
All inputs are finite; a program needn't handle non-finite values.
Results may differ from the reference program's by a relative error of at most 0.0049.
Values may be sent and summed in bfloat16 or wider, within the bound.
A program may use at most 192 MiB of HBM per device.

```python
import math
import jax
import jax.numpy as jnp
from jax import lax

D = 8192
C = 128
SEQ = 16384
GROUP = 512
BLOCKS = 32


def draw_conv_filter(key, part):
    keys = jax.random.split(jax.random.fold_in(key, 7), 5)
    lags = jnp.arange(SEQ, dtype=jnp.float32)
    share = 0.5
    picks = jax.random.uniform(keys[0], (C,), jnp.float32)
    fast = jnp.exp(jax.random.uniform(keys[1], (C,), jnp.float32, math.log(30.0), math.log(50.0)))
    slow = jnp.exp(jax.random.uniform(keys[2], (C,), jnp.float32, math.log(SEQ / 2.0), math.log(8.0 * SEQ)))
    spans = jnp.where(picks < share, slow, fast)
    envelope = jnp.exp(-lags[None, :] / spans[:, None])
    noise = jax.random.truncated_normal(keys[3], -4.0, 4.0, (C, SEQ), jnp.float32)
    noise = noise * jax.random.uniform(keys[4], (C, SEQ), jnp.float32, 0.5, 1.5)
    shaped = noise * envelope
    energy = jnp.sum(shaped * shaped, axis=1)
    return (shaped / jnp.sqrt(energy)[:, None]).astype(jnp.float32)


def raised(entries, own_key, source, target, shards_of, factor):
    def block_of(dim):
        return (jnp.arange(entries.shape[dim]) // (entries.shape[dim] // shards_of)).reshape((-1,) + (1,) * (entries.ndim - 1 - dim))

    first = jax.random.permutation(own_key, shards_of)[block_of(target)]
    far = (block_of(target) + shards_of // 2) % shards_of
    return jnp.where((block_of(source) == first) | (block_of(source) == far), factor * entries, entries)


def steps_of(stream_key, extent, pieces, low, high):
    def one(dim, parts):
        steps = jax.random.uniform(jax.random.fold_in(jax.random.fold_in(stream_key, 6), dim), (parts,), jnp.float32, low / len(pieces), high / len(pieces))
        return jnp.repeat(jnp.exp(steps), extent[dim] // parts).reshape((-1,) + (1,) * (len(extent) - dim - 1))

    loudness = one(*pieces[0])
    for cut in pieces[1:]:
        loudness = loudness * one(*cut)
    return loudness


def centred(key, extent, scale, most, shards=(), kind=jnp.bfloat16):
    drawn = jax.random.normal(key, extent, jnp.float32) * scale
    if len(shards) > 0:
        drawn = steps_of(key, extent, shards, -0.22, 0.18) * drawn
    return jnp.clip(drawn, min=-most, max=most).astype(kind)


def heavy_noise(own_key, extent, scale, limit, pieces, heavy, kind=jnp.bfloat16):
    values = scale * jax.random.normal(own_key, extent, jnp.float32)
    if pieces:
        values = values * steps_of(own_key, extent, pieces, -0.22, 0.18)
    return jnp.clip(raised(values, jax.random.fold_in(own_key, 3), *heavy), -limit, limit).astype(kind)


def setup_inputs(seed: int = 0) -> dict:
    arg_keys = jax.random.split(jax.random.key(seed), 7)
    return {
        "tokens": centred(arg_keys[0], (SEQ, D), 1.0, 6.0, ((0, 16), (1, 2))),
        "in_weight": heavy_noise(arg_keys[1], (C, 3, D), D ** -0.5, 0.09375, ((0, 16), (2, 2)), (2, 0, 16, 2.0)),
        "conv_filter": draw_conv_filter(jax.random.fold_in(arg_keys[6], 71), 0),
        "skip_gain": centred(arg_keys[3], (C,), 1.0, 4.0, ((0, 2),), jnp.float32),
        "group_order": jax.random.permutation(arg_keys[4], BLOCKS).astype(jnp.int32),
        "out_weight": centred(arg_keys[5], (C, D), C ** -0.5, 0.5, ((0, 16), (1, 2))),
    }


def reference(tokens, in_weight, conv_filter, skip_gain, group_order, out_weight):
    flat = in_weight.reshape(3 * C, D)
    token_blocks = tokens.reshape(BLOCKS, GROUP, D)

    def project(block):
        return lax.dot_general(flat, block, (((1,), (1,)), ((), ())), preferred_element_type=jnp.float32)

    proj = lax.map(project, token_blocks)
    proj = jnp.transpose(proj, (1, 0, 2)).reshape(C, 3, SEQ)
    gate_part = proj[:, 0]
    product = proj[:, 1] * proj[:, 2]
    inverse = jnp.zeros((BLOCKS,), jnp.int32).at[group_order].set(jnp.arange(BLOCKS, dtype=jnp.int32))
    in_sequence = product.reshape(C, BLOCKS, GROUP)[:, inverse].reshape(C, SEQ)
    length = 2 * SEQ
    spectrum = jnp.fft.rfft(in_sequence, length, axis=1) * jnp.fft.rfft(conv_filter, length, axis=1)
    conv_seq = jnp.fft.irfft(spectrum, length, axis=1)[:, :SEQ]
    conv = conv_seq.reshape(C, BLOCKS, GROUP)[:, group_order].reshape(C, SEQ)
    hidden = (gate_part * (conv + skip_gain[:, None] * product)).astype(jnp.bfloat16)
    hidden_blocks = jnp.transpose(hidden.reshape(C, BLOCKS, GROUP), (1, 0, 2))

    def output(block):
        result = lax.dot_general(block, out_weight, (((0,), (0,)), ((), ())), preferred_element_type=jnp.float32)
        return result.astype(jnp.bfloat16)

    return lax.map(output, hidden_blocks).reshape(SEQ, D)
```

```python
import functools
import itertools
import math

import jax
import jax.numpy as jnp
import numpy as np
from jax import lax
from jax.experimental import pallas as pl
from jax.experimental.pallas import tpu as pltpu
from jax.sharding import PartitionSpec as P

high = lax.Precision.HIGH
RELAY_LIMIT = 16


def split_length(length):
    cols = 1 << ((length.bit_length() - 1) // 2)
    return length // cols, cols


def cos_sin(numer, period):
    angle = (numer % period).astype(jnp.float32) * (2.0 * math.pi / period)
    return jnp.cos(angle), jnp.sin(angle)


def row_table(row_ids, rows):
    freq = 4 * jnp.arange(rows, dtype=jnp.int32) + 1
    cos, sin = cos_sin(freq[:, None] * row_ids[None, :], 4 * rows)
    return jnp.concatenate([cos, -sin], axis=0)


def col_table(cols):
    ids = jnp.arange(cols, dtype=jnp.int32)
    cos, sin = cos_sin(ids[:, None] * ids[None, :], cols)
    top = jnp.concatenate([cos, -sin], axis=1)
    bottom = jnp.concatenate([sin, cos], axis=1)
    return jnp.concatenate([top, bottom], axis=0)


def twist(rows, cols):
    freq = 4 * jnp.arange(rows, dtype=jnp.int32) + 1
    return cos_sin(freq[:, None] * jnp.arange(cols, dtype=jnp.int32)[None, :], 4 * rows * cols)


def spectrum(values, row_dft, col_dft, tw):
    rows, chans, cols = values.shape
    cos, sin = tw[0][:, None, :], tw[1][:, None, :]
    part = jnp.dot(row_dft, values.reshape(rows, chans * cols), precision=high)
    real = part[:rows].reshape(rows, chans, cols)
    imag = part[rows:].reshape(rows, chans, cols)
    turned = jnp.concatenate([real * cos + imag * sin, imag * cos - real * sin], axis=2)
    out = jnp.dot(turned.reshape(rows * chans, 2 * cols), col_dft, precision=high)
    return out.reshape(rows, chans, 2 * cols)


def causal_conv(values, taps, row_ids):
    rows, chans, cols = values.shape
    col_dft = col_table(cols)
    tw = twist(rows, cols)
    perm_dft = row_table(row_ids, rows)
    sig = spectrum(values, perm_dft, col_dft, tw)
    fil = spectrum(taps, row_table(jnp.arange(rows, dtype=jnp.int32), rows), col_dft, tw)
    sr, si = sig[..., :cols], sig[..., cols:]
    fr, fi = fil[..., :cols], fil[..., cols:]
    both = jnp.concatenate([sr * fr - si * fi, sr * fi + si * fr], axis=2)
    back = jnp.dot(both.reshape(rows * chans, 2 * cols), col_dft.T, precision=high)
    back = back.reshape(rows, chans, 2 * cols) * (1.0 / (rows * cols))
    br, bi = back[..., :cols], back[..., cols:]
    cos, sin = tw[0][:, None, :], tw[1][:, None, :]
    turned = jnp.concatenate([br * cos - bi * sin, br * sin + bi * cos], axis=0)
    out = jnp.dot(perm_dft.T, turned.reshape(2 * rows, chans * cols), precision=high)
    return out.reshape(rows, chans, cols)


STEPS_UP, STEPS_DOWN, ACROSS, BESIDE = range(4)
PLANE = 4


def plane_of(z, line, slot):
    low = z < line // 2
    w = jnp.where(low, z, line - 1 - z)
    near = (w, w + 1, 2 - 2 * w, line - 1 + 0 * w)[slot]
    return jnp.where(low, near, line - 1 - near)


class Relay:
    reach = (0, 1, 1.6, 2.6)

    def __init__(self, line, own_ref, all_ref, columns, order, send_sems, recv_sems, slot):
        self.line, self.order, self.slot = line, order, slot
        self.own_ref, self.all_ref, self.columns = own_ref, all_ref, columns
        self.send_sems, self.recv_sems = send_sems, recv_sems
        me = lax.axis_index("ctx")
        self.me, self.z, self.y, self.x = me, me // 4, me // 2 % 2, me % 2

    def offsets(self):
        return itertools.product(range(self.line), (0, 1), (0, 1))

    def key(self, offset):
        return self.reach[offset[0]] + offset[1] + offset[2]

    def origin(self, offset):
        dz, dy, dx = offset
        y = 1 - self.y if dy else self.y
        x = 1 - self.x if dx else self.x
        return plane_of(self.z, self.line, dz) * PLANE + y * 2 + x

    def at(self, ref, *lead):
        whole = (slice(None),) * (len(self.own_ref.shape) - 1)
        return ref.at[(*lead, *whole, self.columns)]

    def exits(self, offset):
        along = [k for k, dim in enumerate(self.order) if offset[dim] != 0]
        last = along[-1] if along else -1
        out = []
        if last >= 0 and self.order[last] == 0:
            out.append("on")
        for dim in self.order[last + 1 :]:
            out += ([STEPS_UP, STEPS_DOWN], [ACROSS], [BESIDE])[dim]
        return out

    def copy(self, offset, way):
        origin = self.origin(offset)
        up = self.me + PLANE
        down = self.me - PLANE
        if way == "on":
            rising = plane_of(self.z, self.line, offset[0]) < self.z
            target = jnp.where(rising, up, down)
            index = jnp.where(rising, STEPS_UP, STEPS_DOWN)
        else:
            target = (up, down, self.me + 2 - 4 * self.y, self.me + 1 - 2 * self.x)[way]
            index = way
        own = all(step == 0 for step in offset)
        return pltpu.make_async_remote_copy(
            src_ref=self.at(self.own_ref) if own else self.at(self.all_ref, origin),
            dst_ref=self.at(self.all_ref, origin),
            send_sem=self.send_sems.at[self.slot, origin, index],
            recv_sem=self.recv_sems.at[self.slot, origin],
            device_id={"ctx": target},
            device_id_type=pl.DeviceIdType.MESH,
        )

    def each_exit(self, offset, act):
        for way in self.exits(offset):
            copy = self.copy(offset, way)
            if way in (ACROSS, BESIDE):
                act(copy)
                continue
            room_up, room_down = self.z + 1 < self.line, self.z > 0
            if way == "on":
                rising = plane_of(self.z, self.line, offset[0]) < self.z
                test = jnp.where(rising, room_up, room_down)
            else:
                test = room_up if way == STEPS_UP else room_down

            @pl.when(test)
            def _():
                act(copy)

    def begin(self):
        self.each_exit((0, 0, 0), lambda copy: copy.start())

    def step(self, offset):
        self.copy(offset, BESIDE).wait_recv()
        self.each_exit(offset, lambda copy: copy.start())

    def finish(self):
        for offset in self.offsets():
            self.each_exit(offset, lambda copy: copy.wait_send())


class Rounds:
    def __init__(self, relays):
        self.relays = relays
        todo = [(r.key(o), k, o) for k, r in enumerate(relays) for o in r.offsets() if any(o)]
        self.todo = sorted(todo, key=lambda item: item[:2])

    def begin(self):
        for relay in self.relays:
            relay.begin()

    def upto(self, limit):
        while self.todo and self.todo[0][0] < limit + 0.01:
            _, k, offset = self.todo.pop(0)
            self.relays[k].step(offset)

    def finish(self):
        for relay in self.relays:
            relay.finish()


def greet_all(count):
    me, ch = lax.axis_index("ctx"), lax.axis_index("ch")
    barrier = pltpu.get_barrier_semaphore()

    @pl.loop(1, count)
    def _(step):
        pl.semaphore_signal(
            barrier, inc=1, device_id={"ctx": lax.rem(me + step, count)}, device_id_type=pl.DeviceIdType.MESH
        )

    pl.semaphore_signal(barrier, inc=1, device_id={"ch": 1 - ch}, device_id_type=pl.DeviceIdType.MESH)
    return lambda: pl.semaphore_wait(barrier, count)


def halves(v):
    top = v.astype(jnp.bfloat16)
    return top, (v - top.astype(jnp.float32)).astype(jnp.bfloat16)


def dot_halves(a, b):
    dot = functools.partial(jnp.dot, preferred_element_type=jnp.float32)
    return dot(a[0], b[0]) + (dot(a[0], b[1]) + dot(a[1], b[0]))


def fused_kernel(
    count, sub, in_ref, tok_ref, out_ref, taps_ref, skip_ref, order_ref, row_ref, col_ref, inv_ref, cos_ref, sin_ref,
    hidden_ref, rows_ref,
    in_all, tok, part, inbox, gate, prod, stage, taps_in, taps_stage, taps_got, got, result, back, hid,
    relay_send, relay_recv, pair_send, pair_recv, taps_send, taps_recv, prod_send, prod_recv,
    back_send, back_recv, hid_send, hid_recv, local_sems,
):
    me, ch = lax.axis_index("ctx"), lax.axis_index("ch")
    line = count // PLANE
    z = me // PLANE
    rows, cols = cos_ref.shape
    own_rows = tok_ref.shape[0] // cols
    owned = got.shape[1] // own_rows
    chans = in_ref.shape[1]
    pack = got.shape[1]
    wide = in_ref.shape[2]
    tokens = tok_ref.shape[0]
    ctx_dev = pl.DeviceIdType.MESH

    def cut(*shares):
        edges = [wide * sum(shares[:k]) // sum(shares) for k in range(len(shares) + 1)]
        return [pl.ds(a, b - a) for a, b in zip(edges, edges[1:])]

    first, second, third = cut(6, 7, 3)
    left, right = cut(1, 1)
    weights = Rounds([
        Relay(line, in_ref, in_all, first, (0, 1, 2), relay_send, relay_recv, 0),
        Relay(line, in_ref, in_all, second, (0, 2, 1), relay_send, relay_recv, 1),
        Relay(line, in_ref, in_all, third, (1, 2, 0), relay_send, relay_recv, 2),
    ])
    outs = Rounds([
        Relay(line, out_ref, rows_ref, left, (0, 1, 2), relay_send, relay_recv, 3),
        Relay(line, out_ref, rows_ref, right, (0, 2, 1), relay_send, relay_recv, 4),
    ])

    def turned(device):
        return lax.rem(device + count // 2, count)

    def group(ref, g):
        return ref.at[g // 2, pl.ds(pl.multiple_of(lax.rem(g, 2) * pack, pack), pack)]

    load_taps = pltpu.make_async_copy(taps_ref, taps_in, local_sems.at[0])
    load_in = pltpu.make_async_copy(in_ref, in_all.at[me], local_sems.at[1])
    load_tok = pltpu.make_async_copy(tok_ref, tok, local_sems.at[2])
    load_out = pltpu.make_async_copy(out_ref, rows_ref.at[me], local_sems.at[3])
    keep_taps = pltpu.make_async_copy(group(taps_stage, turned(me)), taps_got.at[me], local_sems.at[4])
    keep_prod = pltpu.make_async_copy(group(stage, turned(me)), got.at[me], local_sems.at[5])
    keep_back = pltpu.make_async_copy(result.at[me], group(back, turned(me)), local_sems.at[6])
    keep_hid = pltpu.make_async_copy(hid, hidden_ref.at[ch], local_sems.at[7])

    all_in = greet_all(count)
    load_taps.start()
    load_in.start()
    load_tok.start()
    load_out.start()
    all_in()
    weights.begin()

    def send_taps(target):
        return pltpu.make_async_remote_copy(
            src_ref=group(taps_stage, turned(target)), dst_ref=taps_got.at[me],
            send_sem=taps_send.at[target], recv_sem=taps_recv.at[me],
            device_id={"ctx": target}, device_id_type=ctx_dev,
        )

    def recv_taps(source):
        return pltpu.make_async_remote_copy(
            src_ref=group(taps_stage, turned(source)), dst_ref=taps_got.at[source],
            send_sem=taps_send.at[source], recv_sem=taps_recv.at[source],
            device_id={"ctx": source}, device_id_type=ctx_dev,
        )

    def send_prod(target):
        return pltpu.make_async_remote_copy(
            src_ref=group(stage, turned(target)), dst_ref=got.at[me],
            send_sem=prod_send.at[target], recv_sem=prod_recv.at[me],
            device_id={"ctx": target}, device_id_type=ctx_dev,
        )

    def recv_prod(source):
        return pltpu.make_async_remote_copy(
            src_ref=group(stage, turned(source)), dst_ref=got.at[source],
            send_sem=prod_send.at[source], recv_sem=prod_recv.at[source],
            device_id={"ctx": source}, device_id_type=ctx_dev,
        )

    def send_back(target):
        return pltpu.make_async_remote_copy(
            src_ref=result.at[target], dst_ref=group(back, turned(me)),
            send_sem=back_send.at[target], recv_sem=back_recv.at[me],
            device_id={"ctx": target}, device_id_type=ctx_dev,
        )

    def recv_back(source):
        return pltpu.make_async_remote_copy(
            src_ref=result.at[source], dst_ref=group(back, turned(source)),
            send_sem=back_send.at[source], recv_sem=back_recv.at[source],
            device_id={"ctx": source}, device_id_type=ctx_dev,
        )

    def others(act):
        @pl.loop(1, count)
        def _(step):
            act(lax.rem(me + step, count))

    def spread(values, ref, o):
        for t in range(own_rows):
            ref[o, pl.ds(t, chans, stride=own_rows), :] = values[:, t * cols : (t + 1) * cols]

    load_taps.wait()
    for o in range(taps_in.shape[0]):
        spread(taps_in[o], taps_stage, o)
    keep_taps.start()
    others(lambda target: send_taps(target).start())

    def pair(j):
        return pltpu.make_async_remote_copy(
            src_ref=part.at[j], dst_ref=inbox.at[j], send_sem=pair_send.at[j], recv_sem=pair_recv.at[j],
            device_id={"ch": 1 - ch}, device_id_type=ctx_dev,
        )

    half = tokens // 2
    block = PLANE * 3 * chans

    def project(j):
        q = plane_of(z, line, j)

        @pl.loop(0, tokens // half)
        def _(n):
            at = pl.multiple_of(n * half, half)
            mine = in_all[pl.ds(q * PLANE, PLANE)].reshape(block, wide)
            part[j, :, pl.ds(at, half)] = lax.dot_general(
                mine, tok[pl.ds(at, half), :], (((1,), (1,)), ((), ())), preferred_element_type=jnp.float32
            )

        @pl.when(q // 2 != ch)
        def _():
            pair(j).start()

    def consume(j):
        q = plane_of(z, line, j)

        @pl.when(q // 2 == ch)
        def _():
            pair(j).wait_recv()
            for i in range(PLANE):
                o = lax.rem(q, 2) * PLANE + i
                at = 3 * chans * i
                gate[o], key, value = [
                    part[j, pl.ds(at + m * chans, chans), :] + inbox[j, pl.ds(at + m * chans, chans), :]
                    for m in range(3)
                ]
                values = key * value
                prod[o] = values
                spread(values, stage, o)

            @pl.loop(0, 2 * PLANE)
            def _(n):
                target = turned(lax.rem(q, 2) * 2 * PLANE + n)

                @pl.when(target != me)
                def _():
                    send_prod(target).start()

                @pl.when(target == me)
                def _():
                    keep_prod.start()

        @pl.when(q // 2 != ch)
        def _():
            pair(j).wait_send()

    def iota(shape, dim):
        return lax.broadcasted_iota(jnp.int32, shape, dim)

    blocks = order_ref.shape[1]
    hot = jnp.where(iota((blocks, blocks), 0) == order_ref[...], 1.0, 0.0).astype(jnp.bfloat16)
    down = jnp.where(iota((rows, blocks), 0) // sub == iota((rows, blocks), 1), 1.0, 0.0).astype(jnp.bfloat16)
    over = jnp.where(iota((blocks, rows), 1) // sub == iota((blocks, rows), 0), 1.0, 0.0).astype(jnp.bfloat16)
    dot = functools.partial(jnp.dot, preferred_element_type=jnp.float32)
    moved = dot(dot(down, hot).astype(jnp.bfloat16), over)
    same = lax.rem(iota((rows, rows), 0), sub) == lax.rem(iota((rows, rows), 1), sub)
    moved = jnp.where(same, moved, 0.0).astype(jnp.bfloat16)
    perm_wide = [dot(row_ref[k], moved) for k in range(2)]
    perm = [v.astype(jnp.bfloat16) for v in perm_wide]
    perm_t = [v.T.astype(jnp.bfloat16) for v in perm_wide]
    cos, sin = cos_ref[...], sin_ref[...]

    def transform(ref, table):
        stacked = jnp.concatenate(
            [ref[:, c * own_rows : (c + 1) * own_rows, :].reshape(rows, cols) for c in range(owned)], axis=1
        )
        turn = dot_halves(table, halves(stacked))
        out = []
        for c in range(owned):
            real = turn[:rows, c * cols : (c + 1) * cols]
            imag = turn[rows:, c * cols : (c + 1) * cols]
            out.append(jnp.concatenate([real * cos + imag * sin, imag * cos - real * sin], axis=1))
        return dot_halves(halves(jnp.concatenate(out, axis=0)), (col_ref[0], col_ref[1]))

    load_in.wait()
    load_tok.wait()
    weights.upto(2)
    project(0)
    weights.upto(3)
    project(1)
    consume(0)
    weights.upto(3.6)
    project(2)
    consume(1)
    others(lambda source: recv_taps(source).wait_recv())
    keep_taps.wait()
    fil = transform(taps_got, (row_ref[0], row_ref[1]))
    weights.upto(9)
    load_out.wait()
    outs.begin()
    project(3)
    consume(2)
    outs.upto(1)
    consume(3)
    outs.upto(2)
    others(lambda source: recv_prod(source).wait_recv())
    keep_prod.wait()
    sig = transform(got, perm)
    outs.upto(3)
    sr, si, fr, fi = sig[:, :cols], sig[:, cols:], fil[:, :cols], fil[:, cols:]
    both = jnp.concatenate([sr * fr - si * fi, sr * fi + si * fr], axis=1)
    spun = dot_halves(halves(both), (inv_ref[0], inv_ref[1]))
    turn = []
    for c in range(owned):
        real = spun[c * rows : (c + 1) * rows, :cols]
        imag = spun[c * rows : (c + 1) * rows, cols:]
        turn.append(jnp.concatenate([real * cos - imag * sin, real * sin + imag * cos], axis=0))
    conv = dot_halves(perm_t, halves(jnp.concatenate(turn, axis=1)))
    for c in range(owned):
        piece = conv[:, c * cols : (c + 1) * cols].reshape(count, own_rows, cols)
        result[:, c * own_rows : (c + 1) * own_rows, :] = piece
    keep_back.start()
    others(lambda target: send_back(target).start())
    outs.upto(9)
    others(lambda source: recv_back(source).wait_recv())
    keep_back.wait()
    for o in range(0, gate.shape[0], 2):
        for t in range(own_rows):
            lanes = slice(t * cols, (t + 1) * cols)
            pieces = []
            for k in (o, o + 1):
                near = back[k, pl.ds(t, chans, stride=own_rows), :]
                pieces.append(gate[k, :, lanes] * (near + skip_ref[k] * prod[k, :, lanes]))
            hid[o * chans : (o + 2) * chans, lanes] = jnp.concatenate(pieces, axis=0).astype(jnp.bfloat16)
    share = pltpu.make_async_remote_copy(
        src_ref=hid, dst_ref=hidden_ref.at[ch], send_sem=hid_send.at[0], recv_sem=hid_recv.at[0],
        device_id={"ch": 1 - ch}, device_id_type=ctx_dev,
    )
    share.start()
    keep_hid.start()
    others(lambda target: send_taps(target).wait_send())
    others(lambda target: send_prod(target).wait_send())
    others(lambda target: send_back(target).wait_send())
    weights.finish()
    outs.finish()
    keep_hid.wait()
    share.wait()


def split_table(table):
    top = table.astype(jnp.bfloat16)
    low = (table - top.astype(np.float32)).astype(jnp.bfloat16)
    return np.stack([top, low])


def fused(tokens, in_weight, conv_filter, skip_gain, group_order, out_weight, count):
    tok_count, feat = tokens.shape
    chans = in_weight.shape[0]
    chan_local = conv_filter.shape[0]
    seq = tok_count * count
    rows, cols = split_length(seq)
    own_rows = tok_count // cols
    owned = chan_local // count
    sub = seq // group_order.shape[0] // cols
    freq = 4 * np.arange(rows) + 1

    def turns(numer, period):
        angle = (numer % period) * (2.0 * math.pi / period)
        return np.cos(angle).astype(np.float32), np.sin(angle).astype(np.float32)

    cos, sin = turns(freq[:, None] * np.arange(rows)[None, :], 4 * rows)
    row_dft = np.concatenate([cos, -sin], axis=0)
    cos, sin = turns(np.arange(cols)[:, None] * np.arange(cols)[None, :], cols)
    col_dft = np.concatenate([np.concatenate([cos, -sin], 1), np.concatenate([sin, cos], 1)], 0)
    col_inv = (col_dft.T / (rows * cols)).astype(np.float32)
    tw_cos, tw_sin = turns(freq[:, None] * np.arange(cols)[None, :], 4 * rows * cols)
    pairs = chan_local // chans
    skip = jnp.broadcast_to(skip_gain.reshape(pairs, chans, 1), (pairs, chans, cols))
    vmem, hbm = pl.BlockSpec(memory_space=pltpu.VMEM), pl.BlockSpec(memory_space=pl.ANY)
    f32, bf16 = jnp.float32, jnp.bfloat16
    packed = pltpu.VMEM((pairs, chans * own_rows, cols), f32)
    blocks = pltpu.VMEM((count, owned * own_rows, cols), f32)
    full = pltpu.VMEM((pairs, chans, tok_count), f32)
    strips = pltpu.VMEM((count // PLANE, PLANE * 3 * chans, tok_count), f32)
    each = pltpu.SemaphoreType.DMA((count,))
    hidden, rows_all = pl.pallas_call(
        functools.partial(fused_kernel, count, sub),
        out_shape=(
            jax.ShapeDtypeStruct((2, chan_local, tok_count), bf16),
            jax.ShapeDtypeStruct((count, *out_weight.shape), bf16),
        ),
        in_specs=[hbm] * 4 + [vmem] * 7,
        out_specs=(hbm, hbm),
        scratch_shapes=[
            pltpu.VMEM((count, 3, chans, feat), bf16),
            pltpu.VMEM((tok_count, feat), bf16),
            strips, strips, full, full, packed, full, packed, blocks, blocks, blocks, packed,
            pltpu.VMEM((chan_local, tok_count), bf16),
            pltpu.SemaphoreType.DMA((5, count, 4)),
            pltpu.SemaphoreType.DMA((5, count)),
            pltpu.SemaphoreType.DMA((count // PLANE,)),
            pltpu.SemaphoreType.DMA((count // PLANE,)),
            each, each, each, each, each, each,
            pltpu.SemaphoreType.DMA((1,)),
            pltpu.SemaphoreType.DMA((1,)),
            pltpu.SemaphoreType.DMA((8,)),
        ],
        compiler_params=pltpu.CompilerParams(collective_id=0, has_side_effects=True, vmem_limit_bytes=48 * 2**20),
        name="fused",
    )(
        in_weight.transpose(1, 0, 2), tokens, out_weight, conv_filter.reshape(pairs, chans, tok_count), skip,
        group_order.reshape(1, -1), split_table(row_dft), split_table(col_dft), split_table(col_inv), tw_cos, tw_sin,
    )
    return hidden.reshape(2 * chan_local, tok_count), rows_all.reshape(-1, feat)


def per_device(tokens, in_weight, conv_filter, skip_gain, group_order, out_weight):
    ctx = lax.axis_size("ctx")
    ch = lax.axis_size("ch")
    tok_count, feat_local = tokens.shape
    chan_local = conv_filter.shape[0]
    seq = tok_count * ctx
    group = seq // group_order.shape[0]
    rows, cols = split_length(seq)
    own_rows = tok_count // cols
    owned = -(-chan_local // ctx)
    padded = owned * ctx

    def parts_of(signal):
        signal = jnp.pad(signal, ((0, padded - chan_local), (0, 0)))
        return signal.reshape(ctx, owned, own_rows, cols)

    def swapped(parts):
        return lax.all_to_all(parts, "ctx", split_axis=0, concat_axis=0, tiled=True)

    relayed = ctx == RELAY_LIMIT and ch == 2 and in_weight.shape[0] == 8 and own_rows == 8 and padded == chan_local
    if relayed:
        hidden_all, rows_all = fused(tokens, in_weight, conv_filter, skip_gain, group_order, out_weight, ctx)
        mixed = lax.dot_general(
            hidden_all, rows_all, (((0,), (0,)), ((), ())), preferred_element_type=jnp.float32
        )
        return mixed.astype(jnp.bfloat16)
    mine = in_weight.reshape(-1, feat_local)
    flat = lax.all_gather(mine, "ctx", axis=0, tiled=True)
    rows_all = lax.all_gather(out_weight, "ctx", axis=0, tiled=True)
    taps = swapped(parts_of(conv_filter))
    partial = lax.dot_general(flat, tokens, (((1,), (1,)), ((), ())), preferred_element_type=jnp.float32)
    if ch == 2:
        me = lax.axis_index("ch")
        half = partial.shape[0] // 2
        away = lax.dynamic_slice_in_dim(partial, (1 - me) * half, half, 0)
        kept = lax.dynamic_slice_in_dim(partial, me * half, half, 0)
        proj = kept + lax.ppermute(away, "ch", [(0, 1), (1, 0)])
    else:
        proj = lax.psum_scatter(partial, "ch", scatter_dimension=0, tiled=True)
    proj = proj.reshape(chan_local, 3, tok_count)
    gate = proj[:, 0]
    product = proj[:, 1] * proj[:, 2]
    in_group = jnp.arange(group // cols, dtype=jnp.int32)
    row_ids = (group_order[:, None] * (group // cols) + in_group[None, :]).reshape(rows)

    def grid(parts):
        return parts.transpose(0, 2, 1, 3).reshape(rows, owned, cols)

    conv = causal_conv(grid(swapped(parts_of(product))), grid(taps), row_ids)
    back = swapped(conv.reshape(ctx, own_rows, owned, cols).transpose(0, 2, 1, 3))
    conv = back.reshape(padded, tok_count)[:chan_local]
    hidden = (gate * (conv + skip_gain[:, None] * product)).astype(jnp.bfloat16)
    hidden_all = lax.all_gather(hidden, "ch", axis=0, tiled=True)
    mixed = lax.dot_general(
        hidden_all, rows_all, (((0,), (0,)), ((), ())), preferred_element_type=jnp.float32
    )
    return mixed.astype(jnp.bfloat16)


def solution(mesh):
    in_specs = (P("ctx", "ch"), P("ctx", None, "ch"), P("ch", "ctx"), P("ch"), P(), P("ctx", "ch"))
    return jax.shard_map(
        per_device, mesh=mesh, in_specs=in_specs, out_specs=P("ctx", "ch"), check_vma=False
    )
```

```python
import functools
import itertools
import math

import jax
import jax.numpy as jnp
import numpy as np
from jax import lax
from jax.experimental import pallas as pl
from jax.experimental.pallas import tpu as pltpu
from jax.sharding import PartitionSpec as P

high = lax.Precision.HIGH
RELAY_LIMIT = 16
VMEM_LIMIT = 63 * 2**20


def split_length(length):
    cols = 1 << ((length.bit_length() - 1) // 2)
    return length // cols, cols


def cos_sin(numer, period):
    angle = (numer % period).astype(jnp.float32) * (2.0 * math.pi / period)
    return jnp.cos(angle), jnp.sin(angle)


def row_table(row_ids, rows):
    freq = 4 * jnp.arange(rows, dtype=jnp.int32) + 1
    cos, sin = cos_sin(freq[:, None] * row_ids[None, :], 4 * rows)
    return jnp.concatenate([cos, -sin], axis=0)


def col_table(cols):
    ids = jnp.arange(cols, dtype=jnp.int32)
    cos, sin = cos_sin(ids[:, None] * ids[None, :], cols)
    top = jnp.concatenate([cos, -sin], axis=1)
    bottom = jnp.concatenate([sin, cos], axis=1)
    return jnp.concatenate([top, bottom], axis=0)


def twist(rows, cols):
    freq = 4 * jnp.arange(rows, dtype=jnp.int32) + 1
    return cos_sin(freq[:, None] * jnp.arange(cols, dtype=jnp.int32)[None, :], 4 * rows * cols)


def spectrum(values, row_dft, col_dft, tw):
    rows, chans, cols = values.shape
    cos, sin = tw[0][:, None, :], tw[1][:, None, :]
    part = jnp.dot(row_dft, values.reshape(rows, chans * cols), precision=high)
    real = part[:rows].reshape(rows, chans, cols)
    imag = part[rows:].reshape(rows, chans, cols)
    turned = jnp.concatenate([real * cos + imag * sin, imag * cos - real * sin], axis=2)
    out = jnp.dot(turned.reshape(rows * chans, 2 * cols), col_dft, precision=high)
    return out.reshape(rows, chans, 2 * cols)


def causal_conv(values, taps, row_ids):
    rows, chans, cols = values.shape
    col_dft = col_table(cols)
    tw = twist(rows, cols)
    perm_dft = row_table(row_ids, rows)
    sig = spectrum(values, perm_dft, col_dft, tw)
    fil = spectrum(taps, row_table(jnp.arange(rows, dtype=jnp.int32), rows), col_dft, tw)
    sr, si = sig[..., :cols], sig[..., cols:]
    fr, fi = fil[..., :cols], fil[..., cols:]
    both = jnp.concatenate([sr * fr - si * fi, sr * fi + si * fr], axis=2)
    back = jnp.dot(both.reshape(rows * chans, 2 * cols), col_dft.T, precision=high)
    back = back.reshape(rows, chans, 2 * cols) * (1.0 / (rows * cols))
    br, bi = back[..., :cols], back[..., cols:]
    cos, sin = tw[0][:, None, :], tw[1][:, None, :]
    turned = jnp.concatenate([br * cos - bi * sin, br * sin + bi * cos], axis=0)
    out = jnp.dot(perm_dft.T, turned.reshape(2 * rows, chans * cols), precision=high)
    return out.reshape(rows, chans, cols)


STEPS_UP, STEPS_DOWN, ACROSS, BESIDE = range(4)
PLANE = 4


def plane_of(z, line, slot):
    low = z < line // 2
    w = jnp.where(low, z, line - 1 - z)
    near = (w, w + 1, 2 - 2 * w, line - 1 + 0 * w)[slot]
    return jnp.where(low, near, line - 1 - near)


class Relay:
    reach = (0, 1, 1.6, 2.6)

    def __init__(self, line, own_ref, all_ref, columns, order, send_sems, recv_sems, slot):
        self.line, self.order, self.slot = line, order, slot
        self.own_ref, self.all_ref, self.columns = own_ref, all_ref, columns
        self.send_sems, self.recv_sems = send_sems, recv_sems
        me = lax.axis_index("ctx")
        self.me, self.z, self.y, self.x = me, me // 4, me // 2 % 2, me % 2

    def offsets(self):
        return itertools.product(range(self.line), (0, 1), (0, 1))

    def key(self, offset):
        return self.reach[offset[0]] + offset[1] + offset[2]

    def origin(self, offset):
        dz, dy, dx = offset
        y = 1 - self.y if dy else self.y
        x = 1 - self.x if dx else self.x
        return plane_of(self.z, self.line, dz) * PLANE + y * 2 + x

    def at(self, ref, *lead):
        whole = (slice(None),) * (len(self.own_ref.shape) - 1)
        return ref.at[(*lead, *whole, self.columns)]

    def exits(self, offset):
        along = [k for k, dim in enumerate(self.order) if offset[dim] != 0]
        last = along[-1] if along else -1
        out = []
        if last >= 0 and self.order[last] == 0:
            out.append("on")
        for dim in self.order[last + 1 :]:
            out += ([STEPS_UP, STEPS_DOWN], [ACROSS], [BESIDE])[dim]
        return out

    def copy(self, offset, way):
        origin = self.origin(offset)
        up = self.me + PLANE
        down = self.me - PLANE
        if way == "on":
            rising = plane_of(self.z, self.line, offset[0]) < self.z
            target = jnp.where(rising, up, down)
            index = jnp.where(rising, STEPS_UP, STEPS_DOWN)
        else:
            target = (up, down, self.me + 2 - 4 * self.y, self.me + 1 - 2 * self.x)[way]
            index = way
        own = all(step == 0 for step in offset)
        return pltpu.make_async_remote_copy(
            src_ref=self.at(self.own_ref) if own else self.at(self.all_ref, origin),
            dst_ref=self.at(self.all_ref, origin),
            send_sem=self.send_sems.at[self.slot, origin, index],
            recv_sem=self.recv_sems.at[self.slot, origin],
            device_id={"ctx": target},
            device_id_type=pl.DeviceIdType.MESH,
        )

    def each_exit(self, offset, act):
        for way in self.exits(offset):
            copy = self.copy(offset, way)
            if way in (ACROSS, BESIDE):
                act(copy)
                continue
            room_up, room_down = self.z + 1 < self.line, self.z > 0
            if way == "on":
                rising = plane_of(self.z, self.line, offset[0]) < self.z
                test = jnp.where(rising, room_up, room_down)
            else:
                test = room_up if way == STEPS_UP else room_down

            @pl.when(test)
            def _():
                act(copy)

    def begin(self):
        self.each_exit((0, 0, 0), lambda copy: copy.start())

    def step(self, offset):
        self.copy(offset, BESIDE).wait_recv()
        self.each_exit(offset, lambda copy: copy.start())

    def finish(self):
        for offset in self.offsets():
            self.each_exit(offset, lambda copy: copy.wait_send())


class Rounds:
    def __init__(self, relays):
        self.relays = relays
        todo = [(r.key(o), k, o) for k, r in enumerate(relays) for o in r.offsets() if any(o)]
        self.todo = sorted(todo, key=lambda item: item[:2])

    def begin(self):
        for relay in self.relays:
            relay.begin()

    def upto(self, limit):
        while self.todo and self.todo[0][0] < limit + 0.01:
            _, k, offset = self.todo.pop(0)
            self.relays[k].step(offset)

    def finish(self):
        for relay in self.relays:
            relay.finish()


def greet_all(count):
    me, ch = lax.axis_index("ctx"), lax.axis_index("ch")
    barrier = pltpu.get_barrier_semaphore()

    @pl.loop(1, count)
    def _(step):
        pl.semaphore_signal(
            barrier, inc=1, device_id={"ctx": lax.rem(me + step, count)}, device_id_type=pl.DeviceIdType.MESH
        )

    pl.semaphore_signal(barrier, inc=1, device_id={"ch": 1 - ch}, device_id_type=pl.DeviceIdType.MESH)
    return lambda: pl.semaphore_wait(barrier, count)


def halves(v):
    top = v.astype(jnp.bfloat16)
    return top, (v - top.astype(jnp.float32)).astype(jnp.bfloat16)


def dot_halves(a, b):
    dot = functools.partial(jnp.dot, preferred_element_type=jnp.float32)
    return dot(a[0], b[0]) + (dot(a[0], b[1]) + dot(a[1], b[0]))


def fused_kernel(
    count, sub, in_ref, tok_ref, out_ref, taps_ref, skip_hbm, order_hbm, row_hbm, col_hbm, inv_hbm, turn_hbm,
    hidden_ref, rows_ref,
    skip_ref, order_ref, row_ref, col_ref, inv_ref, turn_ref, in_all, tok, part, inbox, gate, prod, stage, taps_in, taps_stage, taps_got, got, result, back, hid,
    relay_send, relay_recv, pair_send, pair_recv, taps_send, taps_recv, prod_send, prod_recv,
    back_send, back_recv, hid_send, hid_recv, local_sems,
):
    me, ch = lax.axis_index("ctx"), lax.axis_index("ch")
    line = count // PLANE
    z = me // PLANE
    rows, cols = turn_ref.shape[1:]
    own_rows = tok_ref.shape[0] // cols
    owned = got.shape[1] // own_rows
    chans = in_ref.shape[1]
    pack = got.shape[1]
    wide = in_ref.shape[2]
    tokens = tok_ref.shape[0]
    ctx_dev = pl.DeviceIdType.MESH

    def cut(*shares):
        edges = [wide * sum(shares[:k]) // sum(shares) for k in range(len(shares) + 1)]
        return [pl.ds(a, b - a) for a, b in zip(edges, edges[1:])]

    first, second, third = cut(6, 7, 3)
    left, right = cut(1, 1)
    weights = Rounds([
        Relay(line, in_ref, in_all, first, (0, 1, 2), relay_send, relay_recv, 0),
        Relay(line, in_ref, in_all, second, (0, 2, 1), relay_send, relay_recv, 1),
        Relay(line, in_ref, in_all, third, (1, 2, 0), relay_send, relay_recv, 2),
    ])
    outs = Rounds([
        Relay(line, out_ref, rows_ref, left, (0, 1, 2), relay_send, relay_recv, 3),
        Relay(line, out_ref, rows_ref, right, (0, 2, 1), relay_send, relay_recv, 4),
    ])

    def turned(device):
        return lax.rem(device + count // 2, count)

    def group(ref, g):
        return ref.at[g // 2, pl.ds(pl.multiple_of(lax.rem(g, 2) * pack, pack), pack)]

    load_taps = pltpu.make_async_copy(taps_ref, taps_in, local_sems.at[0])
    load_in = pltpu.make_async_copy(in_ref, in_all.at[me], local_sems.at[1])
    load_tok = pltpu.make_async_copy(tok_ref, tok, local_sems.at[2])
    load_out = pltpu.make_async_copy(out_ref, rows_ref.at[me], local_sems.at[3])
    keep_taps = pltpu.make_async_copy(group(taps_stage, turned(me)), taps_got.at[me], local_sems.at[4])
    keep_prod = pltpu.make_async_copy(group(stage, turned(me)), got.at[me], local_sems.at[5])
    keep_back = pltpu.make_async_copy(result.at[me], group(back, turned(me)), local_sems.at[6])
    keep_hid = pltpu.make_async_copy(hid, hidden_ref.at[ch], local_sems.at[7])

    tables = [
        pltpu.make_async_copy(src, dst, local_sems.at[8 + k])
        for k, (src, dst) in enumerate([
            (order_hbm, order_ref), (row_hbm, row_ref), (col_hbm, col_ref),
            (inv_hbm, inv_ref), (turn_hbm, turn_ref), (skip_hbm, skip_ref),
        ])
    ]
    all_in = greet_all(count)
    load_taps.start()
    load_in.start()
    load_tok.start()
    load_out.start()
    for copy in tables:
        copy.start()
    all_in()
    weights.begin()

    def send_taps(target):
        return pltpu.make_async_remote_copy(
            src_ref=group(taps_stage, turned(target)), dst_ref=taps_got.at[me],
            send_sem=taps_send.at[target], recv_sem=taps_recv.at[me],
            device_id={"ctx": target}, device_id_type=ctx_dev,
        )

    def recv_taps(source):
        return pltpu.make_async_remote_copy(
            src_ref=group(taps_stage, turned(source)), dst_ref=taps_got.at[source],
            send_sem=taps_send.at[source], recv_sem=taps_recv.at[source],
            device_id={"ctx": source}, device_id_type=ctx_dev,
        )

    def send_prod(target):
        return pltpu.make_async_remote_copy(
            src_ref=group(stage, turned(target)), dst_ref=got.at[me],
            send_sem=prod_send.at[target], recv_sem=prod_recv.at[me],
            device_id={"ctx": target}, device_id_type=ctx_dev,
        )

    def recv_prod(source):
        return pltpu.make_async_remote_copy(
            src_ref=group(stage, turned(source)), dst_ref=got.at[source],
            send_sem=prod_send.at[source], recv_sem=prod_recv.at[source],
            device_id={"ctx": source}, device_id_type=ctx_dev,
        )

    def send_back(target):
        return pltpu.make_async_remote_copy(
            src_ref=result.at[target], dst_ref=group(back, turned(me)),
            send_sem=back_send.at[target], recv_sem=back_recv.at[me],
            device_id={"ctx": target}, device_id_type=ctx_dev,
        )

    def recv_back(source):
        return pltpu.make_async_remote_copy(
            src_ref=result.at[source], dst_ref=group(back, turned(source)),
            send_sem=back_send.at[source], recv_sem=back_recv.at[source],
            device_id={"ctx": source}, device_id_type=ctx_dev,
        )

    def others(act):
        @pl.loop(1, count)
        def _(step):
            act(lax.rem(me + step, count))

    def spread(values, ref, o):
        for t in range(own_rows):
            ref[o, pl.ds(t, chans, stride=own_rows), :] = values[:, t * cols : (t + 1) * cols]

    load_taps.wait()
    for o in range(taps_in.shape[0]):
        spread(taps_in[o], taps_stage, o)
    keep_taps.start()
    others(lambda target: send_taps(target).start())

    def pair(j):
        return pltpu.make_async_remote_copy(
            src_ref=part.at[j], dst_ref=inbox.at[j], send_sem=pair_send.at[j], recv_sem=pair_recv.at[j],
            device_id={"ch": 1 - ch}, device_id_type=ctx_dev,
        )

    half = tokens // 2
    block = PLANE * 3 * chans

    def project(j):
        q = plane_of(z, line, j)

        @pl.loop(0, tokens // half)
        def _(n):
            at = pl.multiple_of(n * half, half)
            mine = in_all[pl.ds(q * PLANE, PLANE)].reshape(block, wide)
            part[j, :, pl.ds(at, half)] = lax.dot_general(
                mine, tok[pl.ds(at, half), :], (((1,), (1,)), ((), ())), preferred_element_type=jnp.float32
            )

        @pl.when(q // 2 != ch)
        def _():
            pair(j).start()

    def consume(j):
        q = plane_of(z, line, j)

        @pl.when(q // 2 == ch)
        def _():
            pair(j).wait_recv()
            for i in range(PLANE):
                o = lax.rem(q, 2) * PLANE + i
                at = 3 * chans * i
                gate[o], key, value = [
                    part[j, pl.ds(at + m * chans, chans), :] + inbox[j, pl.ds(at + m * chans, chans), :]
                    for m in range(3)
                ]
                values = key * value
                prod[o] = values
                spread(values, stage, o)

            @pl.loop(0, 2 * PLANE)
            def _(n):
                target = turned(lax.rem(q, 2) * 2 * PLANE + n)

                @pl.when(target != me)
                def _():
                    send_prod(target).start()

                @pl.when(target == me)
                def _():
                    keep_prod.start()

        @pl.when(q // 2 != ch)
        def _():
            pair(j).wait_send()

    def iota(shape, dim):
        return lax.broadcasted_iota(jnp.int32, shape, dim)

    for copy in tables:
        copy.wait()
    blocks = order_ref.shape[1]
    hot = jnp.where(iota((blocks, blocks), 0) == order_ref[...], 1.0, 0.0).astype(jnp.bfloat16)
    down = jnp.where(iota((rows, blocks), 0) // sub == iota((rows, blocks), 1), 1.0, 0.0).astype(jnp.bfloat16)
    over = jnp.where(iota((blocks, rows), 1) // sub == iota((blocks, rows), 0), 1.0, 0.0).astype(jnp.bfloat16)
    dot = functools.partial(jnp.dot, preferred_element_type=jnp.float32)
    moved = dot(dot(down, hot).astype(jnp.bfloat16), over)
    same = lax.rem(iota((rows, rows), 0), sub) == lax.rem(iota((rows, rows), 1), sub)
    moved = jnp.where(same, moved, 0.0).astype(jnp.bfloat16)
    perm_wide = [dot(row_ref[k], moved) for k in range(2)]
    perm = [v.astype(jnp.bfloat16) for v in perm_wide]
    perm_t = [v.T.astype(jnp.bfloat16) for v in perm_wide]
    cos, sin = turn_ref[0], turn_ref[1]

    def transform(ref, table):
        stacked = jnp.concatenate(
            [ref[:, c * own_rows : (c + 1) * own_rows, :].reshape(rows, cols) for c in range(owned)], axis=1
        )
        turn = dot_halves(table, halves(stacked))
        out = []
        for c in range(owned):
            real = turn[:rows, c * cols : (c + 1) * cols]
            imag = turn[rows:, c * cols : (c + 1) * cols]
            out.append(jnp.concatenate([real * cos + imag * sin, imag * cos - real * sin], axis=1))
        return dot_halves(halves(jnp.concatenate(out, axis=0)), (col_ref[0], col_ref[1]))

    load_in.wait()
    load_tok.wait()
    weights.upto(2)
    project(0)
    weights.upto(3)
    project(1)
    consume(0)
    weights.upto(3.6)
    project(2)
    consume(1)
    others(lambda source: recv_taps(source).wait_recv())
    keep_taps.wait()
    fil = transform(taps_got, (row_ref[0], row_ref[1]))
    weights.upto(9)
    load_out.wait()
    outs.begin()
    project(3)
    consume(2)
    outs.upto(1)
    consume(3)
    outs.upto(2)
    others(lambda source: recv_prod(source).wait_recv())
    keep_prod.wait()
    sig = transform(got, perm)
    outs.upto(3)
    sr, si, fr, fi = sig[:, :cols], sig[:, cols:], fil[:, :cols], fil[:, cols:]
    both = jnp.concatenate([sr * fr - si * fi, sr * fi + si * fr], axis=1)
    spun = dot_halves(halves(both), (inv_ref[0], inv_ref[1]))
    turn = []
    for c in range(owned):
        real = spun[c * rows : (c + 1) * rows, :cols]
        imag = spun[c * rows : (c + 1) * rows, cols:]
        turn.append(jnp.concatenate([real * cos - imag * sin, real * sin + imag * cos], axis=0))
    conv = dot_halves(perm_t, halves(jnp.concatenate(turn, axis=1)))
    for c in range(owned):
        piece = conv[:, c * cols : (c + 1) * cols].reshape(count, own_rows, cols)
        result[:, c * own_rows : (c + 1) * own_rows, :] = piece
    keep_back.start()
    others(lambda target: send_back(target).start())
    outs.upto(9)
    others(lambda source: recv_back(source).wait_recv())
    keep_back.wait()
    width = skip_ref.shape[1]
    diagonal = iota((width, width), 0) == iota((width, width), 1)
    skip = jnp.sum(jnp.where(diagonal, skip_ref[...], 0.0), axis=1, keepdims=True)
    for o in range(0, gate.shape[0], 2):
        for t in range(own_rows):
            lanes = slice(t * cols, (t + 1) * cols)
            pieces = []
            for k in (o, o + 1):
                near = back[k, pl.ds(t, chans, stride=own_rows), :]
                pieces.append(gate[k, :, lanes] * (near + skip[k * chans : (k + 1) * chans] * prod[k, :, lanes]))
            hid[o * chans : (o + 2) * chans, lanes] = jnp.concatenate(pieces, axis=0).astype(jnp.bfloat16)
    share = pltpu.make_async_remote_copy(
        src_ref=hid, dst_ref=hidden_ref.at[ch], send_sem=hid_send.at[0], recv_sem=hid_recv.at[0],
        device_id={"ch": 1 - ch}, device_id_type=ctx_dev,
    )
    share.start()
    keep_hid.start()
    others(lambda target: send_taps(target).wait_send())
    others(lambda target: send_prod(target).wait_send())
    others(lambda target: send_back(target).wait_send())
    weights.finish()
    outs.finish()
    keep_hid.wait()
    share.wait()


def split_table(table):
    top = table.astype(jnp.bfloat16)
    low = (table - top.astype(np.float32)).astype(jnp.bfloat16)
    return np.stack([top, low])


def fused(tokens, in_weight, conv_filter, skip_gain, group_order, out_weight, count):
    tok_count, feat = tokens.shape
    chans = in_weight.shape[0]
    chan_local = conv_filter.shape[0]
    seq = tok_count * count
    rows, cols = split_length(seq)
    own_rows = tok_count // cols
    owned = chan_local // count
    sub = seq // group_order.shape[0] // cols
    freq = 4 * np.arange(rows) + 1

    def turns(numer, period):
        angle = (numer % period) * (2.0 * math.pi / period)
        return np.cos(angle).astype(np.float32), np.sin(angle).astype(np.float32)

    cos, sin = turns(freq[:, None] * np.arange(rows)[None, :], 4 * rows)
    row_dft = np.concatenate([cos, -sin], axis=0)
    cos, sin = turns(np.arange(cols)[:, None] * np.arange(cols)[None, :], cols)
    col_dft = np.concatenate([np.concatenate([cos, -sin], 1), np.concatenate([sin, cos], 1)], 0)
    col_inv = (col_dft.T / (rows * cols)).astype(np.float32)
    tw_cos, tw_sin = turns(freq[:, None] * np.arange(cols)[None, :], 4 * rows * cols)
    pairs = chan_local // chans
    hbm = pl.BlockSpec(memory_space=pl.ANY)
    f32, bf16 = jnp.float32, jnp.bfloat16
    packed = pltpu.VMEM((pairs, chans * own_rows, cols), f32)
    blocks = pltpu.VMEM((count, owned * own_rows, cols), f32)
    full = pltpu.VMEM((pairs, chans, tok_count), f32)
    strips = pltpu.VMEM((count // PLANE, PLANE * 3 * chans, tok_count), f32)
    each = pltpu.SemaphoreType.DMA((count,))
    hidden, rows_all = pl.pallas_call(
        functools.partial(fused_kernel, count, sub),
        out_shape=(
            jax.ShapeDtypeStruct((2, chan_local, tok_count), bf16),
            jax.ShapeDtypeStruct((count, *out_weight.shape), bf16),
        ),
        in_specs=[hbm] * 10,
        out_specs=(hbm, hbm),
        scratch_shapes=[
            pltpu.VMEM((1, chan_local), f32),
            pltpu.VMEM((1, group_order.shape[0]), jnp.int32),
            pltpu.VMEM((2, *row_dft.shape), bf16),
            pltpu.VMEM((2, *col_dft.shape), bf16),
            pltpu.VMEM((2, *col_inv.shape), bf16),
            pltpu.VMEM((2, rows, cols), f32),
            pltpu.VMEM((count, 3, chans, feat), bf16),
            pltpu.VMEM((tok_count, feat), bf16),
            strips, strips, full, full, packed, full, packed, blocks, blocks, blocks, packed,
            pltpu.VMEM((chan_local, tok_count), bf16),
            pltpu.SemaphoreType.DMA((5, count, 4)),
            pltpu.SemaphoreType.DMA((5, count)),
            pltpu.SemaphoreType.DMA((count // PLANE,)),
            pltpu.SemaphoreType.DMA((count // PLANE,)),
            each, each, each, each, each, each,
            pltpu.SemaphoreType.DMA((1,)),
            pltpu.SemaphoreType.DMA((1,)),
            pltpu.SemaphoreType.DMA((14,)),
        ],
        compiler_params=pltpu.CompilerParams(collective_id=0, has_side_effects=True, vmem_limit_bytes=VMEM_LIMIT),
        name="fused",
    )(
        in_weight.transpose(1, 0, 2), tokens, out_weight, conv_filter.reshape(pairs, chans, tok_count),
        skip_gain.reshape(1, -1), group_order.reshape(1, -1), split_table(row_dft), split_table(col_dft),
        split_table(col_inv), np.stack([tw_cos, tw_sin]),
    )
    return hidden.reshape(2 * chan_local, tok_count), rows_all.reshape(-1, feat)


def per_device(tokens, in_weight, conv_filter, skip_gain, group_order, out_weight):
    ctx = lax.axis_size("ctx")
    ch = lax.axis_size("ch")
    tok_count, feat_local = tokens.shape
    chan_local = conv_filter.shape[0]
    seq = tok_count * ctx
    group = seq // group_order.shape[0]
    rows, cols = split_length(seq)
    own_rows = tok_count // cols
    owned = -(-chan_local // ctx)
    padded = owned * ctx

    def parts_of(signal):
        signal = jnp.pad(signal, ((0, padded - chan_local), (0, 0)))
        return signal.reshape(ctx, owned, own_rows, cols)

    def swapped(parts):
        return lax.all_to_all(parts, "ctx", split_axis=0, concat_axis=0, tiled=True)

    relayed = ctx == RELAY_LIMIT and ch == 2 and in_weight.shape[0] == 8 and own_rows == 8 and padded == chan_local
    if relayed:
        hidden_all, rows_all = fused(tokens, in_weight, conv_filter, skip_gain, group_order, out_weight, ctx)
        mixed = lax.dot_general(
            hidden_all, rows_all, (((0,), (0,)), ((), ())), preferred_element_type=jnp.float32
        )
        return mixed.astype(jnp.bfloat16)
    mine = in_weight.reshape(-1, feat_local)
    flat = lax.all_gather(mine, "ctx", axis=0, tiled=True)
    rows_all = lax.all_gather(out_weight, "ctx", axis=0, tiled=True)
    taps = swapped(parts_of(conv_filter))
    partial = lax.dot_general(flat, tokens, (((1,), (1,)), ((), ())), preferred_element_type=jnp.float32)
    if ch == 2:
        me = lax.axis_index("ch")
        half = partial.shape[0] // 2
        away = lax.dynamic_slice_in_dim(partial, (1 - me) * half, half, 0)
        kept = lax.dynamic_slice_in_dim(partial, me * half, half, 0)
        proj = kept + lax.ppermute(away, "ch", [(0, 1), (1, 0)])
    else:
        proj = lax.psum_scatter(partial, "ch", scatter_dimension=0, tiled=True)
    proj = proj.reshape(chan_local, 3, tok_count)
    gate = proj[:, 0]
    product = proj[:, 1] * proj[:, 2]
    in_group = jnp.arange(group // cols, dtype=jnp.int32)
    row_ids = (group_order[:, None] * (group // cols) + in_group[None, :]).reshape(rows)

    def grid(parts):
        return parts.transpose(0, 2, 1, 3).reshape(rows, owned, cols)

    conv = causal_conv(grid(swapped(parts_of(product))), grid(taps), row_ids)
    back = swapped(conv.reshape(ctx, own_rows, owned, cols).transpose(0, 2, 1, 3))
    conv = back.reshape(padded, tok_count)[:chan_local]
    hidden = (gate * (conv + skip_gain[:, None] * product)).astype(jnp.bfloat16)
    hidden_all = lax.all_gather(hidden, "ch", axis=0, tiled=True)
    mixed = lax.dot_general(
        hidden_all, rows_all, (((0,), (0,)), ((), ())), preferred_element_type=jnp.float32
    )
    return mixed.astype(jnp.bfloat16)


def solution(mesh):
    in_specs = (P("ctx", "ch"), P("ctx", None, "ch"), P("ch", "ctx"), P("ch"), P(), P("ctx", "ch"))
    return jax.shard_map(
        per_device, mesh=mesh, in_specs=in_specs, out_specs=P("ctx", "ch"), check_vma=False
    )
```

```python
import functools
import itertools
import math

import jax
import jax.numpy as jnp
import numpy as np
from jax import lax
from jax.experimental import pallas as pl
from jax.experimental.pallas import tpu as pltpu
from jax.sharding import PartitionSpec as P

high = lax.Precision.HIGH
RELAY_LIMIT = 16
VMEM_LIMIT = 63 * 2**20


def split_length(length):
    cols = 1 << ((length.bit_length() - 1) // 2)
    return length // cols, cols


def cos_sin(numer, period):
    angle = (numer % period).astype(jnp.float32) * (2.0 * math.pi / period)
    return jnp.cos(angle), jnp.sin(angle)


def row_table(row_ids, rows):
    freq = 4 * jnp.arange(rows, dtype=jnp.int32) + 1
    cos, sin = cos_sin(freq[:, None] * row_ids[None, :], 4 * rows)
    return jnp.concatenate([cos, -sin], axis=0)


def col_table(cols):
    ids = jnp.arange(cols, dtype=jnp.int32)
    cos, sin = cos_sin(ids[:, None] * ids[None, :], cols)
    top = jnp.concatenate([cos, -sin], axis=1)
    bottom = jnp.concatenate([sin, cos], axis=1)
    return jnp.concatenate([top, bottom], axis=0)


def twist(rows, cols):
    freq = 4 * jnp.arange(rows, dtype=jnp.int32) + 1
    return cos_sin(freq[:, None] * jnp.arange(cols, dtype=jnp.int32)[None, :], 4 * rows * cols)


def spectrum(values, row_dft, col_dft, tw):
    rows, chans, cols = values.shape
    cos, sin = tw[0][:, None, :], tw[1][:, None, :]
    part = jnp.dot(row_dft, values.reshape(rows, chans * cols), precision=high)
    real = part[:rows].reshape(rows, chans, cols)
    imag = part[rows:].reshape(rows, chans, cols)
    turned = jnp.concatenate([real * cos + imag * sin, imag * cos - real * sin], axis=2)
    out = jnp.dot(turned.reshape(rows * chans, 2 * cols), col_dft, precision=high)
    return out.reshape(rows, chans, 2 * cols)


def causal_conv(values, taps, row_ids):
    rows, chans, cols = values.shape
    col_dft = col_table(cols)
    tw = twist(rows, cols)
    perm_dft = row_table(row_ids, rows)
    sig = spectrum(values, perm_dft, col_dft, tw)
    fil = spectrum(taps, row_table(jnp.arange(rows, dtype=jnp.int32), rows), col_dft, tw)
    sr, si = sig[..., :cols], sig[..., cols:]
    fr, fi = fil[..., :cols], fil[..., cols:]
    both = jnp.concatenate([sr * fr - si * fi, sr * fi + si * fr], axis=2)
    back = jnp.dot(both.reshape(rows * chans, 2 * cols), col_dft.T, precision=high)
    back = back.reshape(rows, chans, 2 * cols) * (1.0 / (rows * cols))
    br, bi = back[..., :cols], back[..., cols:]
    cos, sin = tw[0][:, None, :], tw[1][:, None, :]
    turned = jnp.concatenate([br * cos - bi * sin, br * sin + bi * cos], axis=0)
    out = jnp.dot(perm_dft.T, turned.reshape(2 * rows, chans * cols), precision=high)
    return out.reshape(rows, chans, cols)


PLANE = 4
ACROSS, BESIDE = 2, 3


def plane_of(z, line, slot):
    low = z < line // 2
    w = jnp.where(low, z, line - 1 - z)
    near = (w, w + 1, 2 - 2 * w, line - 1 + 0 * w)[slot]
    return jnp.where(low, near, line - 1 - near)


class Relay:
    reach = (0, 1, 1.6, 2.6)

    def __init__(self, line, own_ref, all_ref, columns, order, send_sems, recv_sems, slot):
        self.line, self.order, self.slot = line, order, slot
        self.own_ref, self.all_ref, self.columns = own_ref, all_ref, columns
        self.send_sems, self.recv_sems = send_sems, recv_sems
        me = lax.axis_index("ctx")
        self.me, self.z, self.y, self.x = me, me // 4, me // 2 % 2, me % 2

    def offsets(self):
        return itertools.product(range(self.line), (0, 1), (0, 1))

    def key(self, offset):
        return self.reach[offset[0]] + offset[1] + offset[2]

    def origin(self, offset):
        dz, dy, dx = offset
        y = 1 - self.y if dy else self.y
        x = 1 - self.x if dx else self.x
        return plane_of(self.z, self.line, dz) * PLANE + y * 2 + x

    def at(self, ref, *lead):
        whole = (slice(None),) * (len(self.own_ref.shape) - 1)
        return ref.at[(*lead, *whole, self.columns)]

    def exits(self, offset):
        along = [k for k, dim in enumerate(self.order) if offset[dim] != 0]
        last = along[-1] if along else -1
        out = []
        if last >= 0 and self.order[last] == 0:
            out.append("on")
        for dim in self.order[last + 1 :]:
            out += (["up", "down"], [ACROSS], [BESIDE])[dim]
        return out

    def copy(self, offset, way):
        origin = self.origin(offset)
        up = self.me + PLANE
        down = self.me - PLANE
        own = all(step == 0 for step in offset)
        if way == "on":
            rising = plane_of(self.z, self.line, offset[0]) < self.z
            target, index = jnp.where(rising, up, down), jnp.where(rising, 0, 1)
        elif way in ("up", "down"):
            target, index = (up, 0) if way == "up" else (down, 1)
        else:
            target = self.me + 2 - 4 * self.y if way == ACROSS else self.me + 1 - 2 * self.x
            index = way
        return pltpu.make_async_remote_copy(
            src_ref=self.at(self.own_ref) if own else self.at(self.all_ref, origin),
            dst_ref=self.at(self.all_ref, origin),
            send_sem=self.send_sems.at[self.slot, origin, index],
            recv_sem=self.recv_sems.at[self.slot, origin],
            device_id={"ctx": target},
            device_id_type=pl.DeviceIdType.MESH,
        )

    def each_exit(self, offset, act):
        for way in self.exits(offset):
            copy = self.copy(offset, way)
            if way not in ("on", "up", "down"):
                act(copy)
                continue
            room_up, room_down = self.z + 1 < self.line, self.z > 0
            if way == "on":
                rising = plane_of(self.z, self.line, offset[0]) < self.z
                test = jnp.where(rising, room_up, room_down)
            else:
                test = room_up if way == "up" else room_down

            @pl.when(test)
            def _():
                act(copy)

    def begin(self):
        self.each_exit((0, 0, 0), lambda copy: copy.start())

    def step(self, offset):
        self.copy(offset, BESIDE).wait_recv()
        self.each_exit(offset, lambda copy: copy.start())

    def finish(self):
        for offset in self.offsets():
            self.each_exit(offset, lambda copy: copy.wait_send())


class Rounds:
    def __init__(self, relays):
        self.relays = relays
        todo = [(r.key(o), k, o) for k, r in enumerate(relays) for o in r.offsets() if any(o)]
        self.todo = sorted(todo, key=lambda item: item[:2])

    def begin(self):
        for relay in self.relays:
            relay.begin()

    def upto(self, limit):
        while self.todo and self.todo[0][0] < limit + 0.01:
            _, k, offset = self.todo.pop(0)
            self.relays[k].step(offset)

    def finish(self):
        for relay in self.relays:
            relay.finish()


class Spread:
    def __init__(self, line, own_ref, all_ref, columns, order, send_sems, recv_sems, slot):
        self.line, self.order, self.slot = line, order, slot
        self.own_ref, self.all_ref, self.columns = own_ref, all_ref, columns
        self.send_sems, self.recv_sems = send_sems, recv_sems
        me = lax.axis_index("ctx")
        self.me, self.z, self.y, self.x = me, me // 4, me // 2 % 2, me % 2

    def column(self, near, far):
        flips = {self.order[1]: near, self.order[2]: far}
        y = 1 - self.y if flips[1] else self.y
        x = 1 - self.x if flips[2] else self.x
        return self.all_ref.at[:, y, x, :, self.columns]

    def ship(self, source, place, target, send, recv):
        return pltpu.make_async_remote_copy(
            src_ref=source, dst_ref=place,
            send_sem=self.send_sems.at[self.slot, send], recv_sem=self.recv_sems.at[self.slot, recv],
            device_id={"ctx": target}, device_id_type=pl.DeviceIdType.MESH,
        )

    def lift(self, slot, into):
        z = plane_of(self.z, self.line, slot)
        mine = self.all_ref.at[self.z, self.y, self.x, :, self.columns]
        theirs = self.all_ref.at[z, self.y, self.x, :, self.columns]
        target = self.me + (z - self.z) * PLANE
        if into:
            return self.ship(theirs, theirs, target, slot - 1, z)
        return self.ship(self.own_ref.at[:, self.columns], mine, target, slot - 1, self.z)

    def pass_on(self, kind, into):
        near, far = ((1, 0), (0, 1), (1, 1))[kind]
        dim = self.order[1 if kind == 0 else 2]
        target = self.me + 2 - 4 * self.y if dim == 1 else self.me + 1 - 2 * self.x
        held, lands = self.column(near * far, 0), self.column(near, far)
        send, recv = self.line - 1 + kind, self.line + kind
        place = lands if into else held
        return self.ship(place, place, target, send, recv)

    def moves(self, stage, into=False):
        if stage == 0:
            return [self.lift(slot, into) for slot in range(1, self.line)]
        return [self.pass_on(kind, into) for kind in ((), (0, 1), (2,))[stage]]

    def begin(self, stage):
        for out in self.moves(stage):
            out.start()

    def wait_lifted(self):
        for into in self.moves(0, True):
            into.wait_recv()

    def wait_passed(self, kind):
        self.pass_on(kind, True).wait_recv()

    def finish(self):
        for stage in range(3):
            for out in self.moves(stage):
                out.wait_send()


def greet_all(count):
    me, ch = lax.axis_index("ctx"), lax.axis_index("ch")
    barrier = pltpu.get_barrier_semaphore()

    @pl.loop(1, count)
    def _(step):
        pl.semaphore_signal(
            barrier, inc=1, device_id={"ctx": lax.rem(me + step, count)}, device_id_type=pl.DeviceIdType.MESH
        )

    pl.semaphore_signal(barrier, inc=1, device_id={"ch": 1 - ch}, device_id_type=pl.DeviceIdType.MESH)
    return lambda: pl.semaphore_wait(barrier, count)


def halves(v):
    top = v.astype(jnp.bfloat16)
    return top, (v - top.astype(jnp.float32)).astype(jnp.bfloat16)


def dot_halves(a, b):
    dot = functools.partial(jnp.dot, preferred_element_type=jnp.float32)
    return dot(a[0], b[0]) + (dot(a[0], b[1]) + dot(a[1], b[0]))


def fused_kernel(
    count, sub, in_ref, tok_ref, out_ref, taps_ref, skip_hbm, order_hbm, row_hbm, col_hbm, inv_hbm, turn_hbm,
    hidden_ref, rows_ref,
    skip_ref, order_ref, row_ref, col_ref, inv_ref, turn_ref, in_all, tok, part, inbox, gate, prod, stage, taps_in, taps_stage, taps_got, got, result, back, hid,
    relay_send, relay_recv, out_send, out_recv, pair_send, pair_recv, taps_send, taps_recv, prod_send, prod_recv,
    back_send, back_recv, hid_send, hid_recv, local_sems,
):
    me, ch = lax.axis_index("ctx"), lax.axis_index("ch")
    line = count // PLANE
    z = me // PLANE
    rows, cols = turn_ref.shape[1:]
    own_rows = tok_ref.shape[0] // cols
    owned = got.shape[1] // own_rows
    chans = in_ref.shape[1]
    pack = got.shape[1]
    wide = in_ref.shape[2]
    tokens = tok_ref.shape[0]
    ctx_dev = pl.DeviceIdType.MESH

    def cut(*shares):
        edges = [wide * sum(shares[:k]) // sum(shares) for k in range(len(shares) + 1)]
        return [pl.ds(a, b - a) for a, b in zip(edges, edges[1:])]

    first, second, third = cut(6, 7, 3)
    left, right = cut(1, 1)
    weights = Rounds([
        Relay(line, in_ref, in_all, third, (1, 2, 0), relay_send, relay_recv, 2),
        Relay(line, in_ref, in_all, first, (0, 1, 2), relay_send, relay_recv, 0),
        Relay(line, in_ref, in_all, second, (0, 2, 1), relay_send, relay_recv, 1),
    ])
    outs = [
        Spread(line, out_ref, rows_ref, left, (0, 1, 2), out_send, out_recv, 0),
        Spread(line, out_ref, rows_ref, right, (0, 2, 1), out_send, out_recv, 1),
    ]

    def turned(device):
        return lax.rem(device + count // 2, count)

    def group(ref, g):
        return ref.at[g // 2, pl.ds(pl.multiple_of(lax.rem(g, 2) * pack, pack), pack)]

    load_taps = pltpu.make_async_copy(taps_ref, taps_in, local_sems.at[0])
    load_in = pltpu.make_async_copy(in_ref, in_all.at[me], local_sems.at[1])
    load_tok = pltpu.make_async_copy(tok_ref, tok, local_sems.at[2])
    load_out = pltpu.make_async_copy(out_ref, rows_ref.at[me // PLANE, me // 2 % 2, me % 2], local_sems.at[3])
    keep_taps = pltpu.make_async_copy(group(taps_stage, turned(me)), taps_got.at[me], local_sems.at[4])
    keep_prod = pltpu.make_async_copy(group(stage, turned(me)), got.at[me], local_sems.at[5])
    keep_back = pltpu.make_async_copy(result.at[me], group(back, turned(me)), local_sems.at[6])
    keep_hid = pltpu.make_async_copy(hid, hidden_ref.at[ch], local_sems.at[7])

    tables = [
        pltpu.make_async_copy(src, dst, local_sems.at[8 + k])
        for k, (src, dst) in enumerate([
            (order_hbm, order_ref), (row_hbm, row_ref), (col_hbm, col_ref),
            (inv_hbm, inv_ref), (turn_hbm, turn_ref), (skip_hbm, skip_ref),
        ])
    ]
    all_in = greet_all(count)
    load_taps.start()
    load_in.start()
    load_tok.start()
    load_out.start()
    for copy in tables:
        copy.start()
    all_in()
    weights.begin()

    def send_taps(target):
        return pltpu.make_async_remote_copy(
            src_ref=group(taps_stage, turned(target)), dst_ref=taps_got.at[me],
            send_sem=taps_send.at[target], recv_sem=taps_recv.at[me],
            device_id={"ctx": target}, device_id_type=ctx_dev,
        )

    def recv_taps(source):
        return pltpu.make_async_remote_copy(
            src_ref=group(taps_stage, turned(source)), dst_ref=taps_got.at[source],
            send_sem=taps_send.at[source], recv_sem=taps_recv.at[source],
            device_id={"ctx": source}, device_id_type=ctx_dev,
        )

    def send_prod(target):
        return pltpu.make_async_remote_copy(
            src_ref=group(stage, turned(target)), dst_ref=got.at[me],
            send_sem=prod_send.at[target], recv_sem=prod_recv.at[me],
            device_id={"ctx": target}, device_id_type=ctx_dev,
        )

    def recv_prod(source):
        return pltpu.make_async_remote_copy(
            src_ref=group(stage, turned(source)), dst_ref=got.at[source],
            send_sem=prod_send.at[source], recv_sem=prod_recv.at[source],
            device_id={"ctx": source}, device_id_type=ctx_dev,
        )

    def send_back(target):
        return pltpu.make_async_remote_copy(
            src_ref=result.at[target], dst_ref=group(back, turned(me)),
            send_sem=back_send.at[target], recv_sem=back_recv.at[me],
            device_id={"ctx": target}, device_id_type=ctx_dev,
        )

    def recv_back(source):
        return pltpu.make_async_remote_copy(
            src_ref=result.at[source], dst_ref=group(back, turned(source)),
            send_sem=back_send.at[source], recv_sem=back_recv.at[source],
            device_id={"ctx": source}, device_id_type=ctx_dev,
        )

    def others(act):
        @pl.loop(1, count)
        def _(step):
            act(lax.rem(me + step, count))

    def spread(values, ref, o, begin=0):
        for t in range(values.shape[1] // cols):
            ref[o, pl.ds(begin + t, chans, stride=own_rows), :] = values[:, t * cols : (t + 1) * cols]

    load_taps.wait()
    for o in range(taps_in.shape[0]):
        spread(taps_in[o], taps_stage, o)
    keep_taps.start()
    others(lambda target: send_taps(target).start())

    parts = 4
    share = tokens // parts

    def pair(j, n=None):
        lanes = slice(None) if n is None else slice(n * share, (n + 1) * share)
        return pltpu.make_async_remote_copy(
            src_ref=part.at[j, :, lanes], dst_ref=inbox.at[j, :, lanes],
            send_sem=pair_send.at[j, n or 0], recv_sem=pair_recv.at[j, n or 0],
            device_id={"ch": 1 - ch}, device_id_type=ctx_dev,
        )

    block = PLANE * 3 * chans

    def project(j, *pieces):
        q = plane_of(z, line, j)
        for n in pieces:
            mine = in_all[pl.ds(q * PLANE, PLANE)].reshape(block, wide)
            part[j, :, n * share : (n + 1) * share] = lax.dot_general(
                mine, tok[n * share : (n + 1) * share, :], (((1,), (1,)), ((), ())),
                preferred_element_type=jnp.float32,
            )

    def send_pair(j, n=None):
        @pl.when(plane_of(z, line, j) // 2 != ch)
        def _():
            pair(j, n).start()

    def consume(j, n=None, send=True):
        q = plane_of(z, line, j)
        begin, size = (0, tokens) if n is None else (n * share, share)

        @pl.when(q // 2 == ch)
        def _():
            pair(j, n).wait_recv()
            for i in range(PLANE):
                o = lax.rem(q, 2) * PLANE + i
                at = 3 * chans * i
                lanes = slice(begin, begin + size)
                near, key, value = [
                    part[j, pl.ds(at + m * chans, chans), lanes] + inbox[j, pl.ds(at + m * chans, chans), lanes]
                    for m in range(3)
                ]
                gate[o, :, lanes] = near
                values = key * value
                prod[o, :, lanes] = values
                spread(values, stage, o, begin // cols)

            if send:
                @pl.loop(0, 2 * PLANE)
                def _(k):
                    target = turned(lax.rem(q, 2) * 2 * PLANE + k)

                    @pl.when(target != me)
                    def _():
                        send_prod(target).start()

                    @pl.when(target == me)
                    def _():
                        keep_prod.start()

        @pl.when(q // 2 != ch)
        def _():
            pair(j, n).wait_send()

    def iota(shape, dim):
        return lax.broadcasted_iota(jnp.int32, shape, dim)

    weights.upto(1)
    for copy in tables:
        copy.wait()
    blocks = order_ref.shape[1]
    hot = jnp.where(iota((blocks, blocks), 0) == order_ref[...], 1.0, 0.0).astype(jnp.bfloat16)
    down = jnp.where(iota((rows, blocks), 0) // sub == iota((rows, blocks), 1), 1.0, 0.0).astype(jnp.bfloat16)
    over = jnp.where(iota((blocks, rows), 1) // sub == iota((blocks, rows), 0), 1.0, 0.0).astype(jnp.bfloat16)
    dot = functools.partial(jnp.dot, preferred_element_type=jnp.float32)
    moved = dot(dot(down, hot).astype(jnp.bfloat16), over)
    same = lax.rem(iota((rows, rows), 0), sub) == lax.rem(iota((rows, rows), 1), sub)
    moved = jnp.where(same, moved, 0.0).astype(jnp.bfloat16)
    perm_wide = [dot(row_ref[k], moved) for k in range(2)]
    perm = [v.astype(jnp.bfloat16) for v in perm_wide]
    perm_t = [v.T.astype(jnp.bfloat16) for v in perm_wide]
    cos, sin = turn_ref[0], turn_ref[1]

    def transform(ref, table):
        stacked = jnp.concatenate(
            [ref[:, c * own_rows : (c + 1) * own_rows, :].reshape(rows, cols) for c in range(owned)], axis=1
        )
        turn = dot_halves(table, halves(stacked))
        out = []
        for c in range(owned):
            real = turn[:rows, c * cols : (c + 1) * cols]
            imag = turn[rows:, c * cols : (c + 1) * cols]
            out.append(jnp.concatenate([real * cos + imag * sin, imag * cos - real * sin], axis=1))
        return dot_halves(halves(jnp.concatenate(out, axis=0)), (col_ref[0], col_ref[1]))

    weights.upto(2)
    load_in.wait()
    load_tok.wait()
    project(0, 0, 1)
    weights.upto(2.3)
    project(0, 2, 3)
    send_pair(0)
    weights.upto(2.6)
    others(lambda source: recv_taps(source).wait_recv())
    keep_taps.wait()
    fil = transform(taps_got, (row_ref[0], row_ref[1]))
    weights.upto(3)
    for out in outs:
        out.begin(0)
    project(1, 0, 1)
    weights.upto(3.3)
    project(1, 2, 3)
    send_pair(1)
    consume(0)
    weights.upto(3.6)
    project(2, 0, 1)
    weights.upto(9)
    load_out.wait()
    for out in outs:
        out.wait_lifted()
        out.begin(1)
    project(2, 2, 3)
    send_pair(2)
    consume(1)
    project(3, 0)
    send_pair(3, 0)
    consume(2)
    project(3, 1)
    send_pair(3, 1)
    consume(3, 0, False)
    project(3, 2)
    send_pair(3, 2)
    consume(3, 1, False)
    project(3, 3)
    send_pair(3, 3)
    consume(3, 2, False)
    consume(3, 3)
    others(lambda source: recv_prod(source).wait_recv())
    keep_prod.wait()
    sig = transform(got, perm)
    for out in outs:
        out.wait_passed(0)
        out.begin(2)
    sr, si, fr, fi = sig[:, :cols], sig[:, cols:], fil[:, :cols], fil[:, cols:]
    both = jnp.concatenate([sr * fr - si * fi, sr * fi + si * fr], axis=1)
    spun = dot_halves(halves(both), (inv_ref[0], inv_ref[1]))
    turn = []
    for c in range(owned):
        real = spun[c * rows : (c + 1) * rows, :cols]
        imag = spun[c * rows : (c + 1) * rows, cols:]
        turn.append(jnp.concatenate([real * cos - imag * sin, real * sin + imag * cos], axis=0))
    conv = dot_halves(perm_t, halves(jnp.concatenate(turn, axis=1)))
    for c in range(owned):
        piece = conv[:, c * cols : (c + 1) * cols].reshape(count, own_rows, cols)
        result[:, c * own_rows : (c + 1) * own_rows, :] = piece
    keep_back.start()
    others(lambda target: send_back(target).start())
    others(lambda source: recv_back(source).wait_recv())
    keep_back.wait()
    width = skip_ref.shape[1]
    diagonal = iota((width, width), 0) == iota((width, width), 1)
    skip = jnp.sum(jnp.where(diagonal, skip_ref[...], 0.0), axis=1, keepdims=True)
    for o in range(0, gate.shape[0], 2):
        for t in range(own_rows):
            lanes = slice(t * cols, (t + 1) * cols)
            pieces = []
            for k in (o, o + 1):
                near = back[k, pl.ds(t, chans, stride=own_rows), :]
                pieces.append(gate[k, :, lanes] * (near + skip[k * chans : (k + 1) * chans] * prod[k, :, lanes]))
            hid[o * chans : (o + 2) * chans, lanes] = jnp.concatenate(pieces, axis=0).astype(jnp.bfloat16)
    hand = pltpu.make_async_remote_copy(
        src_ref=hid, dst_ref=hidden_ref.at[ch], send_sem=hid_send.at[0], recv_sem=hid_recv.at[0],
        device_id={"ch": 1 - ch}, device_id_type=ctx_dev,
    )
    hand.start()
    keep_hid.start()
    others(lambda target: send_taps(target).wait_send())
    others(lambda target: send_prod(target).wait_send())
    others(lambda target: send_back(target).wait_send())
    weights.finish()
    for out in outs:
        out.wait_passed(1)
        out.wait_passed(2)
        out.finish()
    keep_hid.wait()
    hand.wait()


def split_table(table):
    top = table.astype(jnp.bfloat16)
    low = (table - top.astype(np.float32)).astype(jnp.bfloat16)
    return np.stack([top, low])


def fused(tokens, in_weight, conv_filter, skip_gain, group_order, out_weight, count):
    tok_count, feat = tokens.shape
    chans = in_weight.shape[0]
    chan_local = conv_filter.shape[0]
    seq = tok_count * count
    rows, cols = split_length(seq)
    own_rows = tok_count // cols
    owned = chan_local // count
    sub = seq // group_order.shape[0] // cols
    freq = 4 * np.arange(rows) + 1

    def turns(numer, period):
        angle = (numer % period) * (2.0 * math.pi / period)
        return np.cos(angle).astype(np.float32), np.sin(angle).astype(np.float32)

    cos, sin = turns(freq[:, None] * np.arange(rows)[None, :], 4 * rows)
    row_dft = np.concatenate([cos, -sin], axis=0)
    cos, sin = turns(np.arange(cols)[:, None] * np.arange(cols)[None, :], cols)
    col_dft = np.concatenate([np.concatenate([cos, -sin], 1), np.concatenate([sin, cos], 1)], 0)
    col_inv = (col_dft.T / (rows * cols)).astype(np.float32)
    tw_cos, tw_sin = turns(freq[:, None] * np.arange(cols)[None, :], 4 * rows * cols)
    pairs = chan_local // chans
    hbm = pl.BlockSpec(memory_space=pl.ANY)
    f32, bf16 = jnp.float32, jnp.bfloat16
    packed = pltpu.VMEM((pairs, chans * own_rows, cols), f32)
    blocks = pltpu.VMEM((count, owned * own_rows, cols), f32)
    full = pltpu.VMEM((pairs, chans, tok_count), f32)
    strips = pltpu.VMEM((count // PLANE, PLANE * 3 * chans, tok_count), f32)
    each = pltpu.SemaphoreType.DMA((count,))
    hidden, rows_all = pl.pallas_call(
        functools.partial(fused_kernel, count, sub),
        out_shape=(
            jax.ShapeDtypeStruct((2, chan_local, tok_count), bf16),
            jax.ShapeDtypeStruct((count // PLANE, 2, 2, *out_weight.shape), bf16),
        ),
        in_specs=[hbm] * 10,
        out_specs=(hbm, hbm),
        scratch_shapes=[
            pltpu.VMEM((1, chan_local), f32),
            pltpu.VMEM((1, group_order.shape[0]), jnp.int32),
            pltpu.VMEM((2, *row_dft.shape), bf16),
            pltpu.VMEM((2, *col_dft.shape), bf16),
            pltpu.VMEM((2, *col_inv.shape), bf16),
            pltpu.VMEM((2, rows, cols), f32),
            pltpu.VMEM((count, 3, chans, feat), bf16),
            pltpu.VMEM((tok_count, feat), bf16),
            strips, strips, full, full, packed, full, packed, blocks, blocks, blocks, packed,
            pltpu.VMEM((chan_local, tok_count), bf16),
            pltpu.SemaphoreType.DMA((3, count, 4)),
            pltpu.SemaphoreType.DMA((3, count)),
            pltpu.SemaphoreType.DMA((2, 6)),
            pltpu.SemaphoreType.DMA((2, 7)),
            pltpu.SemaphoreType.DMA((count // PLANE, 4)),
            pltpu.SemaphoreType.DMA((count // PLANE, 4)),
            each, each, each, each, each, each,
            pltpu.SemaphoreType.DMA((1,)),
            pltpu.SemaphoreType.DMA((1,)),
            pltpu.SemaphoreType.DMA((14,)),
        ],
        compiler_params=pltpu.CompilerParams(collective_id=0, has_side_effects=True, vmem_limit_bytes=VMEM_LIMIT),
        name="fused",
    )(
        in_weight.transpose(1, 0, 2), tokens, out_weight, conv_filter.reshape(pairs, chans, tok_count),
        skip_gain.reshape(1, -1), group_order.reshape(1, -1), split_table(row_dft), split_table(col_dft),
        split_table(col_inv), np.stack([tw_cos, tw_sin]),
    )
    return hidden.reshape(2 * chan_local, tok_count), rows_all.reshape(-1, feat)


def mix_kernel(tile, wide, hidden_hbm, rows_hbm, out_ref, hidden, rows, tiles, sems):
    loads = [
        pltpu.make_async_copy(hidden_hbm, hidden, sems.at[0]),
        pltpu.make_async_copy(rows_hbm, rows, sems.at[1]),
    ]
    for copy in loads:
        copy.start()
    for copy in loads:
        copy.wait()
    stores = []
    for k in range(tiles.shape[0]):
        mine = hidden[:, k * tile : (k + 1) * tile]
        for at in range(0, tiles.shape[2], wide):
            tiles[k, :, at : at + wide] = lax.dot_general(
                mine, rows[:, at : at + wide], (((0,), (0,)), ((), ())), preferred_element_type=jnp.float32
            ).astype(tiles.dtype)
        stores.append(pltpu.make_async_copy(tiles.at[k], out_ref.at[pl.ds(k * tile, tile)], sems.at[2 + k]))
        stores[-1].start()
    for copy in stores:
        copy.wait()


def mix(hidden, rows, tile=64, wide=512):
    count, feat = hidden.shape[1], rows.shape[1]
    hbm = pl.BlockSpec(memory_space=pl.ANY)
    return pl.pallas_call(
        functools.partial(mix_kernel, tile, wide),
        out_shape=jax.ShapeDtypeStruct((count, feat), jnp.bfloat16),
        in_specs=[hbm, hbm],
        out_specs=hbm,
        scratch_shapes=[
            pltpu.VMEM(hidden.shape, hidden.dtype),
            pltpu.VMEM(rows.shape, rows.dtype),
            pltpu.VMEM((count // tile, tile, feat), jnp.bfloat16),
            pltpu.SemaphoreType.DMA((2 + count // tile,)),
        ],
        compiler_params=pltpu.CompilerParams(vmem_limit_bytes=VMEM_LIMIT),
        name="mix",
    )(hidden, rows)


def per_device(tokens, in_weight, conv_filter, skip_gain, group_order, out_weight):
    ctx = lax.axis_size("ctx")
    ch = lax.axis_size("ch")
    tok_count, feat_local = tokens.shape
    chan_local = conv_filter.shape[0]
    seq = tok_count * ctx
    group = seq // group_order.shape[0]
    rows, cols = split_length(seq)
    own_rows = tok_count // cols
    owned = -(-chan_local // ctx)
    padded = owned * ctx

    def parts_of(signal):
        signal = jnp.pad(signal, ((0, padded - chan_local), (0, 0)))
        return signal.reshape(ctx, owned, own_rows, cols)

    def swapped(parts):
        return lax.all_to_all(parts, "ctx", split_axis=0, concat_axis=0, tiled=True)

    relayed = ctx == RELAY_LIMIT and ch == 2 and in_weight.shape[0] == 8 and own_rows == 8 and padded == chan_local
    if relayed:
        hidden_all, rows_all = fused(tokens, in_weight, conv_filter, skip_gain, group_order, out_weight, ctx)
        return mix(hidden_all, rows_all)
    mine = in_weight.reshape(-1, feat_local)
    flat = lax.all_gather(mine, "ctx", axis=0, tiled=True)
    rows_all = lax.all_gather(out_weight, "ctx", axis=0, tiled=True)
    taps = swapped(parts_of(conv_filter))
    partial = lax.dot_general(flat, tokens, (((1,), (1,)), ((), ())), preferred_element_type=jnp.float32)
    if ch == 2:
        me = lax.axis_index("ch")
        half = partial.shape[0] // 2
        away = lax.dynamic_slice_in_dim(partial, (1 - me) * half, half, 0)
        kept = lax.dynamic_slice_in_dim(partial, me * half, half, 0)
        proj = kept + lax.ppermute(away, "ch", [(0, 1), (1, 0)])
    else:
        proj = lax.psum_scatter(partial, "ch", scatter_dimension=0, tiled=True)
    proj = proj.reshape(chan_local, 3, tok_count)
    gate = proj[:, 0]
    product = proj[:, 1] * proj[:, 2]
    in_group = jnp.arange(group // cols, dtype=jnp.int32)
    row_ids = (group_order[:, None] * (group // cols) + in_group[None, :]).reshape(rows)

    def grid(parts):
        return parts.transpose(0, 2, 1, 3).reshape(rows, owned, cols)

    conv = causal_conv(grid(swapped(parts_of(product))), grid(taps), row_ids)
    back = swapped(conv.reshape(ctx, own_rows, owned, cols).transpose(0, 2, 1, 3))
    conv = back.reshape(padded, tok_count)[:chan_local]
    hidden = (gate * (conv + skip_gain[:, None] * product)).astype(jnp.bfloat16)
    hidden_all = lax.all_gather(hidden, "ch", axis=0, tiled=True)
    mixed = lax.dot_general(
        hidden_all, rows_all, (((0,), (0,)), ((), ())), preferred_element_type=jnp.float32
    )
    return mixed.astype(jnp.bfloat16)


def solution(mesh):
    in_specs = (P("ctx", "ch"), P("ctx", None, "ch"), P("ch", "ctx"), P("ch"), P(), P("ctx", "ch"))
    return jax.shard_map(
        per_device, mesh=mesh, in_specs=in_specs, out_specs=P("ctx", "ch"), check_vma=False
    )
```

```python
import functools
import itertools
import math

import jax
import jax.numpy as jnp
import numpy as np
from jax import lax
from jax.experimental import pallas as pl
from jax.experimental.pallas import tpu as pltpu
from jax.sharding import PartitionSpec as P

high = lax.Precision.HIGH
RELAY_LIMIT = 16
VMEM_LIMIT = 63 * 2**20


def split_length(length):
    cols = 1 << ((length.bit_length() - 1) // 2)
    return length // cols, cols


def cos_sin(numer, period):
    angle = (numer % period).astype(jnp.float32) * (2.0 * math.pi / period)
    return jnp.cos(angle), jnp.sin(angle)


def row_table(row_ids, rows):
    freq = 4 * jnp.arange(rows, dtype=jnp.int32) + 1
    cos, sin = cos_sin(freq[:, None] * row_ids[None, :], 4 * rows)
    return jnp.concatenate([cos, -sin], axis=0)


def col_table(cols):
    ids = jnp.arange(cols, dtype=jnp.int32)
    cos, sin = cos_sin(ids[:, None] * ids[None, :], cols)
    top = jnp.concatenate([cos, -sin], axis=1)
    bottom = jnp.concatenate([sin, cos], axis=1)
    return jnp.concatenate([top, bottom], axis=0)


def twist(rows, cols):
    freq = 4 * jnp.arange(rows, dtype=jnp.int32) + 1
    return cos_sin(freq[:, None] * jnp.arange(cols, dtype=jnp.int32)[None, :], 4 * rows * cols)


def spectrum(values, row_dft, col_dft, tw):
    rows, chans, cols = values.shape
    cos, sin = tw[0][:, None, :], tw[1][:, None, :]
    part = jnp.dot(row_dft, values.reshape(rows, chans * cols), precision=high)
    real = part[:rows].reshape(rows, chans, cols)
    imag = part[rows:].reshape(rows, chans, cols)
    turned = jnp.concatenate([real * cos + imag * sin, imag * cos - real * sin], axis=2)
    out = jnp.dot(turned.reshape(rows * chans, 2 * cols), col_dft, precision=high)
    return out.reshape(rows, chans, 2 * cols)


def causal_conv(values, taps, row_ids):
    rows, chans, cols = values.shape
    col_dft = col_table(cols)
    tw = twist(rows, cols)
    perm_dft = row_table(row_ids, rows)
    sig = spectrum(values, perm_dft, col_dft, tw)
    fil = spectrum(taps, row_table(jnp.arange(rows, dtype=jnp.int32), rows), col_dft, tw)
    sr, si = sig[..., :cols], sig[..., cols:]
    fr, fi = fil[..., :cols], fil[..., cols:]
    both = jnp.concatenate([sr * fr - si * fi, sr * fi + si * fr], axis=2)
    back = jnp.dot(both.reshape(rows * chans, 2 * cols), col_dft.T, precision=high)
    back = back.reshape(rows, chans, 2 * cols) * (1.0 / (rows * cols))
    br, bi = back[..., :cols], back[..., cols:]
    cos, sin = tw[0][:, None, :], tw[1][:, None, :]
    turned = jnp.concatenate([br * cos - bi * sin, br * sin + bi * cos], axis=0)
    out = jnp.dot(perm_dft.T, turned.reshape(2 * rows, chans * cols), precision=high)
    return out.reshape(rows, chans, cols)


PLANE = 4
ACROSS, BESIDE = 2, 3


def plane_of(z, line, slot):
    low = z < line // 2
    w = jnp.where(low, z, line - 1 - z)
    near = (w, 1 - w, w * 0 + 2, w * 0 + 3)[slot]
    return jnp.where(low, near, line - 1 - near)


class Relay:
    reach = (0, 1, 1.6, 2.6)

    def __init__(self, line, own_ref, all_ref, columns, order, send_sems, recv_sems, slot):
        self.line, self.order, self.slot = line, order, slot
        self.own_ref, self.all_ref, self.columns = own_ref, all_ref, columns
        self.send_sems, self.recv_sems = send_sems, recv_sems
        me = lax.axis_index("ctx")
        self.me, self.z, self.y, self.x = me, me // 4, me // 2 % 2, me % 2

    def offsets(self):
        return itertools.product(range(self.line), (0, 1), (0, 1))

    def key(self, offset):
        return self.reach[offset[0]] + offset[1] + offset[2]

    def origin(self, offset):
        dz, dy, dx = offset
        y = 1 - self.y if dy else self.y
        x = 1 - self.x if dx else self.x
        return plane_of(self.z, self.line, dz) * PLANE + y * 2 + x

    def at(self, ref, *lead):
        whole = (slice(None),) * (len(self.own_ref.shape) - 1)
        return ref.at[(*lead, *whole, self.columns)]

    def exits(self, offset):
        along = [k for k, dim in enumerate(self.order) if offset[dim] != 0]
        last = along[-1] if along else -1
        out = []
        if last >= 0 and self.order[last] == 0:
            out.append("on")
        for dim in self.order[last + 1 :]:
            out += (["up", "down"], [ACROSS], [BESIDE])[dim]
        return out

    def copy(self, offset, way):
        origin = self.origin(offset)
        up = self.me + PLANE
        down = self.me - PLANE
        own = all(step == 0 for step in offset)
        if way == "on":
            rising = plane_of(self.z, self.line, offset[0]) < self.z
            target, index = jnp.where(rising, up, down), jnp.where(rising, 0, 1)
        elif way in ("up", "down"):
            target, index = (up, 0) if way == "up" else (down, 1)
        else:
            target = self.me + 2 - 4 * self.y if way == ACROSS else self.me + 1 - 2 * self.x
            index = way
        return pltpu.make_async_remote_copy(
            src_ref=self.at(self.own_ref) if own else self.at(self.all_ref, origin),
            dst_ref=self.at(self.all_ref, origin),
            send_sem=self.send_sems.at[self.slot, origin, index],
            recv_sem=self.recv_sems.at[self.slot, origin],
            device_id={"ctx": target},
            device_id_type=pl.DeviceIdType.MESH,
        )

    def each_exit(self, offset, act):
        for way in self.exits(offset):
            copy = self.copy(offset, way)
            if way not in ("on", "up", "down"):
                act(copy)
                continue
            room_up, room_down = self.z + 1 < self.line, self.z > 0
            if way == "on":
                rising = plane_of(self.z, self.line, offset[0]) < self.z
                test = jnp.where(rising, room_up, room_down)
            else:
                test = room_up if way == "up" else room_down

            @pl.when(test)
            def _():
                act(copy)

    def begin(self):
        self.each_exit((0, 0, 0), lambda copy: copy.start())

    def step(self, offset):
        self.copy(offset, BESIDE).wait_recv()
        self.each_exit(offset, lambda copy: copy.start())

    def finish(self):
        for offset in self.offsets():
            self.each_exit(offset, lambda copy: copy.wait_send())


class Rounds:
    def __init__(self, relays):
        self.relays = relays
        todo = [(r.key(o), k, o) for k, r in enumerate(relays) for o in r.offsets() if any(o)]
        self.todo = sorted(todo, key=lambda item: item[:2])

    def begin(self):
        for relay in self.relays:
            relay.begin()

    def upto(self, limit):
        while self.todo and self.todo[0][0] < limit + 0.01:
            _, k, offset = self.todo.pop(0)
            self.relays[k].step(offset)

    def finish(self):
        for relay in self.relays:
            relay.finish()


class Spread:
    def __init__(self, line, own_ref, all_ref, columns, order, send_sems, recv_sems, slot):
        self.line, self.order, self.slot = line, order, slot
        self.own_ref, self.all_ref, self.columns = own_ref, all_ref, columns
        self.send_sems, self.recv_sems = send_sems, recv_sems
        me = lax.axis_index("ctx")
        self.me, self.z, self.y, self.x = me, me // 4, me // 2 % 2, me % 2

    def column(self, near, far):
        flips = {self.order[1]: near, self.order[2]: far}
        y = 1 - self.y if flips[1] else self.y
        x = 1 - self.x if flips[2] else self.x
        return self.all_ref.at[:, y, x, :, self.columns]

    def ship(self, source, place, target, send, recv):
        return pltpu.make_async_remote_copy(
            src_ref=source, dst_ref=place,
            send_sem=self.send_sems.at[self.slot, send], recv_sem=self.recv_sems.at[self.slot, recv],
            device_id={"ctx": target}, device_id_type=pl.DeviceIdType.MESH,
        )

    def lift(self, slot, into):
        z = plane_of(self.z, self.line, slot)
        mine = self.all_ref.at[self.z, self.y, self.x, :, self.columns]
        theirs = self.all_ref.at[z, self.y, self.x, :, self.columns]
        target = self.me + (z - self.z) * PLANE
        if into:
            return self.ship(theirs, theirs, target, slot - 1, z)
        return self.ship(self.own_ref.at[:, self.columns], mine, target, slot - 1, self.z)

    def pass_on(self, kind, into):
        near, far = ((1, 0), (0, 1), (1, 1))[kind]
        dim = self.order[1 if kind == 0 else 2]
        target = self.me + 2 - 4 * self.y if dim == 1 else self.me + 1 - 2 * self.x
        held, lands = self.column(near * far, 0), self.column(near, far)
        send, recv = self.line - 1 + kind, self.line + kind
        place = lands if into else held
        return self.ship(place, place, target, send, recv)

    def moves(self, stage, into=False):
        if stage == 0:
            return [self.lift(slot, into) for slot in range(1, self.line)]
        return [self.pass_on(kind, into) for kind in ((), (0, 1), (2,))[stage]]

    def begin(self, stage):
        for out in self.moves(stage):
            out.start()

    def wait_lifted(self):
        for into in self.moves(0, True):
            into.wait_recv()

    def wait_passed(self, kind):
        self.pass_on(kind, True).wait_recv()

    def finish(self):
        for stage in range(3):
            for out in self.moves(stage):
                out.wait_send()


def greet_all(count):
    me, ch = lax.axis_index("ctx"), lax.axis_index("ch")
    barrier = pltpu.get_barrier_semaphore()

    @pl.loop(1, count)
    def _(step):
        pl.semaphore_signal(
            barrier, inc=1, device_id={"ctx": lax.rem(me + step, count)}, device_id_type=pl.DeviceIdType.MESH
        )

    pl.semaphore_signal(barrier, inc=1, device_id={"ch": 1 - ch}, device_id_type=pl.DeviceIdType.MESH)
    return lambda: pl.semaphore_wait(barrier, count)


def halves(v):
    top = v.astype(jnp.bfloat16)
    return top, (v - top.astype(jnp.float32)).astype(jnp.bfloat16)


def dot_halves(a, b):
    dot = functools.partial(jnp.dot, preferred_element_type=jnp.float32)
    return dot(a[0], b[0]) + (dot(a[0], b[1]) + dot(a[1], b[0]))


def fused_kernel(
    count, sub, in_ref, tok_ref, out_ref, taps_ref, skip_hbm, order_hbm, row_hbm, col_hbm, inv_hbm, turn_hbm,
    hidden_ref, rows_ref,
    skip_ref, order_ref, row_ref, col_ref, inv_ref, turn_ref, in_all, tok, part, inbox, gate, prod, sorted_prod, stage, taps_in, taps_stage, taps_got, got, result, back, back_wide, hid,
    relay_send, relay_recv, out_send, out_recv, pair_send, pair_recv, taps_send, taps_recv, prod_send, prod_recv,
    back_send, back_recv, hid_send, hid_recv, local_sems,
):
    me, ch = lax.axis_index("ctx"), lax.axis_index("ch")
    line = count // PLANE
    z = me // PLANE
    rows, cols = turn_ref.shape[1:]
    own_rows = tok_ref.shape[0] // cols
    owned = got.shape[1] // own_rows
    chans = in_ref.shape[1]
    pack = got.shape[1]
    pairs = stage.shape[0]
    wide = in_ref.shape[2]
    tokens = tok_ref.shape[0]
    ctx_dev = pl.DeviceIdType.MESH

    def cut(*shares):
        edges = [wide * sum(shares[:k]) // sum(shares) for k in range(len(shares) + 1)]
        return [pl.ds(a, b - a) for a, b in zip(edges, edges[1:])]

    first, second, third = cut(6, 7, 3)
    left, right = cut(1, 1)
    weights = Rounds([
        Relay(line, in_ref, in_all, third, (1, 2, 0), relay_send, relay_recv, 2),
        Relay(line, in_ref, in_all, first, (0, 1, 2), relay_send, relay_recv, 0),
        Relay(line, in_ref, in_all, second, (0, 2, 1), relay_send, relay_recv, 1),
    ])
    outs = [
        Spread(line, out_ref, rows_ref, left, (0, 1, 2), out_send, out_recv, 0),
        Spread(line, out_ref, rows_ref, right, (0, 2, 1), out_send, out_recv, 1),
    ]

    def group(ref, g):
        return ref.at[g // 2, pl.ds(pl.multiple_of(lax.rem(g, 2) * pack, pack), pack)]

    load_taps = pltpu.make_async_copy(taps_ref, taps_in, local_sems.at[0])
    load_in = pltpu.make_async_copy(in_ref, in_all.at[me], local_sems.at[1])
    load_tok = pltpu.make_async_copy(tok_ref, tok, local_sems.at[2])
    load_out = pltpu.make_async_copy(out_ref, rows_ref.at[me // PLANE, me // 2 % 2, me % 2], local_sems.at[3])
    keep_taps = pltpu.make_async_copy(group(taps_stage, me), taps_got.at[me], local_sems.at[4])
    keep_prod = pltpu.make_async_copy(group(stage, me), got.at[me], local_sems.at[5])
    keep_back = pltpu.make_async_copy(result.at[me], group(back, me), local_sems.at[6])
    keep_hid = pltpu.make_async_copy(hid, hidden_ref.at[ch], local_sems.at[7])

    tables = [
        pltpu.make_async_copy(src, dst, local_sems.at[8 + k])
        for k, (src, dst) in enumerate([
            (order_hbm, order_ref), (row_hbm, row_ref), (col_hbm, col_ref),
            (inv_hbm, inv_ref), (turn_hbm, turn_ref), (skip_hbm, skip_ref),
        ])
    ]
    all_in = greet_all(count)
    load_taps.start()
    load_in.start()
    load_tok.start()
    load_out.start()
    for copy in tables:
        copy.start()
    all_in()
    weights.begin()

    def send_taps(target):
        return pltpu.make_async_remote_copy(
            src_ref=group(taps_stage, target), dst_ref=taps_got.at[me],
            send_sem=taps_send.at[target], recv_sem=taps_recv.at[me],
            device_id={"ctx": target}, device_id_type=ctx_dev,
        )

    def recv_taps(source):
        return pltpu.make_async_remote_copy(
            src_ref=group(taps_stage, source), dst_ref=taps_got.at[source],
            send_sem=taps_send.at[source], recv_sem=taps_recv.at[source],
            device_id={"ctx": source}, device_id_type=ctx_dev,
        )

    def send_prod(target):
        return pltpu.make_async_remote_copy(
            src_ref=group(stage, target), dst_ref=got.at[me],
            send_sem=prod_send.at[target], recv_sem=prod_recv.at[me],
            device_id={"ctx": target}, device_id_type=ctx_dev,
        )

    def recv_prod(source):
        return pltpu.make_async_remote_copy(
            src_ref=group(stage, source), dst_ref=got.at[source],
            send_sem=prod_send.at[source], recv_sem=prod_recv.at[source],
            device_id={"ctx": source}, device_id_type=ctx_dev,
        )

    def send_back(target):
        return pltpu.make_async_remote_copy(
            src_ref=result.at[target], dst_ref=group(back, me),
            send_sem=back_send.at[target], recv_sem=back_recv.at[me],
            device_id={"ctx": target}, device_id_type=ctx_dev,
        )

    def recv_back(source):
        return pltpu.make_async_remote_copy(
            src_ref=result.at[source], dst_ref=group(back, source),
            send_sem=back_send.at[source], recv_sem=back_recv.at[source],
            device_id={"ctx": source}, device_id_type=ctx_dev,
        )

    def others(act):
        @pl.loop(1, count)
        def _(step):
            act(lax.rem(me + step, count))

    def spread(values, ref, o, begin=0):
        for t in range(values.shape[1] // cols):
            ref[o, pl.ds(begin + t, chans, stride=own_rows), :] = values[:, t * cols : (t + 1) * cols]

    load_taps.wait()
    for o in range(taps_in.shape[0]):
        spread(taps_in[o], taps_stage, o)
    keep_taps.start()
    others(lambda target: send_taps(target).start())

    parts = 4
    share = tokens // parts

    block = pairs * 3 * chans

    def owner(late):
        low = z < line // 2
        return jnp.where(low, 1, 0) if late else jnp.where(low, 0, 1)

    def pair(late, n):
        lanes = slice(n * share, (n + 1) * share)
        return pltpu.make_async_remote_copy(
            src_ref=part.at[late, :, lanes], dst_ref=inbox.at[:, lanes],
            send_sem=pair_send.at[late, n], recv_sem=pair_recv.at[n],
            device_id={"ch": 1 - ch}, device_id_type=ctx_dev,
        )

    def project(late, *pieces):
        for n in pieces:
            mine = in_all[pl.ds(owner(late) * pairs, pairs)].reshape(block, wide)
            part[late, :, n * share : (n + 1) * share] = lax.dot_general(
                mine, tok[n * share : (n + 1) * share, :], (((1,), (1,)), ((), ())),
                preferred_element_type=jnp.float32,
            )

            @pl.when(owner(late) != ch)
            def _():
                pair(late, n).start()

    def consume(late, *pieces):
        @pl.when(owner(late) == ch)
        def _():
            for n in pieces:
                pair(late, n).wait_recv()
                lanes = slice(n * share, (n + 1) * share)
                for o in range(pairs):
                    near, key, value = [
                        part[late, pl.ds((3 * o + m) * chans, chans), lanes]
                        + inbox[pl.ds((3 * o + m) * chans, chans), lanes]
                        for m in range(3)
                    ]
                    gate[o, :, lanes] = near
                    values = key * value
                    prod[o, :, lanes] = values
                    spread(values, sorted_prod, o, n * share // cols)

    def send_products(late):
        @pl.when(owner(late) == ch)
        def _():
            stage[...] = sorted_prod[...].astype(stage.dtype)
            others(lambda target: send_prod(target).start())
            keep_prod.start()

        @pl.when(owner(late) != ch)
        def _():
            for n in range(parts):
                pair(late, n).wait_send()

    def iota(shape, dim):
        return lax.broadcasted_iota(jnp.int32, shape, dim)

    weights.upto(1)
    for copy in tables:
        copy.wait()
    blocks = order_ref.shape[1]
    hot = jnp.where(iota((blocks, blocks), 0) == order_ref[...], 1.0, 0.0).astype(jnp.bfloat16)
    down = jnp.where(iota((rows, blocks), 0) // sub == iota((rows, blocks), 1), 1.0, 0.0).astype(jnp.bfloat16)
    over = jnp.where(iota((blocks, rows), 1) // sub == iota((blocks, rows), 0), 1.0, 0.0).astype(jnp.bfloat16)
    dot = functools.partial(jnp.dot, preferred_element_type=jnp.float32)
    moved = dot(dot(down, hot).astype(jnp.bfloat16), over)
    same = lax.rem(iota((rows, rows), 0), sub) == lax.rem(iota((rows, rows), 1), sub)
    moved = jnp.where(same, moved, 0.0).astype(jnp.bfloat16)
    perm_wide = [dot(row_ref[k], moved) for k in range(2)]
    perm = [v.astype(jnp.bfloat16) for v in perm_wide]
    perm_t = [v.T.astype(jnp.bfloat16) for v in perm_wide]
    cos, sin = turn_ref[0], turn_ref[1]

    def transform(ref, table):
        values = ref[...].astype(jnp.float32)
        stacked = jnp.concatenate(
            [values[:, c * own_rows : (c + 1) * own_rows, :].reshape(rows, cols) for c in range(owned)], axis=1
        )
        if ref.dtype == jnp.bfloat16:
            stacked = stacked.astype(jnp.bfloat16)
            turn = dot(table[0], stacked) + dot(table[1], stacked)
        else:
            turn = dot_halves(table, halves(stacked))
        out = []
        for c in range(owned):
            real = turn[:rows, c * cols : (c + 1) * cols]
            imag = turn[rows:, c * cols : (c + 1) * cols]
            out.append(jnp.concatenate([real * cos + imag * sin, imag * cos - real * sin], axis=1))
        return dot_halves(halves(jnp.concatenate(out, axis=0)), (col_ref[0], col_ref[1]))

    weights.upto(2.6)
    load_in.wait()
    load_tok.wait()
    others(lambda source: recv_taps(source).wait_recv())
    keep_taps.wait()
    fil = transform(taps_got, (row_ref[0], row_ref[1]))
    weights.upto(3)
    for out in outs:
        out.begin(0)
    project(0, 0, 1)
    weights.upto(3.6)
    project(0, 2, 3)
    consume(0, 0, 1, 2, 3)
    send_products(0)
    weights.upto(9)
    load_out.wait()
    for out in outs:
        out.wait_lifted()
        out.begin(1)
    project(1, 0, 1)
    consume(1, 0)
    project(1, 2)
    consume(1, 1)
    project(1, 3)
    consume(1, 2, 3)
    send_products(1)
    others(lambda source: recv_prod(source).wait_recv())
    keep_prod.wait()
    sig = transform(got, perm)
    sr, si, fr, fi = sig[:, :cols], sig[:, cols:], fil[:, :cols], fil[:, cols:]
    both = jnp.concatenate([sr * fr - si * fi, sr * fi + si * fr], axis=1)
    spun = dot_halves(halves(both), (inv_ref[0], inv_ref[1]))
    turn = []
    for c in range(owned):
        real = spun[c * rows : (c + 1) * rows, :cols]
        imag = spun[c * rows : (c + 1) * rows, cols:]
        turn.append(jnp.concatenate([real * cos - imag * sin, real * sin + imag * cos], axis=0))
    conv = dot_halves(perm_t, halves(jnp.concatenate(turn, axis=1)))
    pieces = [conv[:, c * cols : (c + 1) * cols].reshape(count, own_rows, cols) for c in range(owned)]
    result[...] = jnp.concatenate(pieces, axis=1).astype(result.dtype)
    keep_back.start()
    others(lambda target: send_back(target).start())
    for out in outs:
        out.wait_passed(0)
        out.begin(2)
    others(lambda source: recv_back(source).wait_recv())
    keep_back.wait()
    back_wide[...] = back[...].astype(jnp.float32)
    width = skip_ref.shape[1]
    diagonal = iota((width, width), 0) == iota((width, width), 1)
    skip = jnp.sum(jnp.where(diagonal, skip_ref[...], 0.0), axis=1, keepdims=True)
    for o in range(0, gate.shape[0], 2):
        for t in range(own_rows):
            lanes = slice(t * cols, (t + 1) * cols)
            pieces = []
            for k in (o, o + 1):
                near = back_wide[k, pl.ds(t, chans, stride=own_rows), :]
                pieces.append(gate[k, :, lanes] * (near + skip[k * chans : (k + 1) * chans] * prod[k, :, lanes]))
            hid[o * chans : (o + 2) * chans, lanes] = jnp.concatenate(pieces, axis=0).astype(jnp.bfloat16)
    hand = pltpu.make_async_remote_copy(
        src_ref=hid, dst_ref=hidden_ref.at[ch], send_sem=hid_send.at[0], recv_sem=hid_recv.at[0],
        device_id={"ch": 1 - ch}, device_id_type=ctx_dev,
    )
    hand.start()
    keep_hid.start()
    others(lambda target: send_taps(target).wait_send())
    others(lambda target: send_prod(target).wait_send())
    others(lambda target: send_back(target).wait_send())
    weights.finish()
    for out in outs:
        out.wait_passed(1)
        out.wait_passed(2)
        out.finish()
    keep_hid.wait()
    hand.wait()


def split_table(table):
    top = table.astype(jnp.bfloat16)
    low = (table - top.astype(np.float32)).astype(jnp.bfloat16)
    return np.stack([top, low])


def fused(tokens, in_weight, conv_filter, skip_gain, group_order, out_weight, count):
    tok_count, feat = tokens.shape
    chans = in_weight.shape[0]
    chan_local = conv_filter.shape[0]
    seq = tok_count * count
    rows, cols = split_length(seq)
    own_rows = tok_count // cols
    owned = chan_local // count
    sub = seq // group_order.shape[0] // cols
    freq = 4 * np.arange(rows) + 1

    def turns(numer, period):
        angle = (numer % period) * (2.0 * math.pi / period)
        return np.cos(angle).astype(np.float32), np.sin(angle).astype(np.float32)

    cos, sin = turns(freq[:, None] * np.arange(rows)[None, :], 4 * rows)
    row_dft = np.concatenate([cos, -sin], axis=0)
    cos, sin = turns(np.arange(cols)[:, None] * np.arange(cols)[None, :], cols)
    col_dft = np.concatenate([np.concatenate([cos, -sin], 1), np.concatenate([sin, cos], 1)], 0)
    col_inv = (col_dft.T / (rows * cols)).astype(np.float32)
    tw_cos, tw_sin = turns(freq[:, None] * np.arange(cols)[None, :], 4 * rows * cols)
    pairs = chan_local // chans
    hbm = pl.BlockSpec(memory_space=pl.ANY)
    f32, bf16 = jnp.float32, jnp.bfloat16
    packed, slim = [pltpu.VMEM((pairs, chans * own_rows, cols), kind) for kind in (f32, bf16)]
    blocks, short = [pltpu.VMEM((count, owned * own_rows, cols), kind) for kind in (f32, bf16)]
    full = pltpu.VMEM((pairs, chans, tok_count), f32)
    strips = pltpu.VMEM((2, pairs * 3 * chans, tok_count), f32)
    strip = pltpu.VMEM((pairs * 3 * chans, tok_count), f32)
    each = pltpu.SemaphoreType.DMA((count,))
    hidden, rows_all = pl.pallas_call(
        functools.partial(fused_kernel, count, sub),
        out_shape=(
            jax.ShapeDtypeStruct((2, chan_local, tok_count), bf16),
            jax.ShapeDtypeStruct((count // PLANE, 2, 2, *out_weight.shape), bf16),
        ),
        in_specs=[hbm] * 10,
        out_specs=(hbm, hbm),
        scratch_shapes=[
            pltpu.VMEM((1, chan_local), f32),
            pltpu.VMEM((1, group_order.shape[0]), jnp.int32),
            pltpu.VMEM((2, *row_dft.shape), bf16),
            pltpu.VMEM((2, *col_dft.shape), bf16),
            pltpu.VMEM((2, *col_inv.shape), bf16),
            pltpu.VMEM((2, rows, cols), f32),
            pltpu.VMEM((count, 3, chans, feat), bf16),
            pltpu.VMEM((tok_count, feat), bf16),
            strips, strip, full, full, packed, slim, full, packed, blocks, short, short, slim, packed,
            pltpu.VMEM((chan_local, tok_count), bf16),
            pltpu.SemaphoreType.DMA((3, count, 4)),
            pltpu.SemaphoreType.DMA((3, count)),
            pltpu.SemaphoreType.DMA((2, 6)),
            pltpu.SemaphoreType.DMA((2, 7)),
            pltpu.SemaphoreType.DMA((2, 4)),
            pltpu.SemaphoreType.DMA((4,)),
            each, each, each, each, each, each,
            pltpu.SemaphoreType.DMA((1,)),
            pltpu.SemaphoreType.DMA((1,)),
            pltpu.SemaphoreType.DMA((14,)),
        ],
        compiler_params=pltpu.CompilerParams(collective_id=0, has_side_effects=True, vmem_limit_bytes=VMEM_LIMIT),
        name="fused",
    )(
        in_weight.transpose(1, 0, 2), tokens, out_weight, conv_filter.reshape(pairs, chans, tok_count),
        skip_gain.reshape(1, -1), group_order.reshape(1, -1), split_table(row_dft), split_table(col_dft),
        split_table(col_inv), np.stack([tw_cos, tw_sin]),
    )
    return hidden.reshape(2 * chan_local, tok_count), rows_all.reshape(-1, feat)


def mix_kernel(tile, wide, hidden_hbm, rows_hbm, out_ref, hidden, rows, tiles, sems):
    loads = [
        pltpu.make_async_copy(hidden_hbm, hidden, sems.at[0]),
        pltpu.make_async_copy(rows_hbm, rows, sems.at[1]),
    ]
    for copy in loads:
        copy.start()
    for copy in loads:
        copy.wait()
    stores = []
    for k in range(tiles.shape[0]):
        mine = hidden[:, k * tile : (k + 1) * tile]
        for at in range(0, tiles.shape[2], wide):
            tiles[k, :, at : at + wide] = lax.dot_general(
                mine, rows[:, at : at + wide], (((0,), (0,)), ((), ())), preferred_element_type=jnp.float32
            ).astype(tiles.dtype)
        stores.append(pltpu.make_async_copy(tiles.at[k], out_ref.at[pl.ds(k * tile, tile)], sems.at[2 + k]))
        stores[-1].start()
    for copy in stores:
        copy.wait()


def mix(hidden, rows, tile=64, wide=512):
    count, feat = hidden.shape[1], rows.shape[1]
    hbm = pl.BlockSpec(memory_space=pl.ANY)
    return pl.pallas_call(
        functools.partial(mix_kernel, tile, wide),
        out_shape=jax.ShapeDtypeStruct((count, feat), jnp.bfloat16),
        in_specs=[hbm, hbm],
        out_specs=hbm,
        scratch_shapes=[
            pltpu.VMEM(hidden.shape, hidden.dtype),
            pltpu.VMEM(rows.shape, rows.dtype),
            pltpu.VMEM((count // tile, tile, feat), jnp.bfloat16),
            pltpu.SemaphoreType.DMA((2 + count // tile,)),
        ],
        compiler_params=pltpu.CompilerParams(vmem_limit_bytes=VMEM_LIMIT),
        name="mix",
    )(hidden, rows)


def per_device(tokens, in_weight, conv_filter, skip_gain, group_order, out_weight):
    ctx = lax.axis_size("ctx")
    ch = lax.axis_size("ch")
    tok_count, feat_local = tokens.shape
    chan_local = conv_filter.shape[0]
    seq = tok_count * ctx
    group = seq // group_order.shape[0]
    rows, cols = split_length(seq)
    own_rows = tok_count // cols
    owned = -(-chan_local // ctx)
    padded = owned * ctx

    def parts_of(signal):
        signal = jnp.pad(signal, ((0, padded - chan_local), (0, 0)))
        return signal.reshape(ctx, owned, own_rows, cols)

    def swapped(parts):
        return lax.all_to_all(parts, "ctx", split_axis=0, concat_axis=0, tiled=True)

    relayed = ctx == RELAY_LIMIT and ch == 2 and in_weight.shape[0] == 8 and own_rows == 8 and padded == chan_local
    if relayed:
        hidden_all, rows_all = fused(tokens, in_weight, conv_filter, skip_gain, group_order, out_weight, ctx)
        return mix(hidden_all, rows_all)
    mine = in_weight.reshape(-1, feat_local)
    flat = lax.all_gather(mine, "ctx", axis=0, tiled=True)
    rows_all = lax.all_gather(out_weight, "ctx", axis=0, tiled=True)
    taps = swapped(parts_of(conv_filter))
    partial = lax.dot_general(flat, tokens, (((1,), (1,)), ((), ())), preferred_element_type=jnp.float32)
    if ch == 2:
        me = lax.axis_index("ch")
        half = partial.shape[0] // 2
        away = lax.dynamic_slice_in_dim(partial, (1 - me) * half, half, 0)
        kept = lax.dynamic_slice_in_dim(partial, me * half, half, 0)
        proj = kept + lax.ppermute(away, "ch", [(0, 1), (1, 0)])
    else:
        proj = lax.psum_scatter(partial, "ch", scatter_dimension=0, tiled=True)
    proj = proj.reshape(chan_local, 3, tok_count)
    gate = proj[:, 0]
    product = proj[:, 1] * proj[:, 2]
    in_group = jnp.arange(group // cols, dtype=jnp.int32)
    row_ids = (group_order[:, None] * (group // cols) + in_group[None, :]).reshape(rows)

    def grid(parts):
        return parts.transpose(0, 2, 1, 3).reshape(rows, owned, cols)

    conv = causal_conv(grid(swapped(parts_of(product))), grid(taps), row_ids)
    back = swapped(conv.reshape(ctx, own_rows, owned, cols).transpose(0, 2, 1, 3))
    conv = back.reshape(padded, tok_count)[:chan_local]
    hidden = (gate * (conv + skip_gain[:, None] * product)).astype(jnp.bfloat16)
    hidden_all = lax.all_gather(hidden, "ch", axis=0, tiled=True)
    mixed = lax.dot_general(
        hidden_all, rows_all, (((0,), (0,)), ((), ())), preferred_element_type=jnp.float32
    )
    return mixed.astype(jnp.bfloat16)


def solution(mesh):
    in_specs = (P("ctx", "ch"), P("ctx", None, "ch"), P("ch", "ctx"), P("ch"), P(), P("ctx", "ch"))
    return jax.shard_map(
        per_device, mesh=mesh, in_specs=in_specs, out_specs=P("ctx", "ch"), check_vma=False
    )
```

```python
import functools
import itertools
import math

import jax
import jax.numpy as jnp
import numpy as np
from jax import lax
from jax.experimental import pallas as pl
from jax.experimental.pallas import tpu as pltpu
from jax.sharding import PartitionSpec as P

high = lax.Precision.HIGH
RELAY_LIMIT = 16
VMEM_LIMIT = 63 * 2**20


def split_length(length):
    cols = 1 << ((length.bit_length() - 1) // 2)
    return length // cols, cols


def cos_sin(numer, period):
    angle = (numer % period).astype(jnp.float32) * (2.0 * math.pi / period)
    return jnp.cos(angle), jnp.sin(angle)


def row_table(row_ids, rows):
    freq = 4 * jnp.arange(rows, dtype=jnp.int32) + 1
    cos, sin = cos_sin(freq[:, None] * row_ids[None, :], 4 * rows)
    return jnp.concatenate([cos, -sin], axis=0)


def col_table(cols):
    ids = jnp.arange(cols, dtype=jnp.int32)
    cos, sin = cos_sin(ids[:, None] * ids[None, :], cols)
    top = jnp.concatenate([cos, -sin], axis=1)
    bottom = jnp.concatenate([sin, cos], axis=1)
    return jnp.concatenate([top, bottom], axis=0)


def twist(rows, cols):
    freq = 4 * jnp.arange(rows, dtype=jnp.int32) + 1
    return cos_sin(freq[:, None] * jnp.arange(cols, dtype=jnp.int32)[None, :], 4 * rows * cols)


def spectrum(values, row_dft, col_dft, tw):
    rows, chans, cols = values.shape
    cos, sin = tw[0][:, None, :], tw[1][:, None, :]
    part = jnp.dot(row_dft, values.reshape(rows, chans * cols), precision=high)
    real = part[:rows].reshape(rows, chans, cols)
    imag = part[rows:].reshape(rows, chans, cols)
    turned = jnp.concatenate([real * cos + imag * sin, imag * cos - real * sin], axis=2)
    out = jnp.dot(turned.reshape(rows * chans, 2 * cols), col_dft, precision=high)
    return out.reshape(rows, chans, 2 * cols)


def causal_conv(values, taps, row_ids):
    rows, chans, cols = values.shape
    col_dft = col_table(cols)
    tw = twist(rows, cols)
    perm_dft = row_table(row_ids, rows)
    sig = spectrum(values, perm_dft, col_dft, tw)
    fil = spectrum(taps, row_table(jnp.arange(rows, dtype=jnp.int32), rows), col_dft, tw)
    sr, si = sig[..., :cols], sig[..., cols:]
    fr, fi = fil[..., :cols], fil[..., cols:]
    both = jnp.concatenate([sr * fr - si * fi, sr * fi + si * fr], axis=2)
    back = jnp.dot(both.reshape(rows * chans, 2 * cols), col_dft.T, precision=high)
    back = back.reshape(rows, chans, 2 * cols) * (1.0 / (rows * cols))
    br, bi = back[..., :cols], back[..., cols:]
    cos, sin = tw[0][:, None, :], tw[1][:, None, :]
    turned = jnp.concatenate([br * cos - bi * sin, br * sin + bi * cos], axis=0)
    out = jnp.dot(perm_dft.T, turned.reshape(2 * rows, chans * cols), precision=high)
    return out.reshape(rows, chans, cols)


PLANE = 4
ACROSS, BESIDE = 2, 3


def plane_of(z, line, slot):
    low = z < line // 2
    w = jnp.where(low, z, line - 1 - z)
    near = (w, 1 - w, w * 0 + 2, w * 0 + 3)[slot]
    return jnp.where(low, near, line - 1 - near)


class Relay:
    reach = (0, 1, 1.6, 2.6)

    def __init__(self, line, own_ref, all_ref, columns, order, send_sems, recv_sems, slot):
        self.line, self.order, self.slot = line, order, slot
        self.own_ref, self.all_ref, self.columns = own_ref, all_ref, columns
        self.send_sems, self.recv_sems = send_sems, recv_sems
        me = lax.axis_index("ctx")
        self.me, self.z, self.y, self.x = me, me // 4, me // 2 % 2, me % 2

    def offsets(self):
        return itertools.product(range(self.line), (0, 1), (0, 1))

    def key(self, offset):
        return self.reach[offset[0]] + offset[1] + offset[2]

    def origin(self, offset):
        dz, dy, dx = offset
        y = 1 - self.y if dy else self.y
        x = 1 - self.x if dx else self.x
        return plane_of(self.z, self.line, dz) * PLANE + y * 2 + x

    def at(self, ref, *lead):
        whole = (slice(None),) * (len(self.own_ref.shape) - 1)
        return ref.at[(*lead, *whole, self.columns)]

    def exits(self, offset):
        along = [k for k, dim in enumerate(self.order) if offset[dim] != 0]
        last = along[-1] if along else -1
        out = []
        if last >= 0 and self.order[last] == 0:
            out.append("on")
        for dim in self.order[last + 1 :]:
            out += (["up", "down"], [ACROSS], [BESIDE])[dim]
        return out

    def copy(self, offset, way):
        origin = self.origin(offset)
        up = self.me + PLANE
        down = self.me - PLANE
        own = all(step == 0 for step in offset)
        if way == "on":
            rising = plane_of(self.z, self.line, offset[0]) < self.z
            target, index = jnp.where(rising, up, down), jnp.where(rising, 0, 1)
        elif way in ("up", "down"):
            target, index = (up, 0) if way == "up" else (down, 1)
        else:
            target = self.me + 2 - 4 * self.y if way == ACROSS else self.me + 1 - 2 * self.x
            index = way
        return pltpu.make_async_remote_copy(
            src_ref=self.at(self.own_ref) if own else self.at(self.all_ref, origin),
            dst_ref=self.at(self.all_ref, origin),
            send_sem=self.send_sems.at[self.slot, origin, index],
            recv_sem=self.recv_sems.at[self.slot, origin],
            device_id={"ctx": target},
            device_id_type=pl.DeviceIdType.MESH,
        )

    def each_exit(self, offset, act):
        for way in self.exits(offset):
            copy = self.copy(offset, way)
            if way not in ("on", "up", "down"):
                act(copy)
                continue
            room_up, room_down = self.z + 1 < self.line, self.z > 0
            if way == "on":
                rising = plane_of(self.z, self.line, offset[0]) < self.z
                test = jnp.where(rising, room_up, room_down)
            else:
                test = room_up if way == "up" else room_down

            @pl.when(test)
            def _():
                act(copy)

    def begin(self):
        self.each_exit((0, 0, 0), lambda copy: copy.start())

    def step(self, offset):
        self.copy(offset, BESIDE).wait_recv()
        self.each_exit(offset, lambda copy: copy.start())

    def finish(self):
        for offset in self.offsets():
            self.each_exit(offset, lambda copy: copy.wait_send())


class Rounds:
    def __init__(self, relays):
        self.relays = relays
        todo = [(r.key(o), k, o) for k, r in enumerate(relays) for o in r.offsets() if any(o)]
        self.todo = sorted(todo, key=lambda item: item[:2])

    def begin(self):
        for relay in self.relays:
            relay.begin()

    def upto(self, limit):
        while self.todo and self.todo[0][0] < limit + 0.01:
            _, k, offset = self.todo.pop(0)
            self.relays[k].step(offset)

    def some(self, count):
        for _ in range(min(count, len(self.todo))):
            _, k, offset = self.todo.pop(0)
            self.relays[k].step(offset)

    def finish(self):
        for relay in self.relays:
            relay.finish()


class Spread:
    def __init__(self, line, own_ref, all_ref, columns, order, send_sems, recv_sems, slot):
        self.line, self.order, self.slot = line, order, slot
        self.own_ref, self.all_ref, self.columns = own_ref, all_ref, columns
        self.send_sems, self.recv_sems = send_sems, recv_sems
        me = lax.axis_index("ctx")
        self.me, self.z, self.y, self.x = me, me // 4, me // 2 % 2, me % 2

    def column(self, near, far):
        flips = {self.order[1]: near, self.order[2]: far}
        y = 1 - self.y if flips[1] else self.y
        x = 1 - self.x if flips[2] else self.x
        return self.all_ref.at[:, y, x, :, self.columns]

    def ship(self, source, place, target, send, recv):
        return pltpu.make_async_remote_copy(
            src_ref=source, dst_ref=place,
            send_sem=self.send_sems.at[self.slot, send], recv_sem=self.recv_sems.at[self.slot, recv],
            device_id={"ctx": target}, device_id_type=pl.DeviceIdType.MESH,
        )

    def lift(self, slot, into):
        z = plane_of(self.z, self.line, slot)
        mine = self.all_ref.at[self.z, self.y, self.x, :, self.columns]
        theirs = self.all_ref.at[z, self.y, self.x, :, self.columns]
        target = self.me + (z - self.z) * PLANE
        if into:
            return self.ship(theirs, theirs, target, slot - 1, z)
        return self.ship(self.own_ref.at[:, self.columns], mine, target, slot - 1, self.z)

    def pass_on(self, kind, into):
        near, far = ((1, 0), (0, 1), (1, 1))[kind]
        dim = self.order[1 if kind == 0 else 2]
        target = self.me + 2 - 4 * self.y if dim == 1 else self.me + 1 - 2 * self.x
        held, lands = self.column(near * far, 0), self.column(near, far)
        send, recv = self.line - 1 + kind, self.line + kind
        place = lands if into else held
        return self.ship(place, place, target, send, recv)

    def moves(self, stage, into=False):
        if stage == 0:
            return [self.lift(slot, into) for slot in range(1, self.line)]
        return [self.pass_on(kind, into) for kind in ((), (0, 1), (2,))[stage]]

    def begin(self, stage):
        for out in self.moves(stage):
            out.start()

    def wait_lifted(self):
        for into in self.moves(0, True):
            into.wait_recv()

    def wait_passed(self, kind):
        self.pass_on(kind, True).wait_recv()

    def finish(self):
        for stage in range(3):
            for out in self.moves(stage):
                out.wait_send()


def greet_all(count):
    me, ch = lax.axis_index("ctx"), lax.axis_index("ch")
    barrier = pltpu.get_barrier_semaphore()

    @pl.loop(1, count)
    def _(step):
        pl.semaphore_signal(
            barrier, inc=1, device_id={"ctx": lax.rem(me + step, count)}, device_id_type=pl.DeviceIdType.MESH
        )

    pl.semaphore_signal(barrier, inc=1, device_id={"ch": 1 - ch}, device_id_type=pl.DeviceIdType.MESH)
    return lambda: pl.semaphore_wait(barrier, count)


def halves(v):
    top = v.astype(jnp.bfloat16)
    return top, (v - top.astype(jnp.float32)).astype(jnp.bfloat16)


def dot_halves(a, b):
    dot = functools.partial(jnp.dot, preferred_element_type=jnp.float32)
    return dot(a[0], b[0]) + (dot(a[0], b[1]) + dot(a[1], b[0]))


def fused_kernel(
    count, sub, in_ref, tok_ref, out_ref, taps_ref, skip_hbm, order_hbm, row_hbm, col_hbm, inv_hbm, turn_hbm,
    hidden_ref, rows_ref,
    skip_ref, order_ref, row_ref, col_ref, inv_ref, turn_ref, in_all, tok, part, inbox, gate, prod, sorted_prod, stage, taps_in, taps_sorted, taps_stage, taps_got, got, result, back, back_wide, hid,
    relay_send, relay_recv, out_send, out_recv, pair_send, pair_recv, taps_send, taps_recv, prod_send, prod_recv,
    back_send, back_recv, hid_send, hid_recv, local_sems,
):
    me, ch = lax.axis_index("ctx"), lax.axis_index("ch")
    line = count // PLANE
    z = me // PLANE
    rows, cols = turn_ref.shape[1:]
    own_rows = tok_ref.shape[0] // cols
    owned = got.shape[1] // own_rows
    chans = in_ref.shape[1]
    pack = got.shape[1]
    pairs = stage.shape[0]
    wide = in_ref.shape[2]
    tokens = tok_ref.shape[0]
    ctx_dev = pl.DeviceIdType.MESH

    def cut(*shares):
        edges = [wide * sum(shares[:k]) // sum(shares) for k in range(len(shares) + 1)]
        return [pl.ds(a, b - a) for a, b in zip(edges, edges[1:])]

    first, second, third = cut(6, 7, 3)
    left, right = cut(1, 1)
    weights = Rounds([
        Relay(line, in_ref, in_all, third, (1, 2, 0), relay_send, relay_recv, 2),
        Relay(line, in_ref, in_all, first, (0, 1, 2), relay_send, relay_recv, 0),
        Relay(line, in_ref, in_all, second, (0, 2, 1), relay_send, relay_recv, 1),
    ])
    outs = [
        Spread(line, out_ref, rows_ref, left, (0, 1, 2), out_send, out_recv, 0),
        Spread(line, out_ref, rows_ref, right, (0, 2, 1), out_send, out_recv, 1),
    ]

    def group(ref, g):
        return ref.at[g // 2, pl.ds(pl.multiple_of(lax.rem(g, 2) * pack, pack), pack)]

    load_taps = pltpu.make_async_copy(taps_ref, taps_in, local_sems.at[0])
    load_in = pltpu.make_async_copy(in_ref, in_all.at[me], local_sems.at[1])
    load_tok = pltpu.make_async_copy(tok_ref, tok, local_sems.at[2])
    load_out = pltpu.make_async_copy(out_ref, rows_ref.at[me // PLANE, me // 2 % 2, me % 2], local_sems.at[3])
    keep_taps = pltpu.make_async_copy(group(taps_stage, me), taps_got.at[me], local_sems.at[4])
    keep_prod = pltpu.make_async_copy(group(stage, me), got.at[me], local_sems.at[5])
    keep_back = pltpu.make_async_copy(result.at[me], group(back, me), local_sems.at[6])
    keep_hid = pltpu.make_async_copy(hid, hidden_ref.at[ch], local_sems.at[7])

    tables = [
        pltpu.make_async_copy(src, dst, local_sems.at[8 + k])
        for k, (src, dst) in enumerate([
            (order_hbm, order_ref), (row_hbm, row_ref), (col_hbm, col_ref),
            (inv_hbm, inv_ref), (turn_hbm, turn_ref), (skip_hbm, skip_ref),
        ])
    ]
    all_in = greet_all(count)
    load_taps.start()
    load_in.start()
    load_tok.start()
    load_out.start()
    for copy in tables:
        copy.start()
    all_in()
    weights.begin()

    def send_taps(target):
        return pltpu.make_async_remote_copy(
            src_ref=group(taps_stage, target), dst_ref=taps_got.at[me],
            send_sem=taps_send.at[target], recv_sem=taps_recv.at[me],
            device_id={"ctx": target}, device_id_type=ctx_dev,
        )

    def recv_taps(source):
        return pltpu.make_async_remote_copy(
            src_ref=group(taps_stage, source), dst_ref=taps_got.at[source],
            send_sem=taps_send.at[source], recv_sem=taps_recv.at[source],
            device_id={"ctx": source}, device_id_type=ctx_dev,
        )

    def send_prod(target):
        return pltpu.make_async_remote_copy(
            src_ref=group(stage, target), dst_ref=got.at[me],
            send_sem=prod_send.at[target], recv_sem=prod_recv.at[me],
            device_id={"ctx": target}, device_id_type=ctx_dev,
        )

    def recv_prod(source):
        return pltpu.make_async_remote_copy(
            src_ref=group(stage, source), dst_ref=got.at[source],
            send_sem=prod_send.at[source], recv_sem=prod_recv.at[source],
            device_id={"ctx": source}, device_id_type=ctx_dev,
        )

    def send_back(target):
        return pltpu.make_async_remote_copy(
            src_ref=result.at[target], dst_ref=group(back, me),
            send_sem=back_send.at[target], recv_sem=back_recv.at[me],
            device_id={"ctx": target}, device_id_type=ctx_dev,
        )

    def recv_back(source):
        return pltpu.make_async_remote_copy(
            src_ref=result.at[source], dst_ref=group(back, source),
            send_sem=back_send.at[source], recv_sem=back_recv.at[source],
            device_id={"ctx": source}, device_id_type=ctx_dev,
        )

    def others(act):
        @pl.loop(1, count)
        def _(step):
            act(lax.rem(me + step, count))

    def spread(values, ref, o, begin=0):
        for t in range(values.shape[1] // cols):
            ref[o, pl.ds(begin + t, chans, stride=own_rows), :] = values[:, t * cols : (t + 1) * cols]

    load_taps.wait()
    for o in range(taps_in.shape[0]):
        spread(taps_in[o], taps_sorted, o)
    taps_stage[...] = taps_sorted[...].astype(taps_stage.dtype)
    keep_taps.start()
    others(lambda target: send_taps(target).start())

    parts = 4
    share = tokens // parts

    block = pairs * 3 * chans

    def owner(late):
        low = z < line // 2
        return jnp.where(low, 1, 0) if late else jnp.where(low, 0, 1)

    def pair(late, n):
        lanes = slice(n * share, (n + 1) * share)
        return pltpu.make_async_remote_copy(
            src_ref=part.at[late, :, lanes], dst_ref=inbox.at[:, lanes],
            send_sem=pair_send.at[late, n], recv_sem=pair_recv.at[n],
            device_id={"ch": 1 - ch}, device_id_type=ctx_dev,
        )

    def project(late, *pieces):
        for n in pieces:
            mine = in_all[pl.ds(owner(late) * pairs, pairs)].reshape(block, wide)
            part[late, :, n * share : (n + 1) * share] = lax.dot_general(
                mine, tok[n * share : (n + 1) * share, :], (((1,), (1,)), ((), ())),
                preferred_element_type=jnp.float32,
            )

            @pl.when(owner(late) != ch)
            def _():
                pair(late, n).start()

    def consume(late, *pieces):
        @pl.when(owner(late) == ch)
        def _():
            for n in pieces:
                pair(late, n).wait_recv()
                lanes = slice(n * share, (n + 1) * share)
                for o in range(pairs):
                    near, key, value = [
                        part[late, pl.ds((3 * o + m) * chans, chans), lanes]
                        + inbox[pl.ds((3 * o + m) * chans, chans), lanes]
                        for m in range(3)
                    ]
                    gate[o, :, lanes] = near
                    values = key * value
                    prod[o, :, lanes] = values
                    spread(values, sorted_prod, o, n * share // cols)

    def send_products(late):
        @pl.when(owner(late) == ch)
        def _():
            stage[...] = sorted_prod[...].astype(stage.dtype)
            others(lambda target: send_prod(target).start())
            keep_prod.start()

        @pl.when(owner(late) != ch)
        def _():
            for n in range(parts):
                pair(late, n).wait_send()

    def iota(shape, dim):
        return lax.broadcasted_iota(jnp.int32, shape, dim)

    weights.upto(1)
    for copy in tables:
        copy.wait()
    blocks = order_ref.shape[1]
    hot = jnp.where(iota((blocks, blocks), 0) == order_ref[...], 1.0, 0.0).astype(jnp.bfloat16)
    down = jnp.where(iota((rows, blocks), 0) // sub == iota((rows, blocks), 1), 1.0, 0.0).astype(jnp.bfloat16)
    over = jnp.where(iota((blocks, rows), 1) // sub == iota((blocks, rows), 0), 1.0, 0.0).astype(jnp.bfloat16)
    dot = functools.partial(jnp.dot, preferred_element_type=jnp.float32)
    moved = dot(dot(down, hot).astype(jnp.bfloat16), over)
    same = lax.rem(iota((rows, rows), 0), sub) == lax.rem(iota((rows, rows), 1), sub)
    moved = jnp.where(same, moved, 0.0).astype(jnp.bfloat16)
    perm_wide = [dot(row_ref[k], moved) for k in range(2)]
    perm = [v.astype(jnp.bfloat16) for v in perm_wide]
    perm_t = [v.T.astype(jnp.bfloat16) for v in perm_wide]
    cos, sin = turn_ref[0], turn_ref[1]

    def transform(ref, table):
        values = ref[...].astype(jnp.float32)
        stacked = jnp.concatenate(
            [values[:, c * own_rows : (c + 1) * own_rows, :].reshape(rows, cols) for c in range(owned)], axis=1
        )
        stacked = stacked.astype(jnp.bfloat16)
        turn = dot(table[0], stacked) + dot(table[1], stacked)
        out = []
        for c in range(owned):
            real = turn[:rows, c * cols : (c + 1) * cols]
            imag = turn[rows:, c * cols : (c + 1) * cols]
            out.append(jnp.concatenate([real * cos + imag * sin, imag * cos - real * sin], axis=1))
        return dot_halves(halves(jnp.concatenate(out, axis=0)), (col_ref[0], col_ref[1]))

    weights.upto(2.6)
    load_in.wait()
    load_tok.wait()
    others(lambda source: recv_taps(source).wait_recv())
    keep_taps.wait()
    fil = transform(taps_got, (row_ref[0], row_ref[1]))
    weights.upto(3)
    for out in outs:
        out.begin(0)
    project(0, 0, 1)
    weights.some(9)
    project(0, 2, 3)
    weights.some(3)
    consume(0, 0, 1, 2, 3)
    send_products(0)
    weights.upto(9)
    load_out.wait()
    for out in outs:
        out.wait_lifted()
        out.begin(1)
    project(1, 0, 1)
    consume(1, 0)
    project(1, 2)
    consume(1, 1)
    project(1, 3)
    consume(1, 2, 3)
    send_products(1)
    weights.finish()
    others(lambda target: send_taps(target).wait_send())
    others(lambda source: recv_prod(source).wait_recv())
    keep_prod.wait()
    sig = transform(got, perm)
    sr, si, fr, fi = sig[:, :cols], sig[:, cols:], fil[:, :cols], fil[:, cols:]
    both = jnp.concatenate([sr * fr - si * fi, sr * fi + si * fr], axis=1)
    spun = dot_halves(halves(both), (inv_ref[0], inv_ref[1]))
    turn = []
    for c in range(owned):
        real = spun[c * rows : (c + 1) * rows, :cols]
        imag = spun[c * rows : (c + 1) * rows, cols:]
        turn.append(jnp.concatenate([real * cos - imag * sin, real * sin + imag * cos], axis=0))
    conv = dot_halves(perm_t, halves(jnp.concatenate(turn, axis=1)))
    pieces = [conv[:, c * cols : (c + 1) * cols].reshape(count, own_rows, cols) for c in range(owned)]
    result[...] = jnp.concatenate(pieces, axis=1).astype(result.dtype)
    keep_back.start()
    others(lambda target: send_back(target).start())
    for out in outs:
        out.wait_passed(0)
        out.begin(2)
    others(lambda source: recv_back(source).wait_recv())
    keep_back.wait()
    back_wide[...] = back[...].astype(jnp.float32)
    width = skip_ref.shape[1]
    diagonal = iota((width, width), 0) == iota((width, width), 1)
    skip = jnp.sum(jnp.where(diagonal, skip_ref[...], 0.0), axis=1, keepdims=True)
    for o in range(0, gate.shape[0], 2):
        for t in range(own_rows):
            lanes = slice(t * cols, (t + 1) * cols)
            pieces = []
            for k in (o, o + 1):
                near = back_wide[k, pl.ds(t, chans, stride=own_rows), :]
                pieces.append(gate[k, :, lanes] * (near + skip[k * chans : (k + 1) * chans] * prod[k, :, lanes]))
            hid[o * chans : (o + 2) * chans, lanes] = jnp.concatenate(pieces, axis=0).astype(jnp.bfloat16)
    hand = pltpu.make_async_remote_copy(
        src_ref=hid, dst_ref=hidden_ref.at[ch], send_sem=hid_send.at[0], recv_sem=hid_recv.at[0],
        device_id={"ch": 1 - ch}, device_id_type=ctx_dev,
    )
    hand.start()
    keep_hid.start()
    others(lambda target: send_prod(target).wait_send())
    others(lambda target: send_back(target).wait_send())
    for out in outs:
        out.wait_passed(1)
        out.wait_passed(2)
        out.finish()
    keep_hid.wait()
    hand.wait()


def split_table(table):
    top = table.astype(jnp.bfloat16)
    low = (table - top.astype(np.float32)).astype(jnp.bfloat16)
    return np.stack([top, low])


def fused(tokens, in_weight, conv_filter, skip_gain, group_order, out_weight, count):
    tok_count, feat = tokens.shape
    chans = in_weight.shape[0]
    chan_local = conv_filter.shape[0]
    seq = tok_count * count
    rows, cols = split_length(seq)
    own_rows = tok_count // cols
    owned = chan_local // count
    sub = seq // group_order.shape[0] // cols
    freq = 4 * np.arange(rows) + 1

    def turns(numer, period):
        angle = (numer % period) * (2.0 * math.pi / period)
        return np.cos(angle).astype(np.float32), np.sin(angle).astype(np.float32)

    cos, sin = turns(freq[:, None] * np.arange(rows)[None, :], 4 * rows)
    row_dft = np.concatenate([cos, -sin], axis=0)
    cos, sin = turns(np.arange(cols)[:, None] * np.arange(cols)[None, :], cols)
    col_dft = np.concatenate([np.concatenate([cos, -sin], 1), np.concatenate([sin, cos], 1)], 0)
    col_inv = (col_dft.T / (rows * cols)).astype(np.float32)
    tw_cos, tw_sin = turns(freq[:, None] * np.arange(cols)[None, :], 4 * rows * cols)
    pairs = chan_local // chans
    hbm = pl.BlockSpec(memory_space=pl.ANY)
    f32, bf16 = jnp.float32, jnp.bfloat16
    packed, slim = [pltpu.VMEM((pairs, chans * own_rows, cols), kind) for kind in (f32, bf16)]
    short = pltpu.VMEM((count, owned * own_rows, cols), bf16)
    full = pltpu.VMEM((pairs, chans, tok_count), f32)
    strips = pltpu.VMEM((2, pairs * 3 * chans, tok_count), f32)
    strip = pltpu.VMEM((pairs * 3 * chans, tok_count), f32)
    each = pltpu.SemaphoreType.DMA((count,))
    hidden, rows_all = pl.pallas_call(
        functools.partial(fused_kernel, count, sub),
        out_shape=(
            jax.ShapeDtypeStruct((2, chan_local, tok_count), bf16),
            jax.ShapeDtypeStruct((count // PLANE, 2, 2, *out_weight.shape), bf16),
        ),
        in_specs=[hbm] * 10,
        out_specs=(hbm, hbm),
        scratch_shapes=[
            pltpu.VMEM((1, chan_local), f32),
            pltpu.VMEM((1, group_order.shape[0]), jnp.int32),
            pltpu.VMEM((2, *row_dft.shape), bf16),
            pltpu.VMEM((2, *col_dft.shape), bf16),
            pltpu.VMEM((2, *col_inv.shape), bf16),
            pltpu.VMEM((2, rows, cols), f32),
            pltpu.VMEM((count, 3, chans, feat), bf16),
            pltpu.VMEM((tok_count, feat), bf16),
            strips, strip, full, full, packed, slim, full, packed, slim, short, short, short, slim, packed,
            pltpu.VMEM((chan_local, tok_count), bf16),
            pltpu.SemaphoreType.DMA((3, count, 4)),
            pltpu.SemaphoreType.DMA((3, count)),
            pltpu.SemaphoreType.DMA((2, 6)),
            pltpu.SemaphoreType.DMA((2, 7)),
            pltpu.SemaphoreType.DMA((2, 4)),
            pltpu.SemaphoreType.DMA((4,)),
            each, each, each, each, each, each,
            pltpu.SemaphoreType.DMA((1,)),
            pltpu.SemaphoreType.DMA((1,)),
            pltpu.SemaphoreType.DMA((14,)),
        ],
        compiler_params=pltpu.CompilerParams(collective_id=0, has_side_effects=True, vmem_limit_bytes=VMEM_LIMIT),
        name="fused",
    )(
        in_weight.transpose(1, 0, 2), tokens, out_weight, conv_filter.reshape(pairs, chans, tok_count),
        skip_gain.reshape(1, -1), group_order.reshape(1, -1), split_table(row_dft), split_table(col_dft),
        split_table(col_inv), np.stack([tw_cos, tw_sin]),
    )
    return hidden.reshape(2 * chan_local, tok_count), rows_all.reshape(-1, feat)


def mix_kernel(tile, wide, hidden_hbm, rows_hbm, out_ref, hidden, rows, tiles, sems):
    loads = [
        pltpu.make_async_copy(hidden_hbm, hidden, sems.at[0]),
        pltpu.make_async_copy(rows_hbm, rows, sems.at[1]),
    ]
    for copy in loads:
        copy.start()
    for copy in loads:
        copy.wait()
    stores = []
    for k in range(tiles.shape[0]):
        mine = hidden[:, k * tile : (k + 1) * tile]
        for at in range(0, tiles.shape[2], wide):
            tiles[k, :, at : at + wide] = lax.dot_general(
                mine, rows[:, at : at + wide], (((0,), (0,)), ((), ())), preferred_element_type=jnp.float32
            ).astype(tiles.dtype)
        stores.append(pltpu.make_async_copy(tiles.at[k], out_ref.at[pl.ds(k * tile, tile)], sems.at[2 + k]))
        stores[-1].start()
    for copy in stores:
        copy.wait()


def mix(hidden, rows, tile=64, wide=512):
    count, feat = hidden.shape[1], rows.shape[1]
    hbm = pl.BlockSpec(memory_space=pl.ANY)
    return pl.pallas_call(
        functools.partial(mix_kernel, tile, wide),
        out_shape=jax.ShapeDtypeStruct((count, feat), jnp.bfloat16),
        in_specs=[hbm, hbm],
        out_specs=hbm,
        scratch_shapes=[
            pltpu.VMEM(hidden.shape, hidden.dtype),
            pltpu.VMEM(rows.shape, rows.dtype),
            pltpu.VMEM((count // tile, tile, feat), jnp.bfloat16),
            pltpu.SemaphoreType.DMA((2 + count // tile,)),
        ],
        compiler_params=pltpu.CompilerParams(vmem_limit_bytes=VMEM_LIMIT),
        name="mix",
    )(hidden, rows)


def per_device(tokens, in_weight, conv_filter, skip_gain, group_order, out_weight):
    ctx = lax.axis_size("ctx")
    ch = lax.axis_size("ch")
    tok_count, feat_local = tokens.shape
    chan_local = conv_filter.shape[0]
    seq = tok_count * ctx
    group = seq // group_order.shape[0]
    rows, cols = split_length(seq)
    own_rows = tok_count // cols
    owned = -(-chan_local // ctx)
    padded = owned * ctx

    def parts_of(signal):
        signal = jnp.pad(signal, ((0, padded - chan_local), (0, 0)))
        return signal.reshape(ctx, owned, own_rows, cols)

    def swapped(parts):
        return lax.all_to_all(parts, "ctx", split_axis=0, concat_axis=0, tiled=True)

    relayed = ctx == RELAY_LIMIT and ch == 2 and in_weight.shape[0] == 8 and own_rows == 8 and padded == chan_local
    if relayed:
        hidden_all, rows_all = fused(tokens, in_weight, conv_filter, skip_gain, group_order, out_weight, ctx)
        return mix(hidden_all, rows_all)
    mine = in_weight.reshape(-1, feat_local)
    flat = lax.all_gather(mine, "ctx", axis=0, tiled=True)
    rows_all = lax.all_gather(out_weight, "ctx", axis=0, tiled=True)
    taps = swapped(parts_of(conv_filter))
    partial = lax.dot_general(flat, tokens, (((1,), (1,)), ((), ())), preferred_element_type=jnp.float32)
    if ch == 2:
        me = lax.axis_index("ch")
        half = partial.shape[0] // 2
        away = lax.dynamic_slice_in_dim(partial, (1 - me) * half, half, 0)
        kept = lax.dynamic_slice_in_dim(partial, me * half, half, 0)
        proj = kept + lax.ppermute(away, "ch", [(0, 1), (1, 0)])
    else:
        proj = lax.psum_scatter(partial, "ch", scatter_dimension=0, tiled=True)
    proj = proj.reshape(chan_local, 3, tok_count)
    gate = proj[:, 0]
    product = proj[:, 1] * proj[:, 2]
    in_group = jnp.arange(group // cols, dtype=jnp.int32)
    row_ids = (group_order[:, None] * (group // cols) + in_group[None, :]).reshape(rows)

    def grid(parts):
        return parts.transpose(0, 2, 1, 3).reshape(rows, owned, cols)

    conv = causal_conv(grid(swapped(parts_of(product))), grid(taps), row_ids)
    back = swapped(conv.reshape(ctx, own_rows, owned, cols).transpose(0, 2, 1, 3))
    conv = back.reshape(padded, tok_count)[:chan_local]
    hidden = (gate * (conv + skip_gain[:, None] * product)).astype(jnp.bfloat16)
    hidden_all = lax.all_gather(hidden, "ch", axis=0, tiled=True)
    mixed = lax.dot_general(
        hidden_all, rows_all, (((0,), (0,)), ((), ())), preferred_element_type=jnp.float32
    )
    return mixed.astype(jnp.bfloat16)


def solution(mesh):
    in_specs = (P("ctx", "ch"), P("ctx", None, "ch"), P("ch", "ctx"), P("ch"), P(), P("ctx", "ch"))
    return jax.shard_map(
        per_device, mesh=mesh, in_specs=in_specs, out_specs=P("ctx", "ch"), check_vma=False
    )
```

```python
import functools
import itertools
import math

import jax
import jax.numpy as jnp
import numpy as np
from jax import lax
from jax.experimental import pallas as pl
from jax.experimental.pallas import tpu as pltpu
from jax.sharding import PartitionSpec as P

high = lax.Precision.HIGH
RELAY_LIMIT = 16
VMEM_LIMIT = 63 * 2**20


def split_length(length):
    cols = 1 << ((length.bit_length() - 1) // 2)
    return length // cols, cols


def cos_sin(numer, period):
    angle = (numer % period).astype(jnp.float32) * (2.0 * math.pi / period)
    return jnp.cos(angle), jnp.sin(angle)


def row_table(row_ids, rows):
    freq = 4 * jnp.arange(rows, dtype=jnp.int32) + 1
    cos, sin = cos_sin(freq[:, None] * row_ids[None, :], 4 * rows)
    return jnp.concatenate([cos, -sin], axis=0)


def col_table(cols):
    ids = jnp.arange(cols, dtype=jnp.int32)
    cos, sin = cos_sin(ids[:, None] * ids[None, :], cols)
    top = jnp.concatenate([cos, -sin], axis=1)
    bottom = jnp.concatenate([sin, cos], axis=1)
    return jnp.concatenate([top, bottom], axis=0)


def twist(rows, cols):
    freq = 4 * jnp.arange(rows, dtype=jnp.int32) + 1
    return cos_sin(freq[:, None] * jnp.arange(cols, dtype=jnp.int32)[None, :], 4 * rows * cols)


def spectrum(values, row_dft, col_dft, tw):
    rows, chans, cols = values.shape
    cos, sin = tw[0][:, None, :], tw[1][:, None, :]
    part = jnp.dot(row_dft, values.reshape(rows, chans * cols), precision=high)
    real = part[:rows].reshape(rows, chans, cols)
    imag = part[rows:].reshape(rows, chans, cols)
    turned = jnp.concatenate([real * cos + imag * sin, imag * cos - real * sin], axis=2)
    out = jnp.dot(turned.reshape(rows * chans, 2 * cols), col_dft, precision=high)
    return out.reshape(rows, chans, 2 * cols)


def causal_conv(values, taps, row_ids):
    rows, chans, cols = values.shape
    col_dft = col_table(cols)
    tw = twist(rows, cols)
    perm_dft = row_table(row_ids, rows)
    sig = spectrum(values, perm_dft, col_dft, tw)
    fil = spectrum(taps, row_table(jnp.arange(rows, dtype=jnp.int32), rows), col_dft, tw)
    sr, si = sig[..., :cols], sig[..., cols:]
    fr, fi = fil[..., :cols], fil[..., cols:]
    both = jnp.concatenate([sr * fr - si * fi, sr * fi + si * fr], axis=2)
    back = jnp.dot(both.reshape(rows * chans, 2 * cols), col_dft.T, precision=high)
    back = back.reshape(rows, chans, 2 * cols) * (1.0 / (rows * cols))
    br, bi = back[..., :cols], back[..., cols:]
    cos, sin = tw[0][:, None, :], tw[1][:, None, :]
    turned = jnp.concatenate([br * cos - bi * sin, br * sin + bi * cos], axis=0)
    out = jnp.dot(perm_dft.T, turned.reshape(2 * rows, chans * cols), precision=high)
    return out.reshape(rows, chans, cols)


PLANE = 4
ACROSS, BESIDE = 2, 3


def plane_of(z, line, slot):
    low = z < line // 2
    w = jnp.where(low, z, line - 1 - z)
    near = (w, 1 - w, w * 0 + 2, w * 0 + 3)[slot]
    return jnp.where(low, near, line - 1 - near)


class Relay:
    reach = (0, 1, 1.6, 2.6)

    def __init__(self, line, own_ref, all_ref, columns, order, send_sems, recv_sems, slot):
        self.line, self.order, self.slot = line, order, slot
        self.own_ref, self.all_ref, self.columns = own_ref, all_ref, columns
        self.send_sems, self.recv_sems = send_sems, recv_sems
        me = lax.axis_index("ctx")
        self.me, self.z, self.y, self.x = me, me // 4, me // 2 % 2, me % 2

    def offsets(self):
        return itertools.product(range(self.line), (0, 1), (0, 1))

    def key(self, offset):
        return self.reach[offset[0]] + offset[1] + offset[2]

    def origin(self, offset):
        dz, dy, dx = offset
        y = 1 - self.y if dy else self.y
        x = 1 - self.x if dx else self.x
        return plane_of(self.z, self.line, dz) * PLANE + y * 2 + x

    def at(self, ref, *lead):
        whole = (slice(None),) * (len(self.own_ref.shape) - 1)
        return ref.at[(*lead, *whole, self.columns)]

    def exits(self, offset):
        along = [k for k, dim in enumerate(self.order) if offset[dim] != 0]
        last = along[-1] if along else -1
        out = []
        if last >= 0 and self.order[last] == 0:
            out.append("on")
        for dim in self.order[last + 1 :]:
            out += (["up", "down"], [ACROSS], [BESIDE])[dim]
        return out

    def copy(self, offset, way):
        origin = self.origin(offset)
        up = self.me + PLANE
        down = self.me - PLANE
        own = all(step == 0 for step in offset)
        if way == "on":
            rising = plane_of(self.z, self.line, offset[0]) < self.z
            target, index = jnp.where(rising, up, down), jnp.where(rising, 0, 1)
        elif way in ("up", "down"):
            target, index = (up, 0) if way == "up" else (down, 1)
        else:
            target = self.me + 2 - 4 * self.y if way == ACROSS else self.me + 1 - 2 * self.x
            index = way
        return pltpu.make_async_remote_copy(
            src_ref=self.at(self.own_ref) if own else self.at(self.all_ref, origin),
            dst_ref=self.at(self.all_ref, origin),
            send_sem=self.send_sems.at[self.slot, origin, index],
            recv_sem=self.recv_sems.at[self.slot, origin],
            device_id={"ctx": target},
            device_id_type=pl.DeviceIdType.MESH,
        )

    def each_exit(self, offset, act):
        for way in self.exits(offset):
            copy = self.copy(offset, way)
            if way not in ("on", "up", "down"):
                act(copy)
                continue
            room_up, room_down = self.z + 1 < self.line, self.z > 0
            if way == "on":
                rising = plane_of(self.z, self.line, offset[0]) < self.z
                test = jnp.where(rising, room_up, room_down)
            else:
                test = room_up if way == "up" else room_down

            @pl.when(test)
            def _():
                act(copy)

    def begin(self):
        self.each_exit((0, 0, 0), lambda copy: copy.start())

    def step(self, offset):
        self.copy(offset, BESIDE).wait_recv()
        self.each_exit(offset, lambda copy: copy.start())

    def finish(self):
        for offset in self.offsets():
            self.each_exit(offset, lambda copy: copy.wait_send())


class Rounds:
    def __init__(self, relays):
        self.relays = relays
        todo = [(r.key(o), k, o) for k, r in enumerate(relays) for o in r.offsets() if any(o)]
        self.todo = sorted(todo, key=lambda item: item[:2])

    def begin(self):
        for relay in self.relays:
            relay.begin()

    def upto(self, limit):
        while self.todo and self.todo[0][0] < limit + 0.01:
            _, k, offset = self.todo.pop(0)
            self.relays[k].step(offset)

    def some(self, count):
        for _ in range(min(count, len(self.todo))):
            _, k, offset = self.todo.pop(0)
            self.relays[k].step(offset)

    def finish(self):
        for relay in self.relays:
            relay.finish()


class Spread:
    def __init__(self, line, own_ref, all_ref, columns, order, send_sems, recv_sems, slot):
        self.line, self.order, self.slot = line, order, slot
        self.own_ref, self.all_ref, self.columns = own_ref, all_ref, columns
        self.send_sems, self.recv_sems = send_sems, recv_sems
        me = lax.axis_index("ctx")
        self.me, self.z, self.y, self.x = me, me // 4, me // 2 % 2, me % 2

    def column(self, near, far):
        flips = {self.order[1]: near, self.order[2]: far}
        y = 1 - self.y if flips[1] else self.y
        x = 1 - self.x if flips[2] else self.x
        return self.all_ref.at[:, y, x, :, self.columns]

    def ship(self, source, place, target, send, recv):
        return pltpu.make_async_remote_copy(
            src_ref=source, dst_ref=place,
            send_sem=self.send_sems.at[self.slot, send], recv_sem=self.recv_sems.at[self.slot, recv],
            device_id={"ctx": target}, device_id_type=pl.DeviceIdType.MESH,
        )

    def lift(self, slot, into):
        z = plane_of(self.z, self.line, slot)
        mine = self.all_ref.at[self.z, self.y, self.x, :, self.columns]
        theirs = self.all_ref.at[z, self.y, self.x, :, self.columns]
        target = self.me + (z - self.z) * PLANE
        if into:
            return self.ship(theirs, theirs, target, slot - 1, z)
        return self.ship(self.own_ref.at[:, self.columns], mine, target, slot - 1, self.z)

    def pass_on(self, kind, into):
        near, far = ((1, 0), (0, 1), (1, 1))[kind]
        dim = self.order[1 if kind == 0 else 2]
        target = self.me + 2 - 4 * self.y if dim == 1 else self.me + 1 - 2 * self.x
        held, lands = self.column(near * far, 0), self.column(near, far)
        send, recv = self.line - 1 + kind, self.line + kind
        place = lands if into else held
        return self.ship(place, place, target, send, recv)

    def moves(self, stage, into=False):
        if stage == 0:
            return [self.lift(slot, into) for slot in range(1, self.line)]
        return [self.pass_on(kind, into) for kind in ((), (0, 1), (2,))[stage]]

    def begin(self, stage):
        for out in self.moves(stage):
            out.start()

    def wait_lifted(self):
        for into in self.moves(0, True):
            into.wait_recv()

    def wait_passed(self, kind):
        self.pass_on(kind, True).wait_recv()

    def finish(self):
        for stage in range(3):
            for out in self.moves(stage):
                out.wait_send()


def greet_all(count):
    me, ch = lax.axis_index("ctx"), lax.axis_index("ch")
    barrier = pltpu.get_barrier_semaphore()

    @pl.loop(1, count)
    def _(step):
        pl.semaphore_signal(
            barrier, inc=1, device_id={"ctx": lax.rem(me + step, count)}, device_id_type=pl.DeviceIdType.MESH
        )

    pl.semaphore_signal(barrier, inc=1, device_id={"ch": 1 - ch}, device_id_type=pl.DeviceIdType.MESH)
    return lambda: pl.semaphore_wait(barrier, count)


def halves(v):
    top = v.astype(jnp.bfloat16)
    return top, (v - top.astype(jnp.float32)).astype(jnp.bfloat16)


def dot_halves(a, b):
    dot = functools.partial(jnp.dot, preferred_element_type=jnp.float32)
    return dot(a[0], b[0]) + (dot(a[0], b[1]) + dot(a[1], b[0]))


def fused_kernel(
    count, sub, in_ref, tok_ref, out_ref, taps_ref, skip_hbm, order_hbm, row_hbm, col_hbm, inv_hbm, turn_hbm,
    hidden_ref, rows_ref,
    skip_ref, order_ref, row_ref, col_ref, inv_ref, turn_ref, in_all, tok, part, inbox, gate, prod, sorted_prod, stage, taps_in, taps_sorted, taps_stage, taps_got, got, result, back, back_wide, hid,
    relay_send, relay_recv, out_send, out_recv, pair_send, pair_recv, taps_send, taps_recv, prod_send, prod_recv,
    back_send, back_recv, hid_send, hid_recv, local_sems,
):
    me, ch = lax.axis_index("ctx"), lax.axis_index("ch")
    line = count // PLANE
    z = me // PLANE
    rows, cols = turn_ref.shape[1:]
    own_rows = tok_ref.shape[0] // cols
    owned = got.shape[1] // own_rows
    chans = in_ref.shape[1]
    pack = got.shape[1]
    pairs = stage.shape[0]
    wide = in_ref.shape[2]
    tokens = tok_ref.shape[0]
    ctx_dev = pl.DeviceIdType.MESH

    def cut(*shares):
        edges = [wide * sum(shares[:k]) // sum(shares) for k in range(len(shares) + 1)]
        return [pl.ds(a, b - a) for a, b in zip(edges, edges[1:])]

    first, second, third = cut(6, 7, 3)
    left, right = cut(1, 1)
    weights = Rounds([
        Relay(line, in_ref, in_all, third, (1, 2, 0), relay_send, relay_recv, 2),
        Relay(line, in_ref, in_all, first, (0, 1, 2), relay_send, relay_recv, 0),
        Relay(line, in_ref, in_all, second, (0, 2, 1), relay_send, relay_recv, 1),
    ])
    outs = [
        Spread(line, out_ref, rows_ref, left, (0, 1, 2), out_send, out_recv, 0),
        Spread(line, out_ref, rows_ref, right, (0, 2, 1), out_send, out_recv, 1),
    ]

    def group(ref, g):
        return ref.at[g // 2, pl.ds(pl.multiple_of(lax.rem(g, 2) * pack, pack), pack)]

    load_taps = pltpu.make_async_copy(taps_ref, taps_in, local_sems.at[0])
    load_in = pltpu.make_async_copy(in_ref, in_all.at[me], local_sems.at[1])
    load_tok = pltpu.make_async_copy(tok_ref, tok, local_sems.at[2])
    load_out = pltpu.make_async_copy(out_ref, rows_ref.at[me // PLANE, me // 2 % 2, me % 2], local_sems.at[3])
    keep_taps = pltpu.make_async_copy(group(taps_stage, me), taps_got.at[me], local_sems.at[4])
    keep_prod = pltpu.make_async_copy(group(stage, me), got.at[me], local_sems.at[5])
    keep_back = pltpu.make_async_copy(result.at[me], group(back, me), local_sems.at[6])
    keep_hid = pltpu.make_async_copy(hid, hidden_ref.at[ch], local_sems.at[7])

    tables = [
        pltpu.make_async_copy(src, dst, local_sems.at[8 + k])
        for k, (src, dst) in enumerate([
            (order_hbm, order_ref), (row_hbm, row_ref), (col_hbm, col_ref),
            (inv_hbm, inv_ref), (turn_hbm, turn_ref), (skip_hbm, skip_ref),
        ])
    ]
    all_in = greet_all(count)
    load_taps.start()
    load_in.start()
    load_tok.start()
    load_out.start()
    for copy in tables:
        copy.start()
    all_in()
    weights.begin()

    def send_taps(target):
        return pltpu.make_async_remote_copy(
            src_ref=group(taps_stage, target), dst_ref=taps_got.at[me],
            send_sem=taps_send.at[target], recv_sem=taps_recv.at[me],
            device_id={"ctx": target}, device_id_type=ctx_dev,
        )

    def recv_taps(source):
        return pltpu.make_async_remote_copy(
            src_ref=group(taps_stage, source), dst_ref=taps_got.at[source],
            send_sem=taps_send.at[source], recv_sem=taps_recv.at[source],
            device_id={"ctx": source}, device_id_type=ctx_dev,
        )

    def send_prod(target):
        return pltpu.make_async_remote_copy(
            src_ref=group(stage, target), dst_ref=got.at[me],
            send_sem=prod_send.at[target], recv_sem=prod_recv.at[me],
            device_id={"ctx": target}, device_id_type=ctx_dev,
        )

    def recv_prod(source):
        return pltpu.make_async_remote_copy(
            src_ref=group(stage, source), dst_ref=got.at[source],
            send_sem=prod_send.at[source], recv_sem=prod_recv.at[source],
            device_id={"ctx": source}, device_id_type=ctx_dev,
        )

    def send_back(target):
        return pltpu.make_async_remote_copy(
            src_ref=result.at[target], dst_ref=group(back, me),
            send_sem=back_send.at[target], recv_sem=back_recv.at[me],
            device_id={"ctx": target}, device_id_type=ctx_dev,
        )

    def recv_back(source):
        return pltpu.make_async_remote_copy(
            src_ref=result.at[source], dst_ref=group(back, source),
            send_sem=back_send.at[source], recv_sem=back_recv.at[source],
            device_id={"ctx": source}, device_id_type=ctx_dev,
        )

    def others(act):
        @pl.loop(1, count)
        def _(step):
            act(lax.rem(me + step, count))

    def spread(values, ref, o, begin=0):
        for t in range(values.shape[1] // cols):
            ref[o, pl.ds(begin + t, chans, stride=own_rows), :] = values[:, t * cols : (t + 1) * cols]

    load_taps.wait()
    for o in range(taps_in.shape[0]):
        spread(taps_in[o], taps_sorted, o)
    taps_stage[...] = taps_sorted[...].astype(taps_stage.dtype)
    keep_taps.start()
    others(lambda target: send_taps(target).start())

    parts = 2
    share = tokens // parts

    block = pairs * 3 * chans

    def owner(late):
        low = z < line // 2
        return jnp.where(low, 1, 0) if late else jnp.where(low, 0, 1)

    def pair(late, n):
        lanes = slice(n * share, (n + 1) * share)
        return pltpu.make_async_remote_copy(
            src_ref=part.at[late, :, lanes], dst_ref=inbox.at[:, lanes],
            send_sem=pair_send.at[late, n], recv_sem=pair_recv.at[n],
            device_id={"ch": 1 - ch}, device_id_type=ctx_dev,
        )

    def project(late, *pieces):
        for n in pieces:
            mine = in_all[pl.ds(owner(late) * pairs, pairs)].reshape(block, wide)
            part[late, :, n * share : (n + 1) * share] = lax.dot_general(
                mine, tok[n * share : (n + 1) * share, :], (((1,), (1,)), ((), ())),
                preferred_element_type=jnp.float32,
            )

            @pl.when(owner(late) != ch)
            def _():
                pair(late, n).start()

    def consume(late, *pieces):
        @pl.when(owner(late) == ch)
        def _():
            for n in pieces:
                pair(late, n).wait_recv()
                lanes = slice(n * share, (n + 1) * share)
                for o in range(pairs):
                    near, key, value = [
                        part[late, pl.ds((3 * o + m) * chans, chans), lanes]
                        + inbox[pl.ds((3 * o + m) * chans, chans), lanes]
                        for m in range(3)
                    ]
                    gate[o, :, lanes] = near
                    values = key * value
                    prod[o, :, lanes] = values
                    spread(values, sorted_prod, o, n * share // cols)

    def send_products(late):
        @pl.when(owner(late) == ch)
        def _():
            stage[...] = sorted_prod[...].astype(stage.dtype)
            others(lambda target: send_prod(target).start())
            keep_prod.start()

        @pl.when(owner(late) != ch)
        def _():
            for n in range(parts):
                pair(late, n).wait_send()

    def iota(shape, dim):
        return lax.broadcasted_iota(jnp.int32, shape, dim)

    weights.upto(1)
    for copy in tables:
        copy.wait()
    blocks = order_ref.shape[1]
    hot = jnp.where(iota((blocks, blocks), 0) == order_ref[...], 1.0, 0.0).astype(jnp.bfloat16)
    down = jnp.where(iota((rows, blocks), 0) // sub == iota((rows, blocks), 1), 1.0, 0.0).astype(jnp.bfloat16)
    over = jnp.where(iota((blocks, rows), 1) // sub == iota((blocks, rows), 0), 1.0, 0.0).astype(jnp.bfloat16)
    dot = functools.partial(jnp.dot, preferred_element_type=jnp.float32)
    moved = dot(dot(down, hot).astype(jnp.bfloat16), over)
    same = lax.rem(iota((rows, rows), 0), sub) == lax.rem(iota((rows, rows), 1), sub)
    moved = jnp.where(same, moved, 0.0).astype(jnp.bfloat16)
    perm_wide = [dot(row_ref[k], moved) for k in range(2)]
    perm = [v.astype(jnp.bfloat16) for v in perm_wide]
    perm_t = [v.T.astype(jnp.bfloat16) for v in perm_wide]
    cos, sin = turn_ref[0], turn_ref[1]

    def transform(ref, table):
        values = ref[...].astype(jnp.float32)
        stacked = jnp.concatenate(
            [values[:, c * own_rows : (c + 1) * own_rows, :].reshape(rows, cols) for c in range(owned)], axis=1
        )
        stacked = stacked.astype(jnp.bfloat16)
        turn = dot(table[0], stacked) + dot(table[1], stacked)
        out = []
        for c in range(owned):
            real = turn[:rows, c * cols : (c + 1) * cols]
            imag = turn[rows:, c * cols : (c + 1) * cols]
            out.append(jnp.concatenate([real * cos + imag * sin, imag * cos - real * sin], axis=1))
        return dot_halves(halves(jnp.concatenate(out, axis=0)), (col_ref[0], col_ref[1]))

    weights.upto(2.6)
    load_in.wait()
    load_tok.wait()
    others(lambda source: recv_taps(source).wait_recv())
    keep_taps.wait()
    fil = transform(taps_got, (row_ref[0], row_ref[1]))
    weights.upto(3)
    for out in outs:
        out.begin(0)
    project(0, 0)
    weights.some(9)
    project(0, 1)
    weights.some(3)
    consume(0, 0, 1)
    send_products(0)
    weights.upto(9)
    load_out.wait()
    for out in outs:
        out.wait_lifted()
        out.begin(1)
    project(1, 0, 1)
    consume(1, 0, 1)
    send_products(1)
    weights.finish()
    others(lambda target: send_taps(target).wait_send())
    others(lambda source: recv_prod(source).wait_recv())
    keep_prod.wait()
    sig = transform(got, perm)
    sr, si, fr, fi = sig[:, :cols], sig[:, cols:], fil[:, :cols], fil[:, cols:]
    both = jnp.concatenate([sr * fr - si * fi, sr * fi + si * fr], axis=1)
    spun = dot_halves(halves(both), (inv_ref[0], inv_ref[1]))
    turn = []
    for c in range(owned):
        real = spun[c * rows : (c + 1) * rows, :cols]
        imag = spun[c * rows : (c + 1) * rows, cols:]
        turn.append(jnp.concatenate([real * cos - imag * sin, real * sin + imag * cos], axis=0))
    conv = dot_halves(perm_t, halves(jnp.concatenate(turn, axis=1)))
    pieces = [conv[:, c * cols : (c + 1) * cols].reshape(count, own_rows, cols) for c in range(owned)]
    result[...] = jnp.concatenate(pieces, axis=1).astype(result.dtype)
    keep_back.start()
    others(lambda target: send_back(target).start())
    for out in outs:
        out.wait_passed(0)
        out.begin(2)
    others(lambda source: recv_back(source).wait_recv())
    keep_back.wait()
    back_wide[...] = back[...].astype(jnp.float32)
    width = skip_ref.shape[1]
    diagonal = iota((width, width), 0) == iota((width, width), 1)
    skip = jnp.sum(jnp.where(diagonal, skip_ref[...], 0.0), axis=1, keepdims=True)
    for o in range(0, gate.shape[0], 2):
        for t in range(own_rows):
            lanes = slice(t * cols, (t + 1) * cols)
            pieces = []
            for k in (o, o + 1):
                near = back_wide[k, pl.ds(t, chans, stride=own_rows), :]
                pieces.append(gate[k, :, lanes] * (near + skip[k * chans : (k + 1) * chans] * prod[k, :, lanes]))
            hid[o * chans : (o + 2) * chans, lanes] = jnp.concatenate(pieces, axis=0).astype(jnp.bfloat16)
    hand = pltpu.make_async_remote_copy(
        src_ref=hid, dst_ref=hidden_ref.at[ch], send_sem=hid_send.at[0], recv_sem=hid_recv.at[0],
        device_id={"ch": 1 - ch}, device_id_type=ctx_dev,
    )
    hand.start()
    keep_hid.start()
    others(lambda target: send_prod(target).wait_send())
    others(lambda target: send_back(target).wait_send())
    for out in outs:
        out.wait_passed(1)
        out.wait_passed(2)
        out.finish()
    keep_hid.wait()
    hand.wait()


def split_table(table):
    top = table.astype(jnp.bfloat16)
    low = (table - top.astype(np.float32)).astype(jnp.bfloat16)
    return np.stack([top, low])


def fused(tokens, in_weight, conv_filter, skip_gain, group_order, out_weight, count):
    tok_count, feat = tokens.shape
    chans = in_weight.shape[0]
    chan_local = conv_filter.shape[0]
    seq = tok_count * count
    rows, cols = split_length(seq)
    own_rows = tok_count // cols
    owned = chan_local // count
    sub = seq // group_order.shape[0] // cols
    freq = 4 * np.arange(rows) + 1

    def turns(numer, period):
        angle = (numer % period) * (2.0 * math.pi / period)
        return np.cos(angle).astype(np.float32), np.sin(angle).astype(np.float32)

    cos, sin = turns(freq[:, None] * np.arange(rows)[None, :], 4 * rows)
    row_dft = np.concatenate([cos, -sin], axis=0)
    cos, sin = turns(np.arange(cols)[:, None] * np.arange(cols)[None, :], cols)
    col_dft = np.concatenate([np.concatenate([cos, -sin], 1), np.concatenate([sin, cos], 1)], 0)
    col_inv = (col_dft.T / (rows * cols)).astype(np.float32)
    tw_cos, tw_sin = turns(freq[:, None] * np.arange(cols)[None, :], 4 * rows * cols)
    pairs = chan_local // chans
    hbm = pl.BlockSpec(memory_space=pl.ANY)
    f32, bf16 = jnp.float32, jnp.bfloat16
    packed, slim = [pltpu.VMEM((pairs, chans * own_rows, cols), kind) for kind in (f32, bf16)]
    short = pltpu.VMEM((count, owned * own_rows, cols), bf16)
    full = pltpu.VMEM((pairs, chans, tok_count), f32)
    strips = pltpu.VMEM((2, pairs * 3 * chans, tok_count), f32)
    strip = pltpu.VMEM((pairs * 3 * chans, tok_count), f32)
    each = pltpu.SemaphoreType.DMA((count,))
    hidden, rows_all = pl.pallas_call(
        functools.partial(fused_kernel, count, sub),
        out_shape=(
            jax.ShapeDtypeStruct((2, chan_local, tok_count), bf16),
            jax.ShapeDtypeStruct((count // PLANE, 2, 2, *out_weight.shape), bf16),
        ),
        in_specs=[hbm] * 10,
        out_specs=(hbm, hbm),
        scratch_shapes=[
            pltpu.VMEM((1, chan_local), f32),
            pltpu.VMEM((1, group_order.shape[0]), jnp.int32),
            pltpu.VMEM((2, *row_dft.shape), bf16),
            pltpu.VMEM((2, *col_dft.shape), bf16),
            pltpu.VMEM((2, *col_inv.shape), bf16),
            pltpu.VMEM((2, rows, cols), f32),
            pltpu.VMEM((count, 3, chans, feat), bf16),
            pltpu.VMEM((tok_count, feat), bf16),
            strips, strip, full, full, packed, slim, full, packed, slim, short, short, short, slim, packed,
            pltpu.VMEM((chan_local, tok_count), bf16),
            pltpu.SemaphoreType.DMA((3, count, 4)),
            pltpu.SemaphoreType.DMA((3, count)),
            pltpu.SemaphoreType.DMA((2, 6)),
            pltpu.SemaphoreType.DMA((2, 7)),
            pltpu.SemaphoreType.DMA((2, 4)),
            pltpu.SemaphoreType.DMA((4,)),
            each, each, each, each, each, each,
            pltpu.SemaphoreType.DMA((1,)),
            pltpu.SemaphoreType.DMA((1,)),
            pltpu.SemaphoreType.DMA((14,)),
        ],
        compiler_params=pltpu.CompilerParams(collective_id=0, has_side_effects=True, vmem_limit_bytes=VMEM_LIMIT),
        name="fused",
    )(
        in_weight.transpose(1, 0, 2), tokens, out_weight, conv_filter.reshape(pairs, chans, tok_count),
        skip_gain.reshape(1, -1), group_order.reshape(1, -1), split_table(row_dft), split_table(col_dft),
        split_table(col_inv), np.stack([tw_cos, tw_sin]),
    )
    return hidden.reshape(2 * chan_local, tok_count), rows_all.reshape(-1, feat)


def mix_kernel(tile, wide, hidden_hbm, rows_hbm, out_ref, hidden, rows, tiles, sems):
    loads = [
        pltpu.make_async_copy(hidden_hbm, hidden, sems.at[0]),
        pltpu.make_async_copy(rows_hbm, rows, sems.at[1]),
    ]
    for copy in loads:
        copy.start()
    for copy in loads:
        copy.wait()
    stores = []
    for k in range(tiles.shape[0]):
        mine = hidden[:, k * tile : (k + 1) * tile]
        for at in range(0, tiles.shape[2], wide):
            tiles[k, :, at : at + wide] = lax.dot_general(
                mine, rows[:, at : at + wide], (((0,), (0,)), ((), ())), preferred_element_type=jnp.float32
            ).astype(tiles.dtype)
        stores.append(pltpu.make_async_copy(tiles.at[k], out_ref.at[pl.ds(k * tile, tile)], sems.at[2 + k]))
        stores[-1].start()
    for copy in stores:
        copy.wait()


def mix(hidden, rows, tile=64, wide=512):
    count, feat = hidden.shape[1], rows.shape[1]
    hbm = pl.BlockSpec(memory_space=pl.ANY)
    return pl.pallas_call(
        functools.partial(mix_kernel, tile, wide),
        out_shape=jax.ShapeDtypeStruct((count, feat), jnp.bfloat16),
        in_specs=[hbm, hbm],
        out_specs=hbm,
        scratch_shapes=[
            pltpu.VMEM(hidden.shape, hidden.dtype),
            pltpu.VMEM(rows.shape, rows.dtype),
            pltpu.VMEM((count // tile, tile, feat), jnp.bfloat16),
            pltpu.SemaphoreType.DMA((2 + count // tile,)),
        ],
        compiler_params=pltpu.CompilerParams(vmem_limit_bytes=VMEM_LIMIT),
        name="mix",
    )(hidden, rows)


def per_device(tokens, in_weight, conv_filter, skip_gain, group_order, out_weight):
    ctx = lax.axis_size("ctx")
    ch = lax.axis_size("ch")
    tok_count, feat_local = tokens.shape
    chan_local = conv_filter.shape[0]
    seq = tok_count * ctx
    group = seq // group_order.shape[0]
    rows, cols = split_length(seq)
    own_rows = tok_count // cols
    owned = -(-chan_local // ctx)
    padded = owned * ctx

    def parts_of(signal):
        signal = jnp.pad(signal, ((0, padded - chan_local), (0, 0)))
        return signal.reshape(ctx, owned, own_rows, cols)

    def swapped(parts):
        return lax.all_to_all(parts, "ctx", split_axis=0, concat_axis=0, tiled=True)

    relayed = ctx == RELAY_LIMIT and ch == 2 and in_weight.shape[0] == 8 and own_rows == 8 and padded == chan_local
    if relayed:
        hidden_all, rows_all = fused(tokens, in_weight, conv_filter, skip_gain, group_order, out_weight, ctx)
        return mix(hidden_all, rows_all)
    mine = in_weight.reshape(-1, feat_local)
    flat = lax.all_gather(mine, "ctx", axis=0, tiled=True)
    rows_all = lax.all_gather(out_weight, "ctx", axis=0, tiled=True)
    taps = swapped(parts_of(conv_filter))
    partial = lax.dot_general(flat, tokens, (((1,), (1,)), ((), ())), preferred_element_type=jnp.float32)
    if ch == 2:
        me = lax.axis_index("ch")
        half = partial.shape[0] // 2
        away = lax.dynamic_slice_in_dim(partial, (1 - me) * half, half, 0)
        kept = lax.dynamic_slice_in_dim(partial, me * half, half, 0)
        proj = kept + lax.ppermute(away, "ch", [(0, 1), (1, 0)])
    else:
        proj = lax.psum_scatter(partial, "ch", scatter_dimension=0, tiled=True)
    proj = proj.reshape(chan_local, 3, tok_count)
    gate = proj[:, 0]
    product = proj[:, 1] * proj[:, 2]
    in_group = jnp.arange(group // cols, dtype=jnp.int32)
    row_ids = (group_order[:, None] * (group // cols) + in_group[None, :]).reshape(rows)

    def grid(parts):
        return parts.transpose(0, 2, 1, 3).reshape(rows, owned, cols)

    conv = causal_conv(grid(swapped(parts_of(product))), grid(taps), row_ids)
    back = swapped(conv.reshape(ctx, own_rows, owned, cols).transpose(0, 2, 1, 3))
    conv = back.reshape(padded, tok_count)[:chan_local]
    hidden = (gate * (conv + skip_gain[:, None] * product)).astype(jnp.bfloat16)
    hidden_all = lax.all_gather(hidden, "ch", axis=0, tiled=True)
    mixed = lax.dot_general(
        hidden_all, rows_all, (((0,), (0,)), ((), ())), preferred_element_type=jnp.float32
    )
    return mixed.astype(jnp.bfloat16)


def solution(mesh):
    in_specs = (P("ctx", "ch"), P("ctx", None, "ch"), P("ch", "ctx"), P("ch"), P(), P("ctx", "ch"))
    return jax.shard_map(
        per_device, mesh=mesh, in_specs=in_specs, out_specs=P("ctx", "ch"), check_vma=False
    )
```

```python
import functools
import itertools
import math

import jax
import jax.numpy as jnp
import numpy as np
from jax import lax
from jax.experimental import pallas as pl
from jax.experimental.pallas import tpu as pltpu
from jax.sharding import PartitionSpec as P

high = lax.Precision.HIGH
RELAY_LIMIT = 16
VMEM_LIMIT = 63 * 2**20


def split_length(length):
    cols = 1 << ((length.bit_length() - 1) // 2)
    return length // cols, cols


def cos_sin(numer, period):
    angle = (numer % period).astype(jnp.float32) * (2.0 * math.pi / period)
    return jnp.cos(angle), jnp.sin(angle)


def row_table(row_ids, rows):
    freq = 4 * jnp.arange(rows, dtype=jnp.int32) + 1
    cos, sin = cos_sin(freq[:, None] * row_ids[None, :], 4 * rows)
    return jnp.concatenate([cos, -sin], axis=0)


def col_table(cols):
    ids = jnp.arange(cols, dtype=jnp.int32)
    cos, sin = cos_sin(ids[:, None] * ids[None, :], cols)
    top = jnp.concatenate([cos, -sin], axis=1)
    bottom = jnp.concatenate([sin, cos], axis=1)
    return jnp.concatenate([top, bottom], axis=0)


def twist(rows, cols):
    freq = 4 * jnp.arange(rows, dtype=jnp.int32) + 1
    return cos_sin(freq[:, None] * jnp.arange(cols, dtype=jnp.int32)[None, :], 4 * rows * cols)


def spectrum(values, row_dft, col_dft, tw):
    rows, chans, cols = values.shape
    cos, sin = tw[0][:, None, :], tw[1][:, None, :]
    part = jnp.dot(row_dft, values.reshape(rows, chans * cols), precision=high)
    real = part[:rows].reshape(rows, chans, cols)
    imag = part[rows:].reshape(rows, chans, cols)
    turned = jnp.concatenate([real * cos + imag * sin, imag * cos - real * sin], axis=2)
    out = jnp.dot(turned.reshape(rows * chans, 2 * cols), col_dft, precision=high)
    return out.reshape(rows, chans, 2 * cols)


def causal_conv(values, taps, row_ids):
    rows, chans, cols = values.shape
    col_dft = col_table(cols)
    tw = twist(rows, cols)
    perm_dft = row_table(row_ids, rows)
    sig = spectrum(values, perm_dft, col_dft, tw)
    fil = spectrum(taps, row_table(jnp.arange(rows, dtype=jnp.int32), rows), col_dft, tw)
    sr, si = sig[..., :cols], sig[..., cols:]
    fr, fi = fil[..., :cols], fil[..., cols:]
    both = jnp.concatenate([sr * fr - si * fi, sr * fi + si * fr], axis=2)
    back = jnp.dot(both.reshape(rows * chans, 2 * cols), col_dft.T, precision=high)
    back = back.reshape(rows, chans, 2 * cols) * (1.0 / (rows * cols))
    br, bi = back[..., :cols], back[..., cols:]
    cos, sin = tw[0][:, None, :], tw[1][:, None, :]
    turned = jnp.concatenate([br * cos - bi * sin, br * sin + bi * cos], axis=0)
    out = jnp.dot(perm_dft.T, turned.reshape(2 * rows, chans * cols), precision=high)
    return out.reshape(rows, chans, cols)


PLANE = 4
ACROSS, BESIDE = 2, 3


def plane_of(z, line, slot):
    low = z < line // 2
    w = jnp.where(low, z, line - 1 - z)
    near = (w, 1 - w, w * 0 + 2, w * 0 + 3)[slot]
    return jnp.where(low, near, line - 1 - near)


class Relay:
    reach = (0, 1, 1.6, 2.6)

    def __init__(self, line, own_ref, all_ref, columns, order, send_sems, recv_sems, slot):
        self.line, self.order, self.slot = line, order, slot
        self.own_ref, self.all_ref, self.columns = own_ref, all_ref, columns
        self.send_sems, self.recv_sems = send_sems, recv_sems
        me = lax.axis_index("ctx")
        self.me, self.z, self.y, self.x = me, me // 4, me // 2 % 2, me % 2

    def offsets(self):
        return itertools.product(range(self.line), (0, 1), (0, 1))

    def key(self, offset):
        return self.reach[offset[0]] + offset[1] + offset[2]

    def origin(self, offset):
        dz, dy, dx = offset
        y = 1 - self.y if dy else self.y
        x = 1 - self.x if dx else self.x
        return plane_of(self.z, self.line, dz) * PLANE + y * 2 + x

    def at(self, ref, *lead):
        whole = (slice(None),) * (len(self.own_ref.shape) - 1)
        return ref.at[(*lead, *whole, self.columns)]

    def exits(self, offset):
        along = [k for k, dim in enumerate(self.order) if offset[dim] != 0]
        last = along[-1] if along else -1
        out = []
        if last >= 0 and self.order[last] == 0:
            out.append("on")
        for dim in self.order[last + 1 :]:
            out += (["up", "down"], [ACROSS], [BESIDE])[dim]
        return out

    def copy(self, offset, way):
        origin = self.origin(offset)
        up = self.me + PLANE
        down = self.me - PLANE
        own = all(step == 0 for step in offset)
        if way == "on":
            rising = plane_of(self.z, self.line, offset[0]) < self.z
            target, index = jnp.where(rising, up, down), jnp.where(rising, 0, 1)
        elif way in ("up", "down"):
            target, index = (up, 0) if way == "up" else (down, 1)
        else:
            target = self.me + 2 - 4 * self.y if way == ACROSS else self.me + 1 - 2 * self.x
            index = way
        return pltpu.make_async_remote_copy(
            src_ref=self.at(self.own_ref) if own else self.at(self.all_ref, origin),
            dst_ref=self.at(self.all_ref, origin),
            send_sem=self.send_sems.at[self.slot, origin, index],
            recv_sem=self.recv_sems.at[self.slot, origin],
            device_id={"ctx": target},
            device_id_type=pl.DeviceIdType.MESH,
        )

    def each_exit(self, offset, act):
        for way in self.exits(offset):
            copy = self.copy(offset, way)
            if way not in ("on", "up", "down"):
                act(copy)
                continue
            room_up, room_down = self.z + 1 < self.line, self.z > 0
            if way == "on":
                rising = plane_of(self.z, self.line, offset[0]) < self.z
                test = jnp.where(rising, room_up, room_down)
            else:
                test = room_up if way == "up" else room_down

            @pl.when(test)
            def _():
                act(copy)

    def begin(self):
        self.each_exit((0, 0, 0), lambda copy: copy.start())

    def step(self, offset):
        self.copy(offset, BESIDE).wait_recv()
        self.each_exit(offset, lambda copy: copy.start())

    def finish(self):
        for offset in self.offsets():
            self.each_exit(offset, lambda copy: copy.wait_send())


class Rounds:
    def __init__(self, relays):
        self.relays = relays
        todo = [(r.key(o), k, o) for k, r in enumerate(relays) for o in r.offsets() if any(o)]
        self.todo = sorted(todo, key=lambda item: item[:2])

    def begin(self):
        for relay in self.relays:
            relay.begin()

    def upto(self, limit):
        while self.todo and self.todo[0][0] < limit + 0.01:
            _, k, offset = self.todo.pop(0)
            self.relays[k].step(offset)

    def some(self, count):
        for _ in range(min(count, len(self.todo))):
            _, k, offset = self.todo.pop(0)
            self.relays[k].step(offset)

    def finish(self):
        for relay in self.relays:
            relay.finish()


class Spread:
    def __init__(self, line, own_ref, all_ref, columns, order, send_sems, recv_sems, slot):
        self.line, self.order, self.slot = line, order, slot
        self.own_ref, self.all_ref, self.columns = own_ref, all_ref, columns
        self.send_sems, self.recv_sems = send_sems, recv_sems
        me = lax.axis_index("ctx")
        self.me, self.z, self.y, self.x = me, me // 4, me // 2 % 2, me % 2

    def column(self, near, far):
        flips = {self.order[1]: near, self.order[2]: far}
        y = 1 - self.y if flips[1] else self.y
        x = 1 - self.x if flips[2] else self.x
        return self.all_ref.at[:, y, x, :, self.columns]

    def ship(self, source, place, target, send, recv):
        return pltpu.make_async_remote_copy(
            src_ref=source, dst_ref=place,
            send_sem=self.send_sems.at[self.slot, send], recv_sem=self.recv_sems.at[self.slot, recv],
            device_id={"ctx": target}, device_id_type=pl.DeviceIdType.MESH,
        )

    def lift(self, slot, into):
        z = plane_of(self.z, self.line, slot)
        mine = self.all_ref.at[self.z, self.y, self.x, :, self.columns]
        theirs = self.all_ref.at[z, self.y, self.x, :, self.columns]
        target = self.me + (z - self.z) * PLANE
        if into:
            return self.ship(theirs, theirs, target, slot - 1, z)
        return self.ship(self.own_ref.at[:, self.columns], mine, target, slot - 1, self.z)

    def pass_on(self, kind, into):
        near, far = ((1, 0), (0, 1), (1, 1))[kind]
        dim = self.order[1 if kind == 0 else 2]
        target = self.me + 2 - 4 * self.y if dim == 1 else self.me + 1 - 2 * self.x
        held, lands = self.column(near * far, 0), self.column(near, far)
        send, recv = self.line - 1 + kind, self.line + kind
        place = lands if into else held
        return self.ship(place, place, target, send, recv)

    def moves(self, stage, into=False):
        if stage == 0:
            return [self.lift(slot, into) for slot in range(1, self.line)]
        return [self.pass_on(kind, into) for kind in ((), (0, 1), (2,))[stage]]

    def begin(self, stage):
        for out in self.moves(stage):
            out.start()

    def wait_lifted(self):
        for into in self.moves(0, True):
            into.wait_recv()

    def wait_passed(self, kind):
        self.pass_on(kind, True).wait_recv()

    def finish(self):
        for stage in range(3):
            for out in self.moves(stage):
                out.wait_send()


def greet_all(count):
    me, ch = lax.axis_index("ctx"), lax.axis_index("ch")
    barrier = pltpu.get_barrier_semaphore()

    @pl.loop(1, count)
    def _(step):
        pl.semaphore_signal(
            barrier, inc=1, device_id={"ctx": lax.rem(me + step, count)}, device_id_type=pl.DeviceIdType.MESH
        )

    pl.semaphore_signal(barrier, inc=1, device_id={"ch": 1 - ch}, device_id_type=pl.DeviceIdType.MESH)
    return lambda: pl.semaphore_wait(barrier, count)


def halves(v):
    top = v.astype(jnp.bfloat16)
    return top, (v - top.astype(jnp.float32)).astype(jnp.bfloat16)


def dot_halves(a, b):
    dot = functools.partial(jnp.dot, preferred_element_type=jnp.float32)
    return dot(a[0], b[0]) + (dot(a[0], b[1]) + dot(a[1], b[0]))


def fused_kernel(
    count, sub, in_ref, tok_ref, out_ref, taps_ref, skip_hbm, order_hbm, row_hbm, col_hbm, inv_hbm, turn_hbm,
    hidden_ref, rows_ref,
    skip_ref, order_ref, row_ref, col_ref, inv_ref, turn_ref, in_all, tok, part, inbox, gate, prod, sorted_prod, stage, taps_in, taps_sorted, taps_stage, taps_got, got, result, back, back_wide, hid,
    relay_send, relay_recv, out_send, out_recv, pair_send, pair_recv, taps_send, taps_recv, prod_send, prod_recv,
    back_send, back_recv, hid_send, hid_recv, local_sems,
):
    me, ch = lax.axis_index("ctx"), lax.axis_index("ch")
    line = count // PLANE
    z = me // PLANE
    rows, cols = turn_ref.shape[1:]
    own_rows = tok_ref.shape[0] // cols
    owned = got.shape[1] // own_rows
    chans = in_ref.shape[1]
    pack = got.shape[1]
    pairs = stage.shape[0]
    wide = in_ref.shape[2]
    tokens = tok_ref.shape[0]
    ctx_dev = pl.DeviceIdType.MESH

    def cut(*shares):
        edges = [wide * sum(shares[:k]) // sum(shares) for k in range(len(shares) + 1)]
        return [pl.ds(a, b - a) for a, b in zip(edges, edges[1:])]

    first, second, third = cut(6, 7, 3)
    left, right = cut(1, 1)
    weights = Rounds([
        Relay(line, in_ref, in_all, third, (1, 2, 0), relay_send, relay_recv, 2),
        Relay(line, in_ref, in_all, first, (0, 1, 2), relay_send, relay_recv, 0),
        Relay(line, in_ref, in_all, second, (0, 2, 1), relay_send, relay_recv, 1),
    ])
    outs = [
        Spread(line, out_ref, rows_ref, left, (0, 1, 2), out_send, out_recv, 0),
        Spread(line, out_ref, rows_ref, right, (0, 2, 1), out_send, out_recv, 1),
    ]

    def group(ref, g):
        return ref.at[g // 2, pl.ds(pl.multiple_of(lax.rem(g, 2) * pack, pack), pack)]

    load_taps = pltpu.make_async_copy(taps_ref, taps_in, local_sems.at[0])
    load_in = pltpu.make_async_copy(in_ref, in_all.at[me], local_sems.at[1])
    load_tok = pltpu.make_async_copy(tok_ref, tok, local_sems.at[2])
    load_out = pltpu.make_async_copy(out_ref, rows_ref.at[me // PLANE, me // 2 % 2, me % 2], local_sems.at[3])
    keep_taps = pltpu.make_async_copy(group(taps_stage, me), taps_got.at[me], local_sems.at[4])
    keep_prod = pltpu.make_async_copy(group(stage, me), got.at[me], local_sems.at[5])
    keep_back = pltpu.make_async_copy(result.at[me], group(back, me), local_sems.at[6])
    keep_hid = pltpu.make_async_copy(hid, hidden_ref.at[ch], local_sems.at[7])

    tables = [
        pltpu.make_async_copy(src, dst, local_sems.at[8 + k])
        for k, (src, dst) in enumerate([
            (order_hbm, order_ref), (row_hbm, row_ref), (col_hbm, col_ref),
            (inv_hbm, inv_ref), (turn_hbm, turn_ref), (skip_hbm, skip_ref),
        ])
    ]
    all_in = greet_all(count)
    load_taps.start()
    load_in.start()
    load_tok.start()
    load_out.start()
    for copy in tables:
        copy.start()
    all_in()
    weights.begin()

    def send_taps(target):
        return pltpu.make_async_remote_copy(
            src_ref=group(taps_stage, target), dst_ref=taps_got.at[me],
            send_sem=taps_send.at[target], recv_sem=taps_recv.at[me],
            device_id={"ctx": target}, device_id_type=ctx_dev,
        )

    def recv_taps(source):
        return pltpu.make_async_remote_copy(
            src_ref=group(taps_stage, source), dst_ref=taps_got.at[source],
            send_sem=taps_send.at[source], recv_sem=taps_recv.at[source],
            device_id={"ctx": source}, device_id_type=ctx_dev,
        )

    def send_prod(target):
        return pltpu.make_async_remote_copy(
            src_ref=group(stage, target), dst_ref=got.at[me],
            send_sem=prod_send.at[target], recv_sem=prod_recv.at[me],
            device_id={"ctx": target}, device_id_type=ctx_dev,
        )

    def recv_prod(source):
        return pltpu.make_async_remote_copy(
            src_ref=group(stage, source), dst_ref=got.at[source],
            send_sem=prod_send.at[source], recv_sem=prod_recv.at[source],
            device_id={"ctx": source}, device_id_type=ctx_dev,
        )

    def send_back(target):
        return pltpu.make_async_remote_copy(
            src_ref=result.at[target], dst_ref=group(back, me),
            send_sem=back_send.at[target], recv_sem=back_recv.at[me],
            device_id={"ctx": target}, device_id_type=ctx_dev,
        )

    def recv_back(source):
        return pltpu.make_async_remote_copy(
            src_ref=result.at[source], dst_ref=group(back, source),
            send_sem=back_send.at[source], recv_sem=back_recv.at[source],
            device_id={"ctx": source}, device_id_type=ctx_dev,
        )

    def others(act):
        @pl.loop(1, count)
        def _(step):
            act(lax.rem(me + step, count))

    def spread(values, ref, o, begin=0):
        for t in range(values.shape[1] // cols):
            ref[o, pl.ds(begin + t, chans, stride=own_rows), :] = values[:, t * cols : (t + 1) * cols]

    load_taps.wait()
    for o in range(taps_in.shape[0]):
        spread(taps_in[o], taps_sorted, o)
    taps_stage[...] = taps_sorted[...].astype(taps_stage.dtype)
    keep_taps.start()
    others(lambda target: send_taps(target).start())

    parts = 2
    share = tokens // parts

    block = pairs * 3 * chans

    def owner(late):
        low = z < line // 2
        return jnp.where(low, 1, 0) if late else jnp.where(low, 0, 1)

    def pair(late, n):
        lanes = slice(n * share, (n + 1) * share)
        return pltpu.make_async_remote_copy(
            src_ref=part.at[late, :, lanes], dst_ref=inbox.at[:, lanes],
            send_sem=pair_send.at[late, n], recv_sem=pair_recv.at[n],
            device_id={"ch": 1 - ch}, device_id_type=ctx_dev,
        )

    def project(late, *pieces):
        for n in pieces:
            mine = in_all[pl.ds(owner(late) * pairs, pairs)].reshape(block, wide)
            part[late, :, n * share : (n + 1) * share] = lax.dot_general(
                mine, tok[n * share : (n + 1) * share, :], (((1,), (1,)), ((), ())),
                preferred_element_type=jnp.float32,
            )

            @pl.when(owner(late) != ch)
            def _():
                pair(late, n).start()

    def consume(late, *pieces):
        @pl.when(owner(late) == ch)
        def _():
            for n in pieces:
                pair(late, n).wait_recv()
                lanes = slice(n * share, (n + 1) * share)
                for o in range(pairs):
                    near, key, value = [
                        part[late, pl.ds((3 * o + m) * chans, chans), lanes]
                        + inbox[pl.ds((3 * o + m) * chans, chans), lanes]
                        for m in range(3)
                    ]
                    gate[o, :, lanes] = near
                    values = key * value
                    prod[o, :, lanes] = values
                    spread(values, sorted_prod, o, n * share // cols)

    def send_products(late):
        @pl.when(owner(late) == ch)
        def _():
            stage[...] = sorted_prod[...].astype(stage.dtype)
            others(lambda target: send_prod(target).start())
            keep_prod.start()

        @pl.when(owner(late) != ch)
        def _():
            for n in range(parts):
                pair(late, n).wait_send()

    def iota(shape, dim):
        return lax.broadcasted_iota(jnp.int32, shape, dim)

    weights.upto(1)
    for copy in tables:
        copy.wait()
    blocks = order_ref.shape[1]
    hot = jnp.where(iota((blocks, blocks), 0) == order_ref[...], 1.0, 0.0).astype(jnp.bfloat16)
    down = jnp.where(iota((rows, blocks), 0) // sub == iota((rows, blocks), 1), 1.0, 0.0).astype(jnp.bfloat16)
    over = jnp.where(iota((blocks, rows), 1) // sub == iota((blocks, rows), 0), 1.0, 0.0).astype(jnp.bfloat16)
    dot = functools.partial(jnp.dot, preferred_element_type=jnp.float32)
    moved = dot(dot(down, hot).astype(jnp.bfloat16), over)
    same = lax.rem(iota((rows, rows), 0), sub) == lax.rem(iota((rows, rows), 1), sub)
    moved = jnp.where(same, moved, 0.0).astype(jnp.bfloat16)
    perm_wide = [dot(row_ref[k], moved) for k in range(2)]
    perm = [v.astype(jnp.bfloat16) for v in perm_wide]
    perm_t = [v.T.astype(jnp.bfloat16) for v in perm_wide]
    cos, sin = turn_ref[0], turn_ref[1]

    def transform(ref, table):
        values = ref[...].astype(jnp.float32)
        stacked = jnp.concatenate(
            [values[:, c * own_rows : (c + 1) * own_rows, :].reshape(rows, cols) for c in range(owned)], axis=1
        )
        stacked = stacked.astype(jnp.bfloat16)
        turn = dot(table[0], stacked) + dot(table[1], stacked)
        out = []
        for c in range(owned):
            real = turn[:rows, c * cols : (c + 1) * cols]
            imag = turn[rows:, c * cols : (c + 1) * cols]
            out.append(jnp.concatenate([real * cos + imag * sin, imag * cos - real * sin], axis=1))
        return dot_halves(halves(jnp.concatenate(out, axis=0)), (col_ref[0], col_ref[1]))

    weights.upto(2.6)
    load_in.wait()
    load_tok.wait()
    others(lambda source: recv_taps(source).wait_recv())
    keep_taps.wait()
    fil = transform(taps_got, (row_ref[0], row_ref[1]))
    weights.upto(3)
    for out in outs:
        out.begin(0)
    project(0, 0)
    weights.some(9)
    project(0, 1)
    consume(0, 0, 1)
    send_products(0)
    weights.some(3)
    weights.upto(9)
    load_out.wait()
    for out in outs:
        out.wait_lifted()
        out.begin(1)
    project(1, 0, 1)
    consume(1, 0, 1)
    send_products(1)
    weights.finish()
    others(lambda target: send_taps(target).wait_send())
    others(lambda source: recv_prod(source).wait_recv())
    keep_prod.wait()
    sig = transform(got, perm)
    sr, si, fr, fi = sig[:, :cols], sig[:, cols:], fil[:, :cols], fil[:, cols:]
    both = jnp.concatenate([sr * fr - si * fi, sr * fi + si * fr], axis=1)
    spun = dot_halves(halves(both), (inv_ref[0], inv_ref[1]))
    turn = []
    for c in range(owned):
        real = spun[c * rows : (c + 1) * rows, :cols]
        imag = spun[c * rows : (c + 1) * rows, cols:]
        turn.append(jnp.concatenate([real * cos - imag * sin, real * sin + imag * cos], axis=0))
    conv = dot_halves(perm_t, halves(jnp.concatenate(turn, axis=1)))
    pieces = [conv[:, c * cols : (c + 1) * cols].reshape(count, own_rows, cols) for c in range(owned)]
    result[...] = jnp.concatenate(pieces, axis=1).astype(result.dtype)
    keep_back.start()
    others(lambda target: send_back(target).start())
    for out in outs:
        out.wait_passed(0)
        out.begin(2)
    others(lambda source: recv_back(source).wait_recv())
    keep_back.wait()
    back_wide[...] = back[...].astype(jnp.float32)
    width = skip_ref.shape[1]
    diagonal = iota((width, width), 0) == iota((width, width), 1)
    skip = jnp.sum(jnp.where(diagonal, skip_ref[...], 0.0), axis=1, keepdims=True)
    for o in range(0, gate.shape[0], 2):
        for t in range(own_rows):
            lanes = slice(t * cols, (t + 1) * cols)
            pieces = []
            for k in (o, o + 1):
                near = back_wide[k, pl.ds(t, chans, stride=own_rows), :]
                pieces.append(gate[k, :, lanes] * (near + skip[k * chans : (k + 1) * chans] * prod[k, :, lanes]))
            hid[o * chans : (o + 2) * chans, lanes] = jnp.concatenate(pieces, axis=0).astype(jnp.bfloat16)
    hand = pltpu.make_async_remote_copy(
        src_ref=hid, dst_ref=hidden_ref.at[ch], send_sem=hid_send.at[0], recv_sem=hid_recv.at[0],
        device_id={"ch": 1 - ch}, device_id_type=ctx_dev,
    )
    hand.start()
    keep_hid.start()
    others(lambda target: send_prod(target).wait_send())
    others(lambda target: send_back(target).wait_send())
    for out in outs:
        out.wait_passed(1)
        out.wait_passed(2)
        out.finish()
    keep_hid.wait()
    hand.wait()


def split_table(table):
    top = table.astype(jnp.bfloat16)
    low = (table - top.astype(np.float32)).astype(jnp.bfloat16)
    return np.stack([top, low])


def fused(tokens, in_weight, conv_filter, skip_gain, group_order, out_weight, count):
    tok_count, feat = tokens.shape
    chans = in_weight.shape[0]
    chan_local = conv_filter.shape[0]
    seq = tok_count * count
    rows, cols = split_length(seq)
    own_rows = tok_count // cols
    owned = chan_local // count
    sub = seq // group_order.shape[0] // cols
    freq = 4 * np.arange(rows) + 1

    def turns(numer, period):
        angle = (numer % period) * (2.0 * math.pi / period)
        return np.cos(angle).astype(np.float32), np.sin(angle).astype(np.float32)

    cos, sin = turns(freq[:, None] * np.arange(rows)[None, :], 4 * rows)
    row_dft = np.concatenate([cos, -sin], axis=0)
    cos, sin = turns(np.arange(cols)[:, None] * np.arange(cols)[None, :], cols)
    col_dft = np.concatenate([np.concatenate([cos, -sin], 1), np.concatenate([sin, cos], 1)], 0)
    col_inv = (col_dft.T / (rows * cols)).astype(np.float32)
    tw_cos, tw_sin = turns(freq[:, None] * np.arange(cols)[None, :], 4 * rows * cols)
    pairs = chan_local // chans
    hbm = pl.BlockSpec(memory_space=pl.ANY)
    f32, bf16 = jnp.float32, jnp.bfloat16
    packed, slim = [pltpu.VMEM((pairs, chans * own_rows, cols), kind) for kind in (f32, bf16)]
    short = pltpu.VMEM((count, owned * own_rows, cols), bf16)
    full = pltpu.VMEM((pairs, chans, tok_count), f32)
    strips = pltpu.VMEM((2, pairs * 3 * chans, tok_count), f32)
    strip = pltpu.VMEM((pairs * 3 * chans, tok_count), f32)
    each = pltpu.SemaphoreType.DMA((count,))
    hidden, rows_all = pl.pallas_call(
        functools.partial(fused_kernel, count, sub),
        out_shape=(
            jax.ShapeDtypeStruct((2, chan_local, tok_count), bf16),
            jax.ShapeDtypeStruct((count // PLANE, 2, 2, *out_weight.shape), bf16),
        ),
        in_specs=[hbm] * 10,
        out_specs=(hbm, hbm),
        scratch_shapes=[
            pltpu.VMEM((1, chan_local), f32),
            pltpu.VMEM((1, group_order.shape[0]), jnp.int32),
            pltpu.VMEM((2, *row_dft.shape), bf16),
            pltpu.VMEM((2, *col_dft.shape), bf16),
            pltpu.VMEM((2, *col_inv.shape), bf16),
            pltpu.VMEM((2, rows, cols), f32),
            pltpu.VMEM((count, 3, chans, feat), bf16),
            pltpu.VMEM((tok_count, feat), bf16),
            strips, strip, full, full, packed, slim, full, packed, slim, short, short, short, slim, packed,
            pltpu.VMEM((chan_local, tok_count), bf16),
            pltpu.SemaphoreType.DMA((3, count, 4)),
            pltpu.SemaphoreType.DMA((3, count)),
            pltpu.SemaphoreType.DMA((2, 6)),
            pltpu.SemaphoreType.DMA((2, 7)),
            pltpu.SemaphoreType.DMA((2, 4)),
            pltpu.SemaphoreType.DMA((4,)),
            each, each, each, each, each, each,
            pltpu.SemaphoreType.DMA((1,)),
            pltpu.SemaphoreType.DMA((1,)),
            pltpu.SemaphoreType.DMA((14,)),
        ],
        compiler_params=pltpu.CompilerParams(collective_id=0, has_side_effects=True, vmem_limit_bytes=VMEM_LIMIT),
        name="fused",
    )(
        in_weight.transpose(1, 0, 2), tokens, out_weight, conv_filter.reshape(pairs, chans, tok_count),
        skip_gain.reshape(1, -1), group_order.reshape(1, -1), split_table(row_dft), split_table(col_dft),
        split_table(col_inv), np.stack([tw_cos, tw_sin]),
    )
    return hidden.reshape(2 * chan_local, tok_count), rows_all.reshape(-1, feat)


def mix_kernel(tile, wide, hidden_hbm, rows_hbm, out_ref, hidden, rows, tiles, sems):
    loads = [
        pltpu.make_async_copy(hidden_hbm, hidden, sems.at[0]),
        pltpu.make_async_copy(rows_hbm, rows, sems.at[1]),
    ]
    for copy in loads:
        copy.start()
    for copy in loads:
        copy.wait()
    stores = []
    for k in range(tiles.shape[0]):
        mine = hidden[:, k * tile : (k + 1) * tile]
        for at in range(0, tiles.shape[2], wide):
            tiles[k, :, at : at + wide] = lax.dot_general(
                mine, rows[:, at : at + wide], (((0,), (0,)), ((), ())), preferred_element_type=jnp.float32
            ).astype(tiles.dtype)
        stores.append(pltpu.make_async_copy(tiles.at[k], out_ref.at[pl.ds(k * tile, tile)], sems.at[2 + k]))
        stores[-1].start()
    for copy in stores:
        copy.wait()


def mix(hidden, rows, tile=64, wide=512):
    count, feat = hidden.shape[1], rows.shape[1]
    hbm = pl.BlockSpec(memory_space=pl.ANY)
    return pl.pallas_call(
        functools.partial(mix_kernel, tile, wide),
        out_shape=jax.ShapeDtypeStruct((count, feat), jnp.bfloat16),
        in_specs=[hbm, hbm],
        out_specs=hbm,
        scratch_shapes=[
            pltpu.VMEM(hidden.shape, hidden.dtype),
            pltpu.VMEM(rows.shape, rows.dtype),
            pltpu.VMEM((count // tile, tile, feat), jnp.bfloat16),
            pltpu.SemaphoreType.DMA((2 + count // tile,)),
        ],
        compiler_params=pltpu.CompilerParams(vmem_limit_bytes=VMEM_LIMIT),
        name="mix",
    )(hidden, rows)


def per_device(tokens, in_weight, conv_filter, skip_gain, group_order, out_weight):
    ctx = lax.axis_size("ctx")
    ch = lax.axis_size("ch")
    tok_count, feat_local = tokens.shape
    chan_local = conv_filter.shape[0]
    seq = tok_count * ctx
    group = seq // group_order.shape[0]
    rows, cols = split_length(seq)
    own_rows = tok_count // cols
    owned = -(-chan_local // ctx)
    padded = owned * ctx

    def parts_of(signal):
        signal = jnp.pad(signal, ((0, padded - chan_local), (0, 0)))
        return signal.reshape(ctx, owned, own_rows, cols)

    def swapped(parts):
        return lax.all_to_all(parts, "ctx", split_axis=0, concat_axis=0, tiled=True)

    relayed = ctx == RELAY_LIMIT and ch == 2 and in_weight.shape[0] == 8 and own_rows == 8 and padded == chan_local
    if relayed:
        hidden_all, rows_all = fused(tokens, in_weight, conv_filter, skip_gain, group_order, out_weight, ctx)
        return mix(hidden_all, rows_all)
    mine = in_weight.reshape(-1, feat_local)
    flat = lax.all_gather(mine, "ctx", axis=0, tiled=True)
    rows_all = lax.all_gather(out_weight, "ctx", axis=0, tiled=True)
    taps = swapped(parts_of(conv_filter))
    partial = lax.dot_general(flat, tokens, (((1,), (1,)), ((), ())), preferred_element_type=jnp.float32)
    if ch == 2:
        me = lax.axis_index("ch")
        half = partial.shape[0] // 2
        away = lax.dynamic_slice_in_dim(partial, (1 - me) * half, half, 0)
        kept = lax.dynamic_slice_in_dim(partial, me * half, half, 0)
        proj = kept + lax.ppermute(away, "ch", [(0, 1), (1, 0)])
    else:
        proj = lax.psum_scatter(partial, "ch", scatter_dimension=0, tiled=True)
    proj = proj.reshape(chan_local, 3, tok_count)
    gate = proj[:, 0]
    product = proj[:, 1] * proj[:, 2]
    in_group = jnp.arange(group // cols, dtype=jnp.int32)
    row_ids = (group_order[:, None] * (group // cols) + in_group[None, :]).reshape(rows)

    def grid(parts):
        return parts.transpose(0, 2, 1, 3).reshape(rows, owned, cols)

    conv = causal_conv(grid(swapped(parts_of(product))), grid(taps), row_ids)
    back = swapped(conv.reshape(ctx, own_rows, owned, cols).transpose(0, 2, 1, 3))
    conv = back.reshape(padded, tok_count)[:chan_local]
    hidden = (gate * (conv + skip_gain[:, None] * product)).astype(jnp.bfloat16)
    hidden_all = lax.all_gather(hidden, "ch", axis=0, tiled=True)
    mixed = lax.dot_general(
        hidden_all, rows_all, (((0,), (0,)), ((), ())), preferred_element_type=jnp.float32
    )
    return mixed.astype(jnp.bfloat16)


def solution(mesh):
    in_specs = (P("ctx", "ch"), P("ctx", None, "ch"), P("ch", "ctx"), P("ch"), P(), P("ctx", "ch"))
    return jax.shard_map(
        per_device, mesh=mesh, in_specs=in_specs, out_specs=P("ctx", "ch"), check_vma=False
    )
```

```python
import functools
import itertools
import math

import jax
import jax.numpy as jnp
import numpy as np
from jax import lax
from jax.experimental import pallas as pl
from jax.experimental.pallas import tpu as pltpu
from jax.sharding import PartitionSpec as P

high = lax.Precision.HIGH
RELAY_LIMIT = 16
VMEM_LIMIT = 63 * 2**20


def split_length(length):
    cols = 1 << ((length.bit_length() - 1) // 2)
    return length // cols, cols


def cos_sin(numer, period):
    angle = (numer % period).astype(jnp.float32) * (2.0 * math.pi / period)
    return jnp.cos(angle), jnp.sin(angle)


def row_table(row_ids, rows):
    freq = 4 * jnp.arange(rows, dtype=jnp.int32) + 1
    cos, sin = cos_sin(freq[:, None] * row_ids[None, :], 4 * rows)
    return jnp.concatenate([cos, -sin], axis=0)


def col_table(cols):
    ids = jnp.arange(cols, dtype=jnp.int32)
    cos, sin = cos_sin(ids[:, None] * ids[None, :], cols)
    top = jnp.concatenate([cos, -sin], axis=1)
    bottom = jnp.concatenate([sin, cos], axis=1)
    return jnp.concatenate([top, bottom], axis=0)


def twist(rows, cols):
    freq = 4 * jnp.arange(rows, dtype=jnp.int32) + 1
    return cos_sin(freq[:, None] * jnp.arange(cols, dtype=jnp.int32)[None, :], 4 * rows * cols)


def spectrum(values, row_dft, col_dft, tw):
    rows, chans, cols = values.shape
    cos, sin = tw[0][:, None, :], tw[1][:, None, :]
    part = jnp.dot(row_dft, values.reshape(rows, chans * cols), precision=high)
    real = part[:rows].reshape(rows, chans, cols)
    imag = part[rows:].reshape(rows, chans, cols)
    turned = jnp.concatenate([real * cos + imag * sin, imag * cos - real * sin], axis=2)
    out = jnp.dot(turned.reshape(rows * chans, 2 * cols), col_dft, precision=high)
    return out.reshape(rows, chans, 2 * cols)


def causal_conv(values, taps, row_ids):
    rows, chans, cols = values.shape
    col_dft = col_table(cols)
    tw = twist(rows, cols)
    perm_dft = row_table(row_ids, rows)
    sig = spectrum(values, perm_dft, col_dft, tw)
    fil = spectrum(taps, row_table(jnp.arange(rows, dtype=jnp.int32), rows), col_dft, tw)
    sr, si = sig[..., :cols], sig[..., cols:]
    fr, fi = fil[..., :cols], fil[..., cols:]
    both = jnp.concatenate([sr * fr - si * fi, sr * fi + si * fr], axis=2)
    back = jnp.dot(both.reshape(rows * chans, 2 * cols), col_dft.T, precision=high)
    back = back.reshape(rows, chans, 2 * cols) * (1.0 / (rows * cols))
    br, bi = back[..., :cols], back[..., cols:]
    cos, sin = tw[0][:, None, :], tw[1][:, None, :]
    turned = jnp.concatenate([br * cos - bi * sin, br * sin + bi * cos], axis=0)
    out = jnp.dot(perm_dft.T, turned.reshape(2 * rows, chans * cols), precision=high)
    return out.reshape(rows, chans, cols)


PLANE = 4
ACROSS, BESIDE = 2, 3


def plane_of(z, line, slot):
    low = z < line // 2
    w = jnp.where(low, z, line - 1 - z)
    near = (w, 1 - w, w * 0 + 2, w * 0 + 3)[slot]
    return jnp.where(low, near, line - 1 - near)


class Relay:
    reach = (0, 1, 1.6, 2.6)

    def __init__(self, line, own_ref, all_ref, columns, order, send_sems, recv_sems, slot):
        self.line, self.order, self.slot = line, order, slot
        self.own_ref, self.all_ref, self.columns = own_ref, all_ref, columns
        self.send_sems, self.recv_sems = send_sems, recv_sems
        me = lax.axis_index("ctx")
        self.me, self.z, self.y, self.x = me, me // 4, me // 2 % 2, me % 2

    def offsets(self):
        return itertools.product(range(self.line), (0, 1), (0, 1))

    def key(self, offset):
        return self.reach[offset[0]] + offset[1] + offset[2]

    def origin(self, offset):
        dz, dy, dx = offset
        y = 1 - self.y if dy else self.y
        x = 1 - self.x if dx else self.x
        return plane_of(self.z, self.line, dz) * PLANE + y * 2 + x

    def at(self, ref, *lead):
        whole = (slice(None),) * (len(self.own_ref.shape) - 1)
        return ref.at[(*lead, *whole, self.columns)]

    def exits(self, offset):
        along = [k for k, dim in enumerate(self.order) if offset[dim] != 0]
        last = along[-1] if along else -1
        out = []
        if last >= 0 and self.order[last] == 0:
            out.append("on")
        for dim in self.order[last + 1 :]:
            out += (["up", "down"], [ACROSS], [BESIDE])[dim]
        return out

    def copy(self, offset, way):
        origin = self.origin(offset)
        up = self.me + PLANE
        down = self.me - PLANE
        own = all(step == 0 for step in offset)
        if way == "on":
            rising = plane_of(self.z, self.line, offset[0]) < self.z
            target, index = jnp.where(rising, up, down), jnp.where(rising, 0, 1)
        elif way in ("up", "down"):
            target, index = (up, 0) if way == "up" else (down, 1)
        else:
            target = self.me + 2 - 4 * self.y if way == ACROSS else self.me + 1 - 2 * self.x
            index = way
        return pltpu.make_async_remote_copy(
            src_ref=self.at(self.own_ref) if own else self.at(self.all_ref, origin),
            dst_ref=self.at(self.all_ref, origin),
            send_sem=self.send_sems.at[self.slot, origin, index],
            recv_sem=self.recv_sems.at[self.slot, origin],
            device_id={"ctx": target},
            device_id_type=pl.DeviceIdType.MESH,
        )

    def each_exit(self, offset, act):
        for way in self.exits(offset):
            copy = self.copy(offset, way)
            if way not in ("on", "up", "down"):
                act(copy)
                continue
            room_up, room_down = self.z + 1 < self.line, self.z > 0
            if way == "on":
                rising = plane_of(self.z, self.line, offset[0]) < self.z
                test = jnp.where(rising, room_up, room_down)
            else:
                test = room_up if way == "up" else room_down

            @pl.when(test)
            def _():
                act(copy)

    def begin(self):
        self.each_exit((0, 0, 0), lambda copy: copy.start())

    def step(self, offset):
        self.copy(offset, BESIDE).wait_recv()
        self.each_exit(offset, lambda copy: copy.start())

    def finish(self):
        for offset in self.offsets():
            self.each_exit(offset, lambda copy: copy.wait_send())


class Rounds:
    def __init__(self, relays):
        self.relays = relays
        todo = [(r.key(o), k, o) for k, r in enumerate(relays) for o in r.offsets() if any(o)]
        self.todo = sorted(todo, key=lambda item: item[:2])

    def begin(self):
        for relay in self.relays:
            relay.begin()

    def upto(self, limit):
        while self.todo and self.todo[0][0] < limit + 0.01:
            _, k, offset = self.todo.pop(0)
            self.relays[k].step(offset)

    def some(self, count):
        for _ in range(min(count, len(self.todo))):
            _, k, offset = self.todo.pop(0)
            self.relays[k].step(offset)

    def finish(self):
        for relay in self.relays:
            relay.finish()


class Spread:
    def __init__(self, line, own_ref, all_ref, columns, order, send_sems, recv_sems, slot):
        self.line, self.order, self.slot = line, order, slot
        self.own_ref, self.all_ref, self.columns = own_ref, all_ref, columns
        self.send_sems, self.recv_sems = send_sems, recv_sems
        me = lax.axis_index("ctx")
        self.me, self.z, self.y, self.x = me, me // 4, me // 2 % 2, me % 2

    def column(self, near, far):
        flips = {self.order[1]: near, self.order[2]: far}
        y = 1 - self.y if flips[1] else self.y
        x = 1 - self.x if flips[2] else self.x
        return self.all_ref.at[:, y, x, :, self.columns]

    def ship(self, source, place, target, send, recv):
        return pltpu.make_async_remote_copy(
            src_ref=source, dst_ref=place,
            send_sem=self.send_sems.at[self.slot, send], recv_sem=self.recv_sems.at[self.slot, recv],
            device_id={"ctx": target}, device_id_type=pl.DeviceIdType.MESH,
        )

    def lift(self, slot, into):
        z = plane_of(self.z, self.line, slot)
        mine = self.all_ref.at[self.z, self.y, self.x, :, self.columns]
        theirs = self.all_ref.at[z, self.y, self.x, :, self.columns]
        target = self.me + (z - self.z) * PLANE
        if into:
            return self.ship(theirs, theirs, target, slot - 1, z)
        return self.ship(self.own_ref.at[:, self.columns], mine, target, slot - 1, self.z)

    def pass_on(self, kind, into):
        near, far = ((1, 0), (0, 1), (1, 1))[kind]
        dim = self.order[1 if kind == 0 else 2]
        target = self.me + 2 - 4 * self.y if dim == 1 else self.me + 1 - 2 * self.x
        held, lands = self.column(near * far, 0), self.column(near, far)
        send, recv = self.line - 1 + kind, self.line + kind
        place = lands if into else held
        return self.ship(place, place, target, send, recv)

    def moves(self, stage, into=False):
        if stage == 0:
            return [self.lift(slot, into) for slot in range(1, self.line)]
        return [self.pass_on(kind, into) for kind in ((), (0, 1), (2,))[stage]]

    def begin(self, stage):
        for out in self.moves(stage):
            out.start()

    def wait_lifted(self):
        for into in self.moves(0, True):
            into.wait_recv()

    def wait_passed(self, kind):
        self.pass_on(kind, True).wait_recv()

    def finish(self):
        for stage in range(3):
            for out in self.moves(stage):
                out.wait_send()


def greet_all(count):
    me, ch = lax.axis_index("ctx"), lax.axis_index("ch")
    barrier = pltpu.get_barrier_semaphore()

    @pl.loop(1, count)
    def _(step):
        pl.semaphore_signal(
            barrier, inc=1, device_id={"ctx": lax.rem(me + step, count)}, device_id_type=pl.DeviceIdType.MESH
        )

    pl.semaphore_signal(barrier, inc=1, device_id={"ch": 1 - ch}, device_id_type=pl.DeviceIdType.MESH)
    return lambda: pl.semaphore_wait(barrier, count)


def halves(v):
    top = v.astype(jnp.bfloat16)
    return top, (v - top.astype(jnp.float32)).astype(jnp.bfloat16)


def dot_halves(a, b):
    dot = functools.partial(jnp.dot, preferred_element_type=jnp.float32)
    return dot(a[0], b[0]) + (dot(a[0], b[1]) + dot(a[1], b[0]))


def fused_kernel(
    count, sub, in_ref, tok_ref, out_ref, taps_ref, skip_hbm, order_hbm, row_hbm, col_hbm, inv_hbm, turn_hbm,
    hidden_ref, rows_ref,
    skip_ref, order_ref, row_ref, col_ref, inv_ref, turn_ref, in_all, tok, part, inbox, gate, prod, sorted_prod, stage, taps_in, taps_sorted, taps_stage, taps_got, got, result, back, back_wide, hid,
    relay_send, relay_recv, out_send, out_recv, pair_send, pair_recv, taps_send, taps_recv, prod_send, prod_recv,
    back_send, back_recv, hid_send, hid_recv, local_sems,
):
    me, ch = lax.axis_index("ctx"), lax.axis_index("ch")
    line = count // PLANE
    z = me // PLANE
    rows, cols = turn_ref.shape[1:]
    own_rows = tok_ref.shape[0] // cols
    owned = got.shape[1] // own_rows
    chans = in_ref.shape[1]
    pack = got.shape[1]
    pairs = stage.shape[0]
    wide = in_ref.shape[2]
    tokens = tok_ref.shape[0]
    ctx_dev = pl.DeviceIdType.MESH

    def cut(*shares):
        edges = [wide * sum(shares[:k]) // sum(shares) for k in range(len(shares) + 1)]
        return [pl.ds(a, b - a) for a, b in zip(edges, edges[1:])]

    first, second, third = cut(6, 7, 3)
    left, right = cut(1, 1)
    weights = Rounds([
        Relay(line, in_ref, in_all, third, (1, 2, 0), relay_send, relay_recv, 2),
        Relay(line, in_ref, in_all, first, (0, 1, 2), relay_send, relay_recv, 0),
        Relay(line, in_ref, in_all, second, (0, 2, 1), relay_send, relay_recv, 1),
    ])
    outs = [
        Spread(line, out_ref, rows_ref, left, (0, 1, 2), out_send, out_recv, 0),
        Spread(line, out_ref, rows_ref, right, (0, 2, 1), out_send, out_recv, 1),
    ]

    def group(ref, g):
        return ref.at[g // 2, pl.ds(pl.multiple_of(lax.rem(g, 2) * pack, pack), pack)]

    load_taps = pltpu.make_async_copy(taps_ref, taps_in, local_sems.at[0])
    load_in = pltpu.make_async_copy(in_ref, in_all.at[me], local_sems.at[1])
    load_tok = pltpu.make_async_copy(tok_ref, tok, local_sems.at[2])
    load_out = pltpu.make_async_copy(out_ref, rows_ref.at[me // PLANE, me // 2 % 2, me % 2], local_sems.at[3])
    keep_taps = pltpu.make_async_copy(group(taps_stage, me), taps_got.at[me], local_sems.at[4])
    keep_prod = pltpu.make_async_copy(group(stage, me), got.at[me], local_sems.at[5])
    keep_back = pltpu.make_async_copy(result.at[me], group(back, me), local_sems.at[6])
    keep_hid = pltpu.make_async_copy(hid, hidden_ref.at[ch], local_sems.at[7])

    tables = [
        pltpu.make_async_copy(src, dst, local_sems.at[8 + k])
        for k, (src, dst) in enumerate([
            (order_hbm, order_ref), (row_hbm, row_ref), (col_hbm, col_ref),
            (inv_hbm, inv_ref), (turn_hbm, turn_ref), (skip_hbm, skip_ref),
        ])
    ]
    all_in = greet_all(count)
    load_taps.start()
    load_in.start()
    load_tok.start()
    load_out.start()
    for copy in tables:
        copy.start()
    all_in()
    weights.begin()

    def send_taps(target):
        return pltpu.make_async_remote_copy(
            src_ref=group(taps_stage, target), dst_ref=taps_got.at[me],
            send_sem=taps_send.at[target], recv_sem=taps_recv.at[me],
            device_id={"ctx": target}, device_id_type=ctx_dev,
        )

    def recv_taps(source):
        return pltpu.make_async_remote_copy(
            src_ref=group(taps_stage, source), dst_ref=taps_got.at[source],
            send_sem=taps_send.at[source], recv_sem=taps_recv.at[source],
            device_id={"ctx": source}, device_id_type=ctx_dev,
        )

    def send_prod(target):
        return pltpu.make_async_remote_copy(
            src_ref=group(stage, target), dst_ref=got.at[me],
            send_sem=prod_send.at[target], recv_sem=prod_recv.at[me],
            device_id={"ctx": target}, device_id_type=ctx_dev,
        )

    def recv_prod(source):
        return pltpu.make_async_remote_copy(
            src_ref=group(stage, source), dst_ref=got.at[source],
            send_sem=prod_send.at[source], recv_sem=prod_recv.at[source],
            device_id={"ctx": source}, device_id_type=ctx_dev,
        )

    def send_back(target):
        return pltpu.make_async_remote_copy(
            src_ref=result.at[target], dst_ref=group(back, me),
            send_sem=back_send.at[target], recv_sem=back_recv.at[me],
            device_id={"ctx": target}, device_id_type=ctx_dev,
        )

    def recv_back(source):
        return pltpu.make_async_remote_copy(
            src_ref=result.at[source], dst_ref=group(back, source),
            send_sem=back_send.at[source], recv_sem=back_recv.at[source],
            device_id={"ctx": source}, device_id_type=ctx_dev,
        )

    def others(act):
        @pl.loop(1, count)
        def _(step):
            act(lax.rem(me + step, count))

    def spread(values, ref, o, begin=0):
        for t in range(values.shape[1] // cols):
            ref[o, pl.ds(begin + t, chans, stride=own_rows), :] = values[:, t * cols : (t + 1) * cols]

    load_taps.wait()
    for o in range(taps_in.shape[0]):
        spread(taps_in[o], taps_sorted, o)
    taps_stage[...] = taps_sorted[...].astype(taps_stage.dtype)
    keep_taps.start()
    others(lambda target: send_taps(target).start())

    parts = 2
    share = tokens // parts

    block = pairs * 3 * chans

    def owner(late):
        low = z < line // 2
        return jnp.where(low, 1, 0) if late else jnp.where(low, 0, 1)

    def pair(late, n):
        lanes = slice(n * share, (n + 1) * share)
        return pltpu.make_async_remote_copy(
            src_ref=part.at[late, :, lanes], dst_ref=inbox.at[:, lanes],
            send_sem=pair_send.at[late, n], recv_sem=pair_recv.at[n],
            device_id={"ch": 1 - ch}, device_id_type=ctx_dev,
        )

    def project(late, *pieces):
        for n in pieces:
            mine = in_all[pl.ds(owner(late) * pairs, pairs)].reshape(block, wide)
            part[late, :, n * share : (n + 1) * share] = lax.dot_general(
                mine, tok[n * share : (n + 1) * share, :], (((1,), (1,)), ((), ())),
                preferred_element_type=jnp.float32,
            )

            @pl.when(owner(late) != ch)
            def _():
                pair(late, n).start()

    def consume(late, *pieces):
        @pl.when(owner(late) == ch)
        def _():
            for n in pieces:
                pair(late, n).wait_recv()
                lanes = slice(n * share, (n + 1) * share)
                for o in range(pairs):
                    near, key, value = [
                        part[late, pl.ds((3 * o + m) * chans, chans), lanes]
                        + inbox[pl.ds((3 * o + m) * chans, chans), lanes]
                        for m in range(3)
                    ]
                    gate[o, :, lanes] = near
                    values = key * value
                    prod[o, :, lanes] = values
                    spread(values, sorted_prod, o, n * share // cols)

    def send_products(late):
        @pl.when(owner(late) == ch)
        def _():
            stage[...] = sorted_prod[...].astype(stage.dtype)
            others(lambda target: send_prod(target).start())
            keep_prod.start()

        @pl.when(owner(late) != ch)
        def _():
            for n in range(parts):
                pair(late, n).wait_send()

    def iota(shape, dim):
        return lax.broadcasted_iota(jnp.int32, shape, dim)

    weights.upto(1)
    for copy in tables:
        copy.wait()
    blocks = order_ref.shape[1]
    hot = jnp.where(iota((blocks, blocks), 0) == order_ref[...], 1.0, 0.0).astype(jnp.bfloat16)
    down = jnp.where(iota((rows, blocks), 0) // sub == iota((rows, blocks), 1), 1.0, 0.0).astype(jnp.bfloat16)
    over = jnp.where(iota((blocks, rows), 1) // sub == iota((blocks, rows), 0), 1.0, 0.0).astype(jnp.bfloat16)
    dot = functools.partial(jnp.dot, preferred_element_type=jnp.float32)
    moved = dot(dot(down, hot).astype(jnp.bfloat16), over)
    same = lax.rem(iota((rows, rows), 0), sub) == lax.rem(iota((rows, rows), 1), sub)
    moved = jnp.where(same, moved, 0.0).astype(jnp.bfloat16)
    perm_wide = [dot(row_ref[k], moved) for k in range(2)]
    perm = [v.astype(jnp.bfloat16) for v in perm_wide]
    perm_t = [v.T.astype(jnp.bfloat16) for v in perm_wide]
    cos, sin = turn_ref[0], turn_ref[1]

    def transform(ref, table):
        values = ref[...].astype(jnp.float32)
        stacked = jnp.concatenate(
            [values[:, c * own_rows : (c + 1) * own_rows, :].reshape(rows, cols) for c in range(owned)], axis=1
        )
        stacked = stacked.astype(jnp.bfloat16)
        turn = dot(table[0], stacked) + dot(table[1], stacked)
        out = []
        for c in range(owned):
            real = turn[:rows, c * cols : (c + 1) * cols]
            imag = turn[rows:, c * cols : (c + 1) * cols]
            out.append(jnp.concatenate([real * cos + imag * sin, imag * cos - real * sin], axis=1))
        return dot_halves(halves(jnp.concatenate(out, axis=0)), (col_ref[0], col_ref[1]))

    weights.upto(2.6)
    load_in.wait()
    load_tok.wait()
    others(lambda source: recv_taps(source).wait_recv())
    keep_taps.wait()
    fil = transform(taps_got, (row_ref[0], row_ref[1]))
    weights.upto(3)
    project(0, 0)
    weights.some(9)
    for out in outs:
        out.begin(0)
    project(0, 1)
    consume(0, 0, 1)
    send_products(0)
    weights.some(3)
    weights.upto(9)
    load_out.wait()
    for out in outs:
        out.wait_lifted()
        out.begin(1)
    project(1, 0, 1)
    consume(1, 0, 1)
    send_products(1)
    weights.finish()
    others(lambda target: send_taps(target).wait_send())
    others(lambda source: recv_prod(source).wait_recv())
    keep_prod.wait()
    sig = transform(got, perm)
    sr, si, fr, fi = sig[:, :cols], sig[:, cols:], fil[:, :cols], fil[:, cols:]
    both = jnp.concatenate([sr * fr - si * fi, sr * fi + si * fr], axis=1)
    spun = dot_halves(halves(both), (inv_ref[0], inv_ref[1]))
    turn = []
    for c in range(owned):
        real = spun[c * rows : (c + 1) * rows, :cols]
        imag = spun[c * rows : (c + 1) * rows, cols:]
        turn.append(jnp.concatenate([real * cos - imag * sin, real * sin + imag * cos], axis=0))
    conv = dot_halves(perm_t, halves(jnp.concatenate(turn, axis=1)))
    pieces = [conv[:, c * cols : (c + 1) * cols].reshape(count, own_rows, cols) for c in range(owned)]
    result[...] = jnp.concatenate(pieces, axis=1).astype(result.dtype)
    keep_back.start()
    others(lambda target: send_back(target).start())
    for out in outs:
        out.wait_passed(0)
        out.begin(2)
    others(lambda source: recv_back(source).wait_recv())
    keep_back.wait()
    back_wide[...] = back[...].astype(jnp.float32)
    width = skip_ref.shape[1]
    diagonal = iota((width, width), 0) == iota((width, width), 1)
    skip = jnp.sum(jnp.where(diagonal, skip_ref[...], 0.0), axis=1, keepdims=True)
    for o in range(0, gate.shape[0], 2):
        for t in range(own_rows):
            lanes = slice(t * cols, (t + 1) * cols)
            pieces = []
            for k in (o, o + 1):
                near = back_wide[k, pl.ds(t, chans, stride=own_rows), :]
                pieces.append(gate[k, :, lanes] * (near + skip[k * chans : (k + 1) * chans] * prod[k, :, lanes]))
            hid[o * chans : (o + 2) * chans, lanes] = jnp.concatenate(pieces, axis=0).astype(jnp.bfloat16)
    hand = pltpu.make_async_remote_copy(
        src_ref=hid, dst_ref=hidden_ref.at[ch], send_sem=hid_send.at[0], recv_sem=hid_recv.at[0],
        device_id={"ch": 1 - ch}, device_id_type=ctx_dev,
    )
    hand.start()
    keep_hid.start()
    others(lambda target: send_prod(target).wait_send())
    others(lambda target: send_back(target).wait_send())
    for out in outs:
        out.wait_passed(1)
        out.wait_passed(2)
        out.finish()
    keep_hid.wait()
    hand.wait()


def split_table(table):
    top = table.astype(jnp.bfloat16)
    low = (table - top.astype(np.float32)).astype(jnp.bfloat16)
    return np.stack([top, low])


def fused(tokens, in_weight, conv_filter, skip_gain, group_order, out_weight, count):
    tok_count, feat = tokens.shape
    chans = in_weight.shape[0]
    chan_local = conv_filter.shape[0]
    seq = tok_count * count
    rows, cols = split_length(seq)
    own_rows = tok_count // cols
    owned = chan_local // count
    sub = seq // group_order.shape[0] // cols
    freq = 4 * np.arange(rows) + 1

    def turns(numer, period):
        angle = (numer % period) * (2.0 * math.pi / period)
        return np.cos(angle).astype(np.float32), np.sin(angle).astype(np.float32)

    cos, sin = turns(freq[:, None] * np.arange(rows)[None, :], 4 * rows)
    row_dft = np.concatenate([cos, -sin], axis=0)
    cos, sin = turns(np.arange(cols)[:, None] * np.arange(cols)[None, :], cols)
    col_dft = np.concatenate([np.concatenate([cos, -sin], 1), np.concatenate([sin, cos], 1)], 0)
    col_inv = (col_dft.T / (rows * cols)).astype(np.float32)
    tw_cos, tw_sin = turns(freq[:, None] * np.arange(cols)[None, :], 4 * rows * cols)
    pairs = chan_local // chans
    hbm = pl.BlockSpec(memory_space=pl.ANY)
    f32, bf16 = jnp.float32, jnp.bfloat16
    packed, slim = [pltpu.VMEM((pairs, chans * own_rows, cols), kind) for kind in (f32, bf16)]
    short = pltpu.VMEM((count, owned * own_rows, cols), bf16)
    full = pltpu.VMEM((pairs, chans, tok_count), f32)
    strips = pltpu.VMEM((2, pairs * 3 * chans, tok_count), f32)
    strip = pltpu.VMEM((pairs * 3 * chans, tok_count), f32)
    each = pltpu.SemaphoreType.DMA((count,))
    hidden, rows_all = pl.pallas_call(
        functools.partial(fused_kernel, count, sub),
        out_shape=(
            jax.ShapeDtypeStruct((2, chan_local, tok_count), bf16),
            jax.ShapeDtypeStruct((count // PLANE, 2, 2, *out_weight.shape), bf16),
        ),
        in_specs=[hbm] * 10,
        out_specs=(hbm, hbm),
        scratch_shapes=[
            pltpu.VMEM((1, chan_local), f32),
            pltpu.VMEM((1, group_order.shape[0]), jnp.int32),
            pltpu.VMEM((2, *row_dft.shape), bf16),
            pltpu.VMEM((2, *col_dft.shape), bf16),
            pltpu.VMEM((2, *col_inv.shape), bf16),
            pltpu.VMEM((2, rows, cols), f32),
            pltpu.VMEM((count, 3, chans, feat), bf16),
            pltpu.VMEM((tok_count, feat), bf16),
            strips, strip, full, full, packed, slim, full, packed, slim, short, short, short, slim, packed,
            pltpu.VMEM((chan_local, tok_count), bf16),
            pltpu.SemaphoreType.DMA((3, count, 4)),
            pltpu.SemaphoreType.DMA((3, count)),
            pltpu.SemaphoreType.DMA((2, 6)),
            pltpu.SemaphoreType.DMA((2, 7)),
            pltpu.SemaphoreType.DMA((2, 4)),
            pltpu.SemaphoreType.DMA((4,)),
            each, each, each, each, each, each,
            pltpu.SemaphoreType.DMA((1,)),
            pltpu.SemaphoreType.DMA((1,)),
            pltpu.SemaphoreType.DMA((14,)),
        ],
        compiler_params=pltpu.CompilerParams(collective_id=0, has_side_effects=True, vmem_limit_bytes=VMEM_LIMIT),
        name="fused",
    )(
        in_weight.transpose(1, 0, 2), tokens, out_weight, conv_filter.reshape(pairs, chans, tok_count),
        skip_gain.reshape(1, -1), group_order.reshape(1, -1), split_table(row_dft), split_table(col_dft),
        split_table(col_inv), np.stack([tw_cos, tw_sin]),
    )
    return hidden.reshape(2 * chan_local, tok_count), rows_all.reshape(-1, feat)


def mix_kernel(tile, wide, hidden_hbm, rows_hbm, out_ref, hidden, rows, tiles, sems):
    loads = [
        pltpu.make_async_copy(hidden_hbm, hidden, sems.at[0]),
        pltpu.make_async_copy(rows_hbm, rows, sems.at[1]),
    ]
    for copy in loads:
        copy.start()
    for copy in loads:
        copy.wait()
    stores = []
    for k in range(tiles.shape[0]):
        mine = hidden[:, k * tile : (k + 1) * tile]
        for at in range(0, tiles.shape[2], wide):
            tiles[k, :, at : at + wide] = lax.dot_general(
                mine, rows[:, at : at + wide], (((0,), (0,)), ((), ())), preferred_element_type=jnp.float32
            ).astype(tiles.dtype)
        stores.append(pltpu.make_async_copy(tiles.at[k], out_ref.at[pl.ds(k * tile, tile)], sems.at[2 + k]))
        stores[-1].start()
    for copy in stores:
        copy.wait()


def mix(hidden, rows, tile=64, wide=512):
    count, feat = hidden.shape[1], rows.shape[1]
    hbm = pl.BlockSpec(memory_space=pl.ANY)
    return pl.pallas_call(
        functools.partial(mix_kernel, tile, wide),
        out_shape=jax.ShapeDtypeStruct((count, feat), jnp.bfloat16),
        in_specs=[hbm, hbm],
        out_specs=hbm,
        scratch_shapes=[
            pltpu.VMEM(hidden.shape, hidden.dtype),
            pltpu.VMEM(rows.shape, rows.dtype),
            pltpu.VMEM((count // tile, tile, feat), jnp.bfloat16),
            pltpu.SemaphoreType.DMA((2 + count // tile,)),
        ],
        compiler_params=pltpu.CompilerParams(vmem_limit_bytes=VMEM_LIMIT),
        name="mix",
    )(hidden, rows)


def per_device(tokens, in_weight, conv_filter, skip_gain, group_order, out_weight):
    ctx = lax.axis_size("ctx")
    ch = lax.axis_size("ch")
    tok_count, feat_local = tokens.shape
    chan_local = conv_filter.shape[0]
    seq = tok_count * ctx
    group = seq // group_order.shape[0]
    rows, cols = split_length(seq)
    own_rows = tok_count // cols
    owned = -(-chan_local // ctx)
    padded = owned * ctx

    def parts_of(signal):
        signal = jnp.pad(signal, ((0, padded - chan_local), (0, 0)))
        return signal.reshape(ctx, owned, own_rows, cols)

    def swapped(parts):
        return lax.all_to_all(parts, "ctx", split_axis=0, concat_axis=0, tiled=True)

    relayed = ctx == RELAY_LIMIT and ch == 2 and in_weight.shape[0] == 8 and own_rows == 8 and padded == chan_local
    if relayed:
        hidden_all, rows_all = fused(tokens, in_weight, conv_filter, skip_gain, group_order, out_weight, ctx)
        return mix(hidden_all, rows_all)
    mine = in_weight.reshape(-1, feat_local)
    flat = lax.all_gather(mine, "ctx", axis=0, tiled=True)
    rows_all = lax.all_gather(out_weight, "ctx", axis=0, tiled=True)
    taps = swapped(parts_of(conv_filter))
    partial = lax.dot_general(flat, tokens, (((1,), (1,)), ((), ())), preferred_element_type=jnp.float32)
    if ch == 2:
        me = lax.axis_index("ch")
        half = partial.shape[0] // 2
        away = lax.dynamic_slice_in_dim(partial, (1 - me) * half, half, 0)
        kept = lax.dynamic_slice_in_dim(partial, me * half, half, 0)
        proj = kept + lax.ppermute(away, "ch", [(0, 1), (1, 0)])
    else:
        proj = lax.psum_scatter(partial, "ch", scatter_dimension=0, tiled=True)
    proj = proj.reshape(chan_local, 3, tok_count)
    gate = proj[:, 0]
    product = proj[:, 1] * proj[:, 2]
    in_group = jnp.arange(group // cols, dtype=jnp.int32)
    row_ids = (group_order[:, None] * (group // cols) + in_group[None, :]).reshape(rows)

    def grid(parts):
        return parts.transpose(0, 2, 1, 3).reshape(rows, owned, cols)

    conv = causal_conv(grid(swapped(parts_of(product))), grid(taps), row_ids)
    back = swapped(conv.reshape(ctx, own_rows, owned, cols).transpose(0, 2, 1, 3))
    conv = back.reshape(padded, tok_count)[:chan_local]
    hidden = (gate * (conv + skip_gain[:, None] * product)).astype(jnp.bfloat16)
    hidden_all = lax.all_gather(hidden, "ch", axis=0, tiled=True)
    mixed = lax.dot_general(
        hidden_all, rows_all, (((0,), (0,)), ((), ())), preferred_element_type=jnp.float32
    )
    return mixed.astype(jnp.bfloat16)


def solution(mesh):
    in_specs = (P("ctx", "ch"), P("ctx", None, "ch"), P("ch", "ctx"), P("ch"), P(), P("ctx", "ch"))
    return jax.shard_map(
        per_device, mesh=mesh, in_specs=in_specs, out_specs=P("ctx", "ch"), check_vma=False
    )
```
